32 devices in a mesh: groups: 2 (over y), rows: 4 (over z), cols: 2 (over x), sub: 2 (over core).
Axes of the slice: x: 2, y: 2, z: 4, core: 2. Of those that a mesh axis runs over, the one named last changes fastest.
Arguments:
- trace: float32 [8, 4096, 32], P(('cols', 'sub'), 'groups', 'rows'), parts along dimension 1, may hold values from -6 to 6
Outputs:
- quotient: float32 [4, 2048, 128], P('groups', ('rows', 'cols', 'sub')), parts along dimension 0
The draws below stay inside these ranges and needn't reach their ends.
There are 2 independent parts, one for each index of `groups`. The reference program is written for one: setup_inputs(seed, part) draws one part's arguments, and reference() takes and returns one part's arrays. A program takes and returns all parts, laid end to end along the dimension named above; each array names one. Nothing has to cross between parts.
All inputs are finite; a program needn't handle non-finite values.
Results may differ from the reference program's by a relative error of at most 0.00011.
Values sent between devices are 32-bit elements; how exact they have to be, the bound alone decides.
A program may use at most 64 MiB of HBM per device.

```python
import math
import jax
import jax.numpy as jnp
from jax import lax

COLUMNS = 8
SLOW = 2048
FAST = 32


def block_scale(rng, shape, pieces, least, largest):
    def one(axis_at, blocks):
        heights = jax.random.uniform(jax.random.fold_in(jax.random.fold_in(rng, 6), axis_at), (blocks,), jnp.float32, least / len(pieces), largest / len(pieces))
        return jnp.repeat(jnp.exp(heights), shape[axis_at] // blocks).reshape((-1,) + (1,) * (len(shape) - axis_at - 1))

    level = one(*pieces[0])
    for cut in pieces[1:]:
        level = level * one(*cut)
    return level


def scatter_about(key, shape, width, most, pieces=(), kind=jnp.bfloat16):
    values = width * jax.random.normal(key, shape, jnp.float32)
    if pieces:
        values = values * block_scale(key, shape, pieces, -0.22, 0.18)
    return jnp.clip(values, -most, most).astype(kind)


def setup_inputs(seed: int = 0, part: int = 0) -> dict:
    keys = jax.random.split(jax.random.key(seed), 2)
    own_keys = jax.random.split(jax.random.fold_in(keys[1], part), 2)
    trace = scatter_about(own_keys[0], (COLUMNS, SLOW, FAST), 1.0, 6.0, ((0, 4), (2, 4)), jnp.float32)
    return {"trace": trace}


def reference(trace):
    all_cols, slow_len, fast_len = trace.shape
    trace_len = slow_len * fast_len
    ext_len = 4 * trace_len
    values = trace.reshape(all_cols, trace_len)
    coeffs = jnp.fft.ifft(values, axis=1)
    positions = jnp.arange(trace_len, dtype=jnp.float32) * (math.pi / (4.0 * trace_len))
    coset_shift = lax.complex(jnp.cos(positions), jnp.sin(positions))
    coeffs = jnp.pad(coeffs * coset_shift[None, :], ((0, 0), (0, ext_len - trace_len)))
    evaluations = jnp.fft.fft(coeffs, axis=1)
    wire_a = evaluations[0]
    wire_b = evaluations[1]
    wire_c = evaluations[2]
    select_mul = evaluations[3]
    select_left = evaluations[4]
    select_right = evaluations[5]
    select_out = evaluations[6]
    select_const = evaluations[7]
    gate = select_mul * wire_a * wire_b * wire_c + select_left * wire_a + select_right * wire_b + select_out * wire_c + select_const
    quarter = (jnp.arange(ext_len, dtype=jnp.int32) % 4).astype(jnp.float32)
    vanish_angle = math.pi / 4.0 - math.pi / 2.0 * quarter
    vanish = lax.complex(jnp.cos(vanish_angle) - 1.0, jnp.sin(vanish_angle))
    ratio = gate / vanish
    spread = jnp.fft.ifft(ratio) * math.sqrt(ext_len)
    ext_positions = jnp.arange(ext_len, dtype=jnp.float32) * (-math.pi / (4.0 * trace_len))
    unshift = lax.complex(jnp.cos(ext_positions), jnp.sin(ext_positions))
    result = (spread * unshift).reshape(4 * fast_len, slow_len).T
    return jnp.stack([jnp.real(result), jnp.imag(result)])
```

```python
from functools import partial
import math

import jax
import jax.numpy as jnp
import numpy as np
from jax import lax
from jax.experimental import pallas as pl
from jax.experimental.pallas import tpu as pltpu
from jax.sharding import PartitionSpec as P


def dft_table(extent, orient):
    points = jnp.arange(extent, dtype=jnp.int32)
    product = points[:, None] * points[None, :] % extent
    angles = product.astype(jnp.float32) * (orient * 2.0 * math.pi / extent)
    return (jnp.cos(angles), jnp.sin(angles))


def complex_apply(table_real, table_imag, data_real, data_imag):
    matmul = partial(jnp.dot, precision=lax.Precision.HIGHEST, preferred_element_type=jnp.float32)
    out_real = matmul(table_real, data_real) - matmul(table_imag, data_imag)
    out_imag = matmul(table_real, data_imag) + matmul(table_imag, data_real)
    return (out_real, out_imag)


def rotate(data_real, data_imag, angles):
    cosine = jnp.cos(angles)
    sine = jnp.sin(angles)
    return (data_real * cosine - data_imag * sine, data_real * sine + data_imag * cosine)


def turn(index_product, modulus, orient):
    return (index_product % modulus).astype(jnp.float32) * (orient * 2.0 * math.pi / modulus)


def transform_lead(data_real, data_imag, orient):
    extent = data_real.shape[0]
    rest_shape = data_real.shape[1:]
    breadth = data_real.size // extent
    flat_real = data_real.reshape(extent, breadth)
    flat_imag = data_imag.reshape(extent, breadth)
    if extent <= 128:
        table_real, table_imag = dft_table(extent, orient)
        out_real, out_imag = complex_apply(table_real, table_imag, flat_real, flat_imag)
    else:
        outer_len = extent // 128
        first_real, first_imag = transform_lead(
            flat_real.reshape(outer_len, 128 * breadth),
            flat_imag.reshape(outer_len, 128 * breadth),
            orient,
        )
        first_real = first_real.reshape(outer_len, 128, breadth)
        first_imag = first_imag.reshape(outer_len, 128, breadth)
        outer_index = jnp.arange(outer_len, dtype=jnp.int32)[:, None]
        inner_index = jnp.arange(128, dtype=jnp.int32)[None, :]
        angles = turn(outer_index * inner_index, extent, orient)[:, :, None]
        first_real, first_imag = rotate(first_real, first_imag, angles)
        first_real = jnp.transpose(first_real, (1, 0, 2)).reshape(128, outer_len * breadth)
        first_imag = jnp.transpose(first_imag, (1, 0, 2)).reshape(128, outer_len * breadth)
        out_real, out_imag = transform_lead(first_real, first_imag, orient)
    return (out_real.reshape((extent,) + rest_shape), out_imag.reshape((extent,) + rest_shape))


def times(first, second):
    return (
        first[0] * second[0] - first[1] * second[1],
        first[0] * second[1] + first[1] * second[0],
    )


def plus(first, second):
    return (first[0] + second[0], first[1] + second[1])


def on_device(trace):
    local_cols = trace.shape[0]
    slow_len = trace.shape[1]
    fast_local = trace.shape[2]
    row_parts = lax.axis_size("rows")
    group_parts = lax.axis_size(("cols", "sub"))
    row_index = lax.axis_index("rows")
    group_index = lax.axis_index(("cols", "sub"))
    fast_len = fast_local * row_parts
    trace_len = slow_len * fast_len
    ext_len = 4 * trace_len
    ext_slow = 4 * fast_len
    slow_block = slow_len // row_parts
    ext_block = ext_slow // row_parts
    point_block = ext_block // group_parts
    coeff_block = slow_block // group_parts
    real_part = jnp.transpose(trace, (1, 0, 2))
    imag_part = jnp.zeros_like(real_part)
    real_part, imag_part = transform_lead(real_part, imag_part, 1.0)
    lead_index = jnp.arange(slow_len, dtype=jnp.int32)[:, None, None]
    fast_index = (row_index * fast_local + jnp.arange(fast_local, dtype=jnp.int32))[None, None, :]
    real_part, imag_part = rotate(
        real_part, imag_part, turn(lead_index * fast_index, trace_len, 1.0)
    )
    moved = lax.all_to_all(
        jnp.stack([real_part, imag_part]), "rows", split_axis=1, concat_axis=3, tiled=True
    )
    moved = jnp.transpose(moved, (0, 3, 2, 1))
    real_part, imag_part = transform_lead(moved[0], moved[1], 1.0)
    slow_index = (row_index * slow_block + jnp.arange(slow_block, dtype=jnp.int32))[None, None, :]
    coeff_index = jnp.arange(fast_len, dtype=jnp.int32)[:, None, None] * slow_len + slow_index
    shift_angle = coeff_index.astype(jnp.float32) * (math.pi / (4.0 * trace_len))
    real_part, imag_part = rotate(real_part / trace_len, imag_part / trace_len, shift_angle)
    padding = jnp.zeros((ext_slow - fast_len, local_cols, slow_index.shape[2]), jnp.float32)
    real_part = jnp.concatenate([real_part, padding], 0)
    imag_part = jnp.concatenate([imag_part, padding], 0)
    real_part, imag_part = transform_lead(real_part, imag_part, -1.0)
    ext_index = jnp.arange(ext_slow, dtype=jnp.int32)[:, None, None]
    real_part, imag_part = rotate(real_part, imag_part, turn(ext_index * slow_index, ext_len, -1.0))
    stacked = jnp.stack([real_part, imag_part])
    moved = lax.all_to_all(stacked, "rows", split_axis=1, concat_axis=3, tiled=True)
    moved = jnp.transpose(moved, (0, 3, 2, 1))
    real_part, imag_part = transform_lead(moved[0], moved[1], -1.0)
    joined = lax.all_to_all(
        jnp.stack([real_part, imag_part]), ("cols", "sub"), split_axis=3, concat_axis=2, tiled=True
    )
    real_part = joined[0]
    imag_part = joined[1]

    def column(number):
        return (real_part[:, number], imag_part[:, number])

    wire_a = column(0)
    wire_b = column(1)
    wire_c = column(2)
    gate = times(times(times(column(3), wire_a), wire_b), wire_c)
    gate = plus(gate, times(column(4), wire_a))
    gate = plus(gate, times(column(5), wire_b))
    gate = plus(gate, times(column(6), wire_c))
    gate = plus(gate, column(7))
    point_index = (
        row_index * ext_block + group_index * point_block + jnp.arange(point_block, dtype=jnp.int32)
    )
    quarter = (point_index % 4).astype(jnp.float32)
    vanish_angle = math.pi / 4.0 - math.pi / 2.0 * quarter
    vanish_real = (jnp.cos(vanish_angle) - 1.0)[None, :]
    vanish_imag = jnp.sin(vanish_angle)[None, :]
    magnitude = vanish_real * vanish_real + vanish_imag * vanish_imag
    ratio_real = (gate[0] * vanish_real + gate[1] * vanish_imag) / magnitude
    ratio_imag = (gate[1] * vanish_real - gate[0] * vanish_imag) / magnitude
    real_part, imag_part = transform_lead(ratio_real, ratio_imag, 1.0)
    freq_index = jnp.arange(slow_len, dtype=jnp.int32)[:, None]
    real_part, imag_part = rotate(
        real_part, imag_part, turn(freq_index * point_index[None, :], ext_len, 1.0)
    )
    moved = lax.all_to_all(
        lax.all_to_all(
            jnp.stack([real_part, imag_part]), "rows", split_axis=1, concat_axis=2, tiled=True
        ),
        ("cols", "sub"),
        split_axis=1,
        concat_axis=2,
        tiled=True,
    )
    moved = moved.reshape(2, coeff_block, group_parts, row_parts, point_block)
    moved = jnp.transpose(moved, (0, 3, 2, 4, 1)).reshape(2, ext_slow, coeff_block)
    real_part, imag_part = transform_lead(moved[0], moved[1], 1.0)
    low_index = (
        row_index * slow_block
        + group_index * coeff_block
        + jnp.arange(coeff_block, dtype=jnp.int32)
    )[None, :]
    final_index = jnp.arange(ext_slow, dtype=jnp.int32)[:, None] * slow_len + low_index
    final_angle = final_index.astype(jnp.float32) * (-math.pi / (4.0 * trace_len))
    real_part, imag_part = rotate(real_part, imag_part, final_angle)
    result = jnp.stack([real_part, imag_part]) * (1.0 / math.sqrt(ext_len))
    return jnp.transpose(result, (0, 2, 1))


MESH = pl.DeviceIdType.MESH
CHUNKS = 4
HALVES = 2
VMEM_LIMIT = 12 * 2**20


def halves(table):
    high = table.astype(jnp.bfloat16)
    low = (table - high.astype(np.float64)).astype(jnp.bfloat16)
    return high, low


def fused_tables(sizes):
    side, fast_len, fast_local, rows, groups, blocks = sizes
    points = side * side
    ext = rows * points
    low_len = side // fast_len
    slow_len = side * low_len
    half = low_len * fast_local
    lows = low_len // HALVES
    cols, subs = blocks
    index = np.arange(side)
    angles = 2.0 * np.pi * (index[:, None] * index[None, :] % side) / side
    dft = np.stack(halves(np.cos(angles)) + halves(np.sin(angles)))
    low_at, fast_at = (
        grid.reshape(-1)
        for grid in np.meshgrid(np.arange(low_len), np.arange(fast_local), indexing="ij")
    )
    freq = low_at[:, None] + low_len * index[None, :]
    centred = freq - slow_len // 2
    members = np.arange(rows)
    inner = fast_local * members[:, None] + fast_at
    theta = 2.0 * np.pi * inner[:, :, None] * centred / points
    base = np.stack([np.cos(theta), np.sin(theta)], 1).astype(np.float32)
    shifts = 0.5 / rows - np.arange(rows) / rows
    angle = centred * (2.0 * np.pi / points) * shifts[:, None, None, None] - theta
    post = np.stack([np.cos(angle), np.sin(angle)], 1).astype(np.float32)
    post = post.reshape(rows, 2, cols, subs, HALVES, lows * fast_local, side)
    post = np.transpose(post, (0, 2, 4, 1, 3, 5, 6)).reshape(rows * cols, HALVES, 2, -1, side)
    slot_at, low_in, fast_in = (
        grid.reshape(-1)
        for grid in np.meshgrid(
            np.arange(rows), np.arange(lows), np.arange(fast_local), indexing="ij"
        )
    )
    inner = fast_local * slot_at + fast_in
    same = low_in[:, None] == low_in[None, :]
    sign = 1.0 - 2.0 * (inner[:, None] % 2)
    kernels = []
    for shift in shifts:
        gap = inner[None, :] - inner[:, None] + shift
        weight = sign / points * np.sin(np.pi * shift) / np.sin(np.pi * gap / fast_len)
        weight = np.where(same, weight, 0.0)
        for part in np.split(weight, cols):
            kernels.append(np.stack(halves(part)))
    kernels = np.stack(kernels)
    spin = 2.0 * np.pi * low_at[:, None] * index[None, :] / slow_len
    spin = np.stack([np.cos(spin), np.sin(spin)]).astype(np.float32)
    row_at, group_at = np.divmod(np.arange(rows * groups), groups)
    digit = rows * (fast_local * group_at[:, None] + fast_at) + row_at[:, None]
    angle = freq * (2 * digit[:, :, None] - 1) % (2 * ext) * (np.pi / ext)
    twist = np.stack([np.cos(angle), np.sin(angle)], 1).astype(np.float32)
    source_row, source_group, fast_at = np.meshgrid(
        np.arange(rows), np.arange(groups), np.arange(fast_local), indexing="ij"
    )
    low_digit = rows * (fast_local * source_group + fast_at) + source_row
    vanish = np.exp(1j * (np.pi / rows - 2.0 * np.pi / rows * source_row)) - 1.0
    finals = np.arange(rows * fast_len)
    turns = np.exp(
        2j * np.pi * low_digit[..., None] * finals / (rows * fast_len)
        - 1j * np.pi * slow_len * finals / ext
    ) / (vanish[..., None] * math.sqrt(ext))
    real_rows = np.concatenate([turns.real, turns.imag], -1)
    imag_rows = np.concatenate([-turns.imag, turns.real], -1)
    final = np.stack([real_rows, imag_rows], 2).reshape(-1, 2 * rows * fast_len)
    final = np.stack(halves(final))
    return dft, spin, base, kernels, post, twist, final


def split(value):
    high = value.astype(jnp.bfloat16)
    return high, (value - high.astype(jnp.float32)).astype(jnp.bfloat16)


def dot3(left, right):
    mul = partial(jnp.dot, preferred_element_type=jnp.float32)
    return mul(left[0], right[0]) + (mul(left[0], right[1]) + mul(left[1], right[0]))


def short_transform(values, orient):
    count = len(values)
    if count == 1:
        return values
    even = short_transform(values[0::2], orient)
    odd = short_transform(values[1::2], orient)
    first, second = [], []
    for at in range(count // 2):
        cosine = math.cos(2.0 * math.pi * at / count)
        sine = orient * math.sin(2.0 * math.pi * at / count)
        real, imag = odd[at]
        if at == 0:
            spun = (real, imag)
        elif 4 * at == count:
            spun = (-orient * imag, orient * real)
        else:
            spun = (real * cosine - imag * sine, real * sine + imag * cosine)
        first.append(plus(even[at], spun))
        second.append((even[at][0] - spun[0], even[at][1] - spun[1]))
    return first + second


def fused_kernel(
    sizes,
    x_hbm,
    dft_hbm,
    spin_hbm,
    base_hbm,
    kern_hbm,
    post_hbm,
    twist_hbm,
    out_ref,
    x_ref,
    dft,
    spin,
    base,
    kern,
    post,
    twist,
    edge,
    gathered,
    send_prod,
    recv_prod,
    spread,
    send_tail,
    recv_tail,
    table_sem,
    gather_send,
    gather_recv,
    prod_send,
    prod_recv,
    tail_send,
    tail_recv,
):
    side, fast_len, fast_local, rows, groups, (cols, subs) = sizes
    points = side * side
    low_len = side // fast_len
    half = low_len * fast_local
    lows = low_len // CHUNKS
    deep = lows * fast_local
    thick = CHUNKS // HALVES * deep
    members = rows * groups
    row = lax.axis_index("rows")
    col = lax.axis_index("cols")
    sub = lax.axis_index("sub")
    group = col * subs + sub
    me = row * groups + group

    def place(member):
        inside = lax.rem(member, groups)
        return {
            "rows": lax.div(member, groups),
            "cols": lax.div(inside, subs),
            "sub": lax.rem(inside, subs),
        }

    first_load = pltpu.make_async_copy(x_hbm, x_ref, table_sem.at[0])
    first_load.start()
    barrier = pltpu.get_barrier_semaphore()

    @pl.when(row > 0)
    def _():
        pl.semaphore_signal(barrier, inc=1, device_id={"rows": row - 1}, device_id_type=MESH)

    @pl.when(row < rows - 1)
    def _():
        pl.semaphore_signal(barrier, inc=1, device_id={"rows": row + 1}, device_id_type=MESH)

    for near in ({"cols": 1 - col}, {"sub": 1 - sub}):
        pl.semaphore_signal(barrier, inc=1, device_id=near, device_id_type=MESH)

    loads = [
        first_load,
        pltpu.make_async_copy(spin_hbm, spin, table_sem.at[1]),
        pltpu.make_async_copy(dft_hbm, dft, table_sem.at[2]),
        pltpu.make_async_copy(base_hbm.at[row], base, table_sem.at[3]),
        pltpu.make_async_copy(kern_hbm.at[row * cols + col], kern, table_sem.at[4]),
        pltpu.make_async_copy(post_hbm.at[row * cols + col], post, table_sem.at[5]),
        pltpu.make_async_copy(twist_hbm.at[me], twist, table_sem.at[6]),
    ]
    for load in loads[1:4]:
        load.start()

    def stacked(values):
        return jnp.concatenate([value for value in values], 0)

    def slices(real, imag):
        return [
            (real[at * fast_local : (at + 1) * fast_local], imag[at * fast_local : (at + 1) * fast_local])
            for at in range(low_len)
        ]

    def lane_transform(real, imag, orient):
        count = real.shape[0]
        data = split(jnp.concatenate([real, imag], 0))
        cosines = dot3(data, (dft[0], dft[1]))
        sines = dot3(data, (dft[2], dft[3]))
        return (
            cosines[:count] - orient * sines[count:],
            cosines[count:] + orient * sines[:count],
        )

    loads[0].wait()
    values = [
        (
            x_ref[0, :, at * side : (at + 1) * side],
            x_ref[1, :, at * side : (at + 1) * side],
        )
        for at in range(low_len)
    ]
    values = short_transform(values, 1.0)
    real = stacked([value[0] for value in values])
    imag = stacked([value[1] for value in values])
    loads[1].wait()
    real, imag = times((real, imag), (spin[0], spin[1]))
    loads[2].wait()
    real, imag = lane_transform(real, imag, 1.0)
    loads[3].wait()
    real, imag = times((real, imag), (base[0], base[1]))
    for chunk in range(CHUNKS):
        gathered[row, col, chunk, 0] = real[chunk * deep : (chunk + 1) * deep]
        gathered[row, col, chunk, 1] = imag[chunk * deep : (chunk + 1) * deep]

    pl.semaphore_wait(
        barrier,
        2 + (row > 0).astype(jnp.int32) + (row < rows - 1).astype(jnp.int32),
    )

    inner = (row > 0) & (row < rows - 1)
    outer = jnp.logical_not(inner)
    end = jnp.where(2 * row < rows, 0, rows - 1)
    far = rows - 1 - end
    beside = jnp.where(row == 0, 1, jnp.where(row == rows - 1, rows - 2, rows - 1 - row))
    other = jnp.where(inner, end, jnp.where(end == 0, rows - 2, 1))
    across = {"cols": 1 - col}

    def hop(slot, pair, chunk, way, target):
        return pltpu.make_async_remote_copy(
            src_ref=gathered.at[slot, pair, chunk],
            dst_ref=gathered.at[slot, pair, chunk],
            send_sem=gather_send.at[way, chunk],
            recv_sem=gather_recv.at[slot, pair, chunk],
            device_id=target,
            device_id_type=MESH,
        )

    def arrive(slot, pair, chunk):
        hop(slot, pair, chunk, 0, across).wait_recv()

    def own_moves(chunk):
        return [
            (None, hop(row, col, chunk, 0, {"rows": beside})),
            (inner, hop(row, col, chunk, 1, {"rows": end})),
            (None, hop(row, col, chunk, 2, across)),
        ]

    def beside_moves(chunk):
        return [
            (inner, hop(beside, col, chunk, 3, {"rows": end})),
            (None, hop(beside, col, chunk, 4, across)),
        ]

    def other_moves(chunk):
        return [
            (inner, hop(other, col, chunk, 5, {"rows": beside})),
            (None, hop(other, col, chunk, 6, across)),
        ]

    def far_moves(chunk):
        return [
            (inner, hop(far, col, chunk, 7, {"rows": end})),
            (None, hop(far, col, chunk, 8, across)),
        ]

    def begin(moves):
        for need, move in moves:
            if need is None:
                move.start()
            else:
                pl.when(need)(move.start)

    def finish(moves):
        for need, move in moves:
            if need is None:
                move.wait_send()
            else:
                pl.when(need)(move.wait_send)

    for chunk in range(CHUNKS):
        begin(own_moves(chunk))
    for load in loads[4:]:
        load.start()

    shift = 0.5 / rows - row.astype(jnp.float32) / rows
    half_turn = jnp.zeros((1, 1), jnp.float32) + shift * math.pi
    half_cos = jnp.cos(half_turn)
    half_sin = jnp.sin(half_turn)
    edge_at = lax.broadcasted_iota(jnp.int32, edge.shape[1:], 0)
    edge_lane = lax.broadcasted_iota(jnp.int32, edge.shape[1:], 1)
    edge_angle = edge_at.astype(jnp.float32) * (math.pi / fast_len)
    edge[0] = jnp.where(edge_lane == 0, jnp.cos(edge_angle) * (1.0 / points), 0.0)
    edge[1] = jnp.where(edge_lane == 0, jnp.sin(edge_angle) * (1.0 / points), 0.0)

    def prod_copy(pair, part, origin):
        span = pl.ds(0, 2 * thick + (8 if part == 0 else 0))
        return pltpu.make_async_remote_copy(
            src_ref=send_prod.at[pair, part, span],
            dst_ref=recv_prod.at[pair * subs + origin, part, span],
            send_sem=prod_send.at[pair, part],
            recv_sem=prod_recv.at[pair * subs + origin, part],
            device_id={"sub": 1 - sub},
            device_id_type=MESH,
        )

    def part_chunks(part):
        return range(part * CHUNKS // HALVES, (part + 1) * CHUNKS // HALVES)

    def contract(pair, part):
        chunks = part_chunks(part)
        real, imag = (
            stacked([gathered[slot, pair, chunk, at] for slot in range(rows) for chunk in chunks])
            for at in range(2)
        )
        data = split(jnp.concatenate([real, imag], 1))
        moved = dot3((kern[0], kern[1]), data)
        real, imag = times((moved[:, :side], moved[:, side:]), (post[part, 0], post[part, 1]))
        mine = pair * subs + sub
        if part == 0:
            firsts = tuple(
                stacked([gathered[slot, pair, 0, at, :fast_local, :128] for slot in range(rows)])
                for at in range(2)
            )
            mean_a, mean_b = (
                jnp.sum(jnp.sum(raw, 0, keepdims=True), 1, keepdims=True)
                for raw in times(firsts, (edge[0], edge[1]))
            )
            row_at = lax.broadcasted_iota(jnp.int32, real.shape, 0)
            lane_at = lax.broadcasted_iota(jnp.int32, real.shape, 1)
            constant = (lane_at == 0) & (row_at % thick < fast_local)
            parity = jnp.where(constant, (1 - 2 * (row_at % 2)).astype(jnp.float32), 0.0)
            real = real - parity * (mean_a * half_cos + mean_b * half_sin)
            imag = imag - parity * (mean_b * half_cos - mean_a * half_sin)
            side_at = lax.broadcasted_iota(jnp.int32, (8, side), 1)
            means = jnp.where(side_at < side // 2, mean_a, mean_b)
            send_prod[pair, part, 2 * thick :] = means
            recv_prod[mine, part, 2 * thick :] = means

        for at in range(subs):
            span = slice(at * thick, (at + 1) * thick)

            @pl.when(sub == at)
            def _():
                recv_prod[mine, part, :thick] = real[span]
                recv_prod[mine, part, thick : 2 * thick] = imag[span]

            @pl.when(sub != at)
            def _():
                send_prod[pair, part, :thick] = real[span]
                send_prod[pair, part, thick : 2 * thick] = imag[span]

        prod_copy(pair, part, sub).start()

    def expand(pair, part):
        prod_copy(pair, part, 1 - sub).wait_recv()
        real, imag = (
            stacked(
                [
                    recv_prod[pair * subs + origin, part, at * thick : (at + 1) * thick]
                    for origin in range(subs)
                ]
            )
            for at in range(2)
        )
        real, imag = lane_transform(real, imag, -1.0)
        rows_at = slice(part * thick, (part + 1) * thick)
        for origin in range(subs):
            span = slice(origin * thick, (origin + 1) * thick)
            turned = times((real[span], imag[span]), (spin[0, rows_at], -spin[1, rows_at]))
            for at in range(2):
                spread[pair * subs + origin, at, rows_at] = turned[at]

    def join(pair):
        for origin in range(subs):
            number = pair * subs + origin
            values = short_transform(slices(spread[number, 0], spread[number, 1]), -1.0)
            for at in range(2):
                spread[number, at] = stacked([value[at] for value in values])

    for chunk in range(CHUNKS):
        arrive(beside, col, chunk)
        begin(beside_moves(chunk))

        @pl.when(inner)
        def _():
            arrive(other, col, chunk)
            begin([(None, move) for _, move in other_moves(chunk)])

    for chunk in range(CHUNKS):

        @pl.when(inner)
        def _():
            arrive(far, col, chunk)
            begin([(None, move) for _, move in far_moves(chunk)])

        @pl.when(outer)
        def _():
            arrive(other, col, chunk)
            begin(other_moves(chunk)[1:])

    loads[4].wait()
    loads[5].wait()
    for part in range(HALVES):
        for chunk in part_chunks(part):

            @pl.when(outer)
            def _():
                arrive(far, col, chunk)
                begin(far_moves(chunk)[1:])

        contract(col, part)
    for part in range(HALVES):
        expand(col, part)
    join(col)
    for part in range(HALVES):
        for slot in (row, beside, other, far):
            for chunk in part_chunks(part):
                arrive(slot, 1 - col, chunk)
        contract(1 - col, part)
        expand(1 - col, part)
    join(1 - col)

    at_row = lax.broadcasted_iota(jnp.int32, (half, side), 0)
    flip = (1 - 2 * (at_row % 2)).astype(jnp.float32)
    part_cos = flip * half_cos
    part_sin = flip * half_sin

    def value(number):
        block, at = divmod(number, 2)
        lane_from = at * (side // 2)
        mean = recv_prod[block, 0, 2 * thick : 2 * thick + 1, lane_from : lane_from + 1]
        data = spread[block, at]
        return (mean + part_cos * data, part_sin * data)

    wire_a = value(0)
    wire_b = value(1)
    wire_c = value(2)
    gate = times(times(times(value(3), wire_a), wire_b), wire_c)
    gate = plus(gate, times(value(4), wire_a))
    gate = plus(gate, times(value(5), wire_b))
    gate = plus(gate, times(value(6), wire_c))
    gate = plus(gate, value(7))
    values = short_transform(slices(*gate), 1.0)
    real = stacked([value[0] for value in values])
    imag = stacked([value[1] for value in values])
    real, imag = times((real, imag), (spin[0], spin[1]))
    loads[6].wait()
    data = split(jnp.concatenate([real, imag], 0))
    breadth = side * low_len // members
    lane_piece = side // members
    tile_lanes = low_len * lane_piece
    tiles = side // tile_lanes
    lanes = lax.broadcasted_iota(jnp.int32, (2 * fast_local, tile_lanes), 1)
    low_side = (2 * row < rows).astype(jnp.int32)

    def tail_copy(target, slot):
        return pltpu.make_async_remote_copy(
            src_ref=send_tail.at[target],
            dst_ref=recv_tail.at[slot],
            send_sem=tail_send.at[target],
            recv_sem=tail_recv.at[slot],
            device_id=place(target),
            device_id_type=MESH,
        )

    for turn_at in range(tiles):
        tile = lax.rem(low_side + turn_at, tiles)
        span = pl.ds(pl.multiple_of(tile * tile_lanes, tile_lanes), tile_lanes)
        cosines = dot3(data, (dft[0, :, span], dft[1, :, span]))
        sines = dot3(data, (dft[2, :, span], dft[3, :, span]))
        real, imag = times(
            (cosines[:half] - sines[half:], cosines[half:] + sines[:half]),
            (twist[0, :, span], twist[1, :, span]),
        )
        pieces = [
            jnp.concatenate(
                [
                    real[at * fast_local : (at + 1) * fast_local],
                    imag[at * fast_local : (at + 1) * fast_local],
                ],
                0,
            )
            for at in range(low_len)
        ]
        bit = low_len // 2
        while bit:
            keep = (lanes // (lane_piece * bit)) % 2 == 0
            for at in range(low_len):
                if at & bit == 0:
                    one, two = pieces[at], pieces[at + bit]
                    pieces[at] = jnp.where(keep, one, pltpu.roll(two, lane_piece * bit, 1))
                    pieces[at + bit] = jnp.where(
                        keep, pltpu.roll(one, tile_lanes - lane_piece * bit, 1), two
                    )
            bit //= 2
        for at in range(low_len):
            send_tail[tile * low_len + at] = pieces[at]
        for at in range(low_len):
            target = tile * low_len + lax.rem(at + low_side * (low_len // 2), low_len)

            @pl.when(target != me)
            def _():
                tail_copy(target, me).start()

    recv_tail[me] = send_tail[me]
    for step in range(1, members):
        source = lax.rem(me + step, members)
        tail_copy(source, source).wait_recv()
    out_ref[...] = recv_tail[...].reshape(members * 2 * fast_local, breadth)

    for step in range(1, members):
        target = lax.rem(me + step, members)
        tail_copy(target, me).wait_send()
    for pair in range(cols):
        for part in range(HALVES):
            prod_copy(pair, part, sub).wait_send()
    for chunk in range(CHUNKS):
        for moves in (
            own_moves,
            beside_moves,
            other_moves,
            far_moves,
        ):
            finish(moves(chunk))


def final_kernel(sizes, flat_ref, final_ref, out_ref):
    side, fast_len, fast_local, rows, groups, blocks = sizes
    low_len = side // fast_len
    lane_piece = side // (rows * groups)
    data = split(jnp.transpose(flat_ref[...]))
    result = dot3(data, (final_ref[0], final_ref[1]))
    for at in range(low_len):
        picked = result[at * lane_piece : (at + 1) * lane_piece]
        rows_at = pl.ds(at, lane_piece, stride=low_len)
        out_ref[0, rows_at] = picked[:, : rows * fast_len]
        out_ref[1, rows_at] = picked[:, rows * fast_len :]


def fused_on_device(sizes, trace):
    side, fast_len, fast_local, rows, groups, (cols, subs) = sizes
    low_len = side // fast_len
    half = low_len * fast_local
    deep = half // CHUNKS
    members = rows * groups
    *tables, final = [jnp.asarray(table) for table in fused_tables(sizes)]
    thick = half // HALVES
    block = jnp.transpose(trace, (0, 2, 1))
    vmem = pltpu.VMEM
    bf16 = jnp.bfloat16
    f32 = jnp.float32
    dma = pltpu.SemaphoreType.DMA
    breadth = side * low_len // members
    flat = pl.pallas_call(
        partial(fused_kernel, sizes),
        out_shape=vmem((members * 2 * fast_local, breadth), f32),
        in_specs=[pl.BlockSpec(memory_space=pltpu.HBM)] * (1 + len(tables)),
        out_specs=pl.BlockSpec(memory_space=vmem),
        scratch_shapes=[
            vmem(block.shape, f32),
            vmem((4, side, side), bf16),
            vmem((2, half, side), f32),
            vmem((2, half, side), f32),
            vmem((2, subs * thick, rows * thick), bf16),
            vmem((HALVES, 2, subs * thick, side), f32),
            vmem((2, half, side), f32),
            vmem((2, fast_len, 128), f32),
            vmem((rows, cols, CHUNKS, 2, deep, side), f32),
            vmem((cols, HALVES, 2 * thick + 8, side), f32),
            vmem((groups, HALVES, 2 * thick + 8, side), f32),
            vmem((groups, 2, half, side), f32),
            vmem((members, 2 * fast_local, breadth), f32),
            vmem((members, 2 * fast_local, breadth), f32),
            dma((8,)),
            dma((9, CHUNKS)),
            dma((rows, cols, CHUNKS)),
            dma((cols, HALVES)),
            dma((groups, HALVES)),
            dma((members,)),
            dma((members,)),
        ],
        compiler_params=pltpu.CompilerParams(
            collective_id=0, has_side_effects=True, vmem_limit_bytes=VMEM_LIMIT
        ),
    )(*[pltpu.with_memory_space_constraint(table, pltpu.HBM) for table in (block, *tables)])
    return pl.pallas_call(
        partial(final_kernel, sizes),
        out_shape=jax.ShapeDtypeStruct((2, breadth, rows * fast_len), f32),
        in_specs=[pl.BlockSpec(memory_space=vmem)] * 2,
        out_specs=pl.BlockSpec(memory_space=vmem),
        compiler_params=pltpu.CompilerParams(vmem_limit_bytes=VMEM_LIMIT),
    )(flat, final)


def fused_sizes(mesh, trace):
    shape = mesh.shape
    rows = shape["rows"]
    groups = shape["cols"] * shape["sub"]
    slow_len = trace.shape[1] // shape["groups"]
    fast_len = trace.shape[2]
    side = math.isqrt(slow_len * fast_len)
    fast_local = fast_len // rows
    local_cols = trace.shape[0] // groups
    low_len = side // fast_len
    fits = (
        side * side == slow_len * fast_len
        and low_len * fast_len == side
        and rows == 4
        and groups == rows
        and shape["cols"] == 2
        and shape["sub"] == 2
        and local_cols == 2
        and fast_local == 8
        and 2 * low_len * fast_local == 128
        and rows * groups == 2 * low_len
    )
    return (side, fast_len, fast_local, rows, groups, (shape["cols"], shape["sub"])) if fits else None


def solution(mesh):
    placed = (P(("cols", "sub"), "groups", "rows"),)

    def whole(trace):
        sizes = fused_sizes(mesh, trace)
        return jax.shard_map(
            on_device if sizes is None else partial(fused_on_device, sizes),
            mesh=mesh,
            in_specs=placed,
            out_specs=P("groups", ("rows", "cols", "sub"), None),
            check_vma=False,
        )(trace)

    return whole
```

```python
from functools import partial
import math

import jax
import jax.numpy as jnp
import numpy as np
from jax import lax
from jax.experimental import pallas as pl
from jax.experimental.pallas import tpu as pltpu
from jax.sharding import PartitionSpec as P


def dft_table(extent, orient):
    points = jnp.arange(extent, dtype=jnp.int32)
    product = points[:, None] * points[None, :] % extent
    angles = product.astype(jnp.float32) * (orient * 2.0 * math.pi / extent)
    return (jnp.cos(angles), jnp.sin(angles))


def complex_apply(table_real, table_imag, data_real, data_imag):
    matmul = partial(jnp.dot, precision=lax.Precision.HIGHEST, preferred_element_type=jnp.float32)
    out_real = matmul(table_real, data_real) - matmul(table_imag, data_imag)
    out_imag = matmul(table_real, data_imag) + matmul(table_imag, data_real)
    return (out_real, out_imag)


def rotate(data_real, data_imag, angles):
    cosine = jnp.cos(angles)
    sine = jnp.sin(angles)
    return (data_real * cosine - data_imag * sine, data_real * sine + data_imag * cosine)


def turn(index_product, modulus, orient):
    return (index_product % modulus).astype(jnp.float32) * (orient * 2.0 * math.pi / modulus)


def transform_lead(data_real, data_imag, orient):
    extent = data_real.shape[0]
    rest_shape = data_real.shape[1:]
    breadth = data_real.size // extent
    flat_real = data_real.reshape(extent, breadth)
    flat_imag = data_imag.reshape(extent, breadth)
    if extent <= 128:
        table_real, table_imag = dft_table(extent, orient)
        out_real, out_imag = complex_apply(table_real, table_imag, flat_real, flat_imag)
    else:
        outer_len = extent // 128
        first_real, first_imag = transform_lead(
            flat_real.reshape(outer_len, 128 * breadth),
            flat_imag.reshape(outer_len, 128 * breadth),
            orient,
        )
        first_real = first_real.reshape(outer_len, 128, breadth)
        first_imag = first_imag.reshape(outer_len, 128, breadth)
        outer_index = jnp.arange(outer_len, dtype=jnp.int32)[:, None]
        inner_index = jnp.arange(128, dtype=jnp.int32)[None, :]
        angles = turn(outer_index * inner_index, extent, orient)[:, :, None]
        first_real, first_imag = rotate(first_real, first_imag, angles)
        first_real = jnp.transpose(first_real, (1, 0, 2)).reshape(128, outer_len * breadth)
        first_imag = jnp.transpose(first_imag, (1, 0, 2)).reshape(128, outer_len * breadth)
        out_real, out_imag = transform_lead(first_real, first_imag, orient)
    return (out_real.reshape((extent,) + rest_shape), out_imag.reshape((extent,) + rest_shape))


def times(first, second):
    return (
        first[0] * second[0] - first[1] * second[1],
        first[0] * second[1] + first[1] * second[0],
    )


def plus(first, second):
    return (first[0] + second[0], first[1] + second[1])


def on_device(trace):
    local_cols = trace.shape[0]
    slow_len = trace.shape[1]
    fast_local = trace.shape[2]
    row_parts = lax.axis_size("rows")
    group_parts = lax.axis_size(("cols", "sub"))
    row_index = lax.axis_index("rows")
    group_index = lax.axis_index(("cols", "sub"))
    fast_len = fast_local * row_parts
    trace_len = slow_len * fast_len
    ext_len = 4 * trace_len
    ext_slow = 4 * fast_len
    slow_block = slow_len // row_parts
    ext_block = ext_slow // row_parts
    point_block = ext_block // group_parts
    coeff_block = slow_block // group_parts
    real_part = jnp.transpose(trace, (1, 0, 2))
    imag_part = jnp.zeros_like(real_part)
    real_part, imag_part = transform_lead(real_part, imag_part, 1.0)
    lead_index = jnp.arange(slow_len, dtype=jnp.int32)[:, None, None]
    fast_index = (row_index * fast_local + jnp.arange(fast_local, dtype=jnp.int32))[None, None, :]
    real_part, imag_part = rotate(
        real_part, imag_part, turn(lead_index * fast_index, trace_len, 1.0)
    )
    moved = lax.all_to_all(
        jnp.stack([real_part, imag_part]), "rows", split_axis=1, concat_axis=3, tiled=True
    )
    moved = jnp.transpose(moved, (0, 3, 2, 1))
    real_part, imag_part = transform_lead(moved[0], moved[1], 1.0)
    slow_index = (row_index * slow_block + jnp.arange(slow_block, dtype=jnp.int32))[None, None, :]
    coeff_index = jnp.arange(fast_len, dtype=jnp.int32)[:, None, None] * slow_len + slow_index
    shift_angle = coeff_index.astype(jnp.float32) * (math.pi / (4.0 * trace_len))
    real_part, imag_part = rotate(real_part / trace_len, imag_part / trace_len, shift_angle)
    padding = jnp.zeros((ext_slow - fast_len, local_cols, slow_index.shape[2]), jnp.float32)
    real_part = jnp.concatenate([real_part, padding], 0)
    imag_part = jnp.concatenate([imag_part, padding], 0)
    real_part, imag_part = transform_lead(real_part, imag_part, -1.0)
    ext_index = jnp.arange(ext_slow, dtype=jnp.int32)[:, None, None]
    real_part, imag_part = rotate(real_part, imag_part, turn(ext_index * slow_index, ext_len, -1.0))
    stacked = jnp.stack([real_part, imag_part])
    moved = lax.all_to_all(stacked, "rows", split_axis=1, concat_axis=3, tiled=True)
    moved = jnp.transpose(moved, (0, 3, 2, 1))
    real_part, imag_part = transform_lead(moved[0], moved[1], -1.0)
    joined = lax.all_to_all(
        jnp.stack([real_part, imag_part]), ("cols", "sub"), split_axis=3, concat_axis=2, tiled=True
    )
    real_part = joined[0]
    imag_part = joined[1]

    def column(number):
        return (real_part[:, number], imag_part[:, number])

    wire_a = column(0)
    wire_b = column(1)
    wire_c = column(2)
    gate = times(times(times(column(3), wire_a), wire_b), wire_c)
    gate = plus(gate, times(column(4), wire_a))
    gate = plus(gate, times(column(5), wire_b))
    gate = plus(gate, times(column(6), wire_c))
    gate = plus(gate, column(7))
    point_index = (
        row_index * ext_block + group_index * point_block + jnp.arange(point_block, dtype=jnp.int32)
    )
    quarter = (point_index % 4).astype(jnp.float32)
    vanish_angle = math.pi / 4.0 - math.pi / 2.0 * quarter
    vanish_real = (jnp.cos(vanish_angle) - 1.0)[None, :]
    vanish_imag = jnp.sin(vanish_angle)[None, :]
    magnitude = vanish_real * vanish_real + vanish_imag * vanish_imag
    ratio_real = (gate[0] * vanish_real + gate[1] * vanish_imag) / magnitude
    ratio_imag = (gate[1] * vanish_real - gate[0] * vanish_imag) / magnitude
    real_part, imag_part = transform_lead(ratio_real, ratio_imag, 1.0)
    freq_index = jnp.arange(slow_len, dtype=jnp.int32)[:, None]
    real_part, imag_part = rotate(
        real_part, imag_part, turn(freq_index * point_index[None, :], ext_len, 1.0)
    )
    moved = lax.all_to_all(
        lax.all_to_all(
            jnp.stack([real_part, imag_part]), "rows", split_axis=1, concat_axis=2, tiled=True
        ),
        ("cols", "sub"),
        split_axis=1,
        concat_axis=2,
        tiled=True,
    )
    moved = moved.reshape(2, coeff_block, group_parts, row_parts, point_block)
    moved = jnp.transpose(moved, (0, 3, 2, 4, 1)).reshape(2, ext_slow, coeff_block)
    real_part, imag_part = transform_lead(moved[0], moved[1], 1.0)
    low_index = (
        row_index * slow_block
        + group_index * coeff_block
        + jnp.arange(coeff_block, dtype=jnp.int32)
    )[None, :]
    final_index = jnp.arange(ext_slow, dtype=jnp.int32)[:, None] * slow_len + low_index
    final_angle = final_index.astype(jnp.float32) * (-math.pi / (4.0 * trace_len))
    real_part, imag_part = rotate(real_part, imag_part, final_angle)
    result = jnp.stack([real_part, imag_part]) * (1.0 / math.sqrt(ext_len))
    return jnp.transpose(result, (0, 2, 1))


MESH = pl.DeviceIdType.MESH
CHUNKS = 4
HALVES = 2
LANES = 128
VMEM_LIMIT = 12 * 2**20


def halves(table):
    high = table.astype(jnp.bfloat16)
    low = (table - high.astype(np.float64)).astype(jnp.bfloat16)
    return high, low


def fused_tables(sizes):
    side, fast_len, fast_local, rows, groups, blocks = sizes
    points = side * side
    ext = rows * points
    low_len = side // fast_len
    slow_len = side * low_len
    half = low_len * fast_local
    lows = low_len // HALVES
    cols, subs = blocks
    index = np.arange(side)
    angles = 2.0 * np.pi * (index[:, None] * index[None, :] % side) / side
    dft = np.stack(
        [
            halves(np.concatenate([np.cos(part), np.sin(part)], 1))
            for part in np.split(angles, side // LANES, 1)
        ]
    )
    low_at, fast_at = (
        grid.reshape(-1)
        for grid in np.meshgrid(np.arange(low_len), np.arange(fast_local), indexing="ij")
    )
    freq = low_at[:, None] + low_len * index[None, :]
    centred = freq - slow_len // 2
    members = np.arange(rows)
    inner = fast_local * members[:, None] + fast_at
    theta = 2.0 * np.pi * inner[:, :, None] * centred / points
    base = np.stack([np.cos(theta), np.sin(theta)], 1).astype(np.float32)
    shifts = 0.5 / rows - np.arange(rows) / rows
    angle = centred * (2.0 * np.pi / points) * shifts[:, None, None, None] - theta
    post = np.stack([np.cos(angle), np.sin(angle)], 1).astype(np.float32)
    post = post.reshape(rows, 2, cols, subs, HALVES, lows * fast_local, side)
    post = np.transpose(post, (0, 2, 4, 1, 3, 5, 6)).reshape(rows * cols, HALVES, 2, -1, side)
    slot_at, low_in, fast_in = (
        grid.reshape(-1)
        for grid in np.meshgrid(
            np.arange(rows), np.arange(lows), np.arange(fast_local), indexing="ij"
        )
    )
    inner = fast_local * slot_at + fast_in
    same = low_in[:, None] == low_in[None, :]
    sign = 1.0 - 2.0 * (inner[:, None] % 2)
    kernels = []
    for shift in shifts:
        gap = inner[None, :] - inner[:, None] + shift
        weight = sign / points * np.sin(np.pi * shift) / np.sin(np.pi * gap / fast_len)
        weight = np.where(same, weight, 0.0)
        for part in np.split(weight, cols):
            kernels.append(np.stack(halves(part)))
    kernels = np.stack(kernels)
    spin = 2.0 * np.pi * low_at[:, None] * index[None, :] / slow_len
    spin = np.stack([np.cos(spin), np.sin(spin)]).astype(np.float32)
    row_at, group_at = np.divmod(np.arange(rows * groups), groups)
    digit = rows * (fast_local * group_at[:, None] + fast_at) + row_at[:, None]
    angle = freq * (2 * digit[:, :, None] - 1) % (2 * ext) * (np.pi / ext)
    twist = np.stack([np.cos(angle), np.sin(angle)], 1).astype(np.float32)
    twist = np.stack(np.split(twist, side // LANES, 3), 1)
    source_row, source_group, fast_at = np.meshgrid(
        np.arange(rows), np.arange(groups), np.arange(fast_local), indexing="ij"
    )
    low_digit = rows * (fast_local * source_group + fast_at) + source_row
    vanish = np.exp(1j * (np.pi / rows - 2.0 * np.pi / rows * source_row)) - 1.0
    finals = np.arange(rows * fast_len)
    turns = np.exp(
        2j * np.pi * low_digit[..., None] * finals / (rows * fast_len)
        - 1j * np.pi * slow_len * finals / ext
    ) / (vanish[..., None] * math.sqrt(ext))
    real_rows = np.concatenate([turns.real, turns.imag], -1)
    imag_rows = np.concatenate([-turns.imag, turns.real], -1)
    final = np.stack([real_rows, imag_rows], 2).reshape(-1, 2 * rows * fast_len)
    final = np.stack(halves(final))
    return dft, spin, base, kernels, post, twist, final


def split(value):
    high = value.astype(jnp.bfloat16)
    return high, (value - high.astype(jnp.float32)).astype(jnp.bfloat16)


def dot3(left, right):
    mul = partial(jnp.dot, preferred_element_type=jnp.float32)
    count = left[0].shape[0]
    both = mul(jnp.concatenate(left, 0), right[0])
    return both[:count] + (both[count:] + mul(left[0], right[1]))


def short_transform(values, orient):
    count = len(values)
    if count == 1:
        return values
    even = short_transform(values[0::2], orient)
    odd = short_transform(values[1::2], orient)
    first, second = [], []
    for at in range(count // 2):
        cosine = math.cos(2.0 * math.pi * at / count)
        sine = orient * math.sin(2.0 * math.pi * at / count)
        real, imag = odd[at]
        if at == 0:
            spun = (real, imag)
        elif 4 * at == count:
            spun = (-orient * imag, orient * real)
        else:
            spun = (real * cosine - imag * sine, real * sine + imag * cosine)
        first.append(plus(even[at], spun))
        second.append((even[at][0] - spun[0], even[at][1] - spun[1]))
    return first + second


def fused_kernel(
    sizes,
    x_hbm,
    dft_hbm,
    spin_hbm,
    base_hbm,
    kern_hbm,
    post_hbm,
    twist_hbm,
    out_ref,
    x_ref,
    dft,
    spin,
    base,
    kern,
    post,
    twist,
    edge,
    gathered,
    send_prod,
    recv_prod,
    spread,
    send_tail,
    recv_tail,
    table_sem,
    gather_send,
    gather_recv,
    prod_send,
    prod_recv,
    tail_send,
    tail_recv,
):
    side, fast_len, fast_local, rows, groups, (cols, subs) = sizes
    points = side * side
    low_len = side // fast_len
    half = low_len * fast_local
    lows = low_len // CHUNKS
    deep = lows * fast_local
    thick = CHUNKS // HALVES * deep
    members = rows * groups
    row = lax.axis_index("rows")
    col = lax.axis_index("cols")
    sub = lax.axis_index("sub")
    group = col * subs + sub
    me = row * groups + group

    def place(member):
        inside = lax.rem(member, groups)
        return {
            "rows": lax.div(member, groups),
            "cols": lax.div(inside, subs),
            "sub": lax.rem(inside, subs),
        }

    first_load = pltpu.make_async_copy(x_hbm, x_ref, table_sem.at[0])
    first_load.start()
    barrier = pltpu.get_barrier_semaphore()

    @pl.when(row > 0)
    def _():
        pl.semaphore_signal(barrier, inc=1, device_id={"rows": row - 1}, device_id_type=MESH)

    @pl.when(row < rows - 1)
    def _():
        pl.semaphore_signal(barrier, inc=1, device_id={"rows": row + 1}, device_id_type=MESH)

    for near in ({"cols": 1 - col}, {"sub": 1 - sub}):
        pl.semaphore_signal(barrier, inc=1, device_id=near, device_id_type=MESH)

    loads = [
        first_load,
        pltpu.make_async_copy(spin_hbm, spin, table_sem.at[1]),
        pltpu.make_async_copy(dft_hbm, dft, table_sem.at[2]),
        pltpu.make_async_copy(base_hbm.at[row], base, table_sem.at[3]),
        pltpu.make_async_copy(kern_hbm.at[row * cols + col], kern, table_sem.at[4]),
        pltpu.make_async_copy(post_hbm.at[row * cols + col], post, table_sem.at[5]),
        pltpu.make_async_copy(twist_hbm.at[me], twist, table_sem.at[6]),
    ]
    for load in loads[1:4]:
        load.start()

    def stacked(values):
        return jnp.concatenate([value for value in values], 0)

    def slices(real, imag):
        return [
            (real[at * fast_local : (at + 1) * fast_local], imag[at * fast_local : (at + 1) * fast_local])
            for at in range(low_len)
        ]

    def lane_tile(data, tile, orient):
        count = data[0].shape[0] // 2
        out = dot3(data, (dft[tile, 0], dft[tile, 1]))
        cosines, sines = out[:, :LANES], out[:, LANES:]
        return (
            cosines[:count] - orient * sines[count:],
            cosines[count:] + orient * sines[:count],
        )

    def lane_transform(real, imag, orient):
        data = split(jnp.concatenate([real, imag], 0))
        tiles = [lane_tile(data, tile, orient) for tile in range(side // LANES)]
        return tuple(jnp.concatenate([tile[at] for tile in tiles], 1) for at in range(2))

    loads[0].wait()
    values = [
        (
            x_ref[0, :, at * side : (at + 1) * side],
            x_ref[1, :, at * side : (at + 1) * side],
        )
        for at in range(low_len)
    ]
    values = short_transform(values, 1.0)
    real = stacked([value[0] for value in values])
    imag = stacked([value[1] for value in values])
    loads[1].wait()
    real, imag = times((real, imag), (spin[0], spin[1]))
    loads[2].wait()
    real, imag = lane_transform(real, imag, 1.0)
    loads[3].wait()
    real, imag = times((real, imag), (base[0], base[1]))
    for chunk in range(CHUNKS):
        gathered[row, col, chunk, 0] = real[chunk * deep : (chunk + 1) * deep]
        gathered[row, col, chunk, 1] = imag[chunk * deep : (chunk + 1) * deep]

    pl.semaphore_wait(
        barrier,
        2 + (row > 0).astype(jnp.int32) + (row < rows - 1).astype(jnp.int32),
    )

    inner = (row > 0) & (row < rows - 1)
    outer = jnp.logical_not(inner)
    end = jnp.where(2 * row < rows, 0, rows - 1)
    far = rows - 1 - end
    beside = jnp.where(row == 0, 1, jnp.where(row == rows - 1, rows - 2, rows - 1 - row))
    other = jnp.where(inner, end, jnp.where(end == 0, rows - 2, 1))
    across = {"cols": 1 - col}

    def hop(slot, pair, chunk, way, target):
        return pltpu.make_async_remote_copy(
            src_ref=gathered.at[slot, pair, chunk],
            dst_ref=gathered.at[slot, pair, chunk],
            send_sem=gather_send.at[way, chunk],
            recv_sem=gather_recv.at[slot, pair, chunk],
            device_id=target,
            device_id_type=MESH,
        )

    def arrive(slot, pair, chunk):
        hop(slot, pair, chunk, 0, across).wait_recv()

    def own_moves(chunk):
        return [
            (None, hop(row, col, chunk, 0, {"rows": beside})),
            (inner, hop(row, col, chunk, 1, {"rows": end})),
            (None, hop(row, col, chunk, 2, across)),
        ]

    def beside_moves(chunk):
        return [
            (inner, hop(beside, col, chunk, 3, {"rows": end})),
            (None, hop(beside, col, chunk, 4, across)),
        ]

    def other_moves(chunk):
        return [
            (inner, hop(other, col, chunk, 5, {"rows": beside})),
            (None, hop(other, col, chunk, 6, across)),
        ]

    def far_moves(chunk):
        return [
            (inner, hop(far, col, chunk, 7, {"rows": end})),
            (None, hop(far, col, chunk, 8, across)),
        ]

    def begin(moves):
        for need, move in moves:
            if need is None:
                move.start()
            else:
                pl.when(need)(move.start)

    def begin_if(need, moves):
        for on, move in moves:
            if on is None or on is need:
                move.start()

    def finish(moves):
        for need, move in moves:
            if need is None:
                move.wait_send()
            else:
                pl.when(need)(move.wait_send)

    for chunk in range(CHUNKS):
        begin(own_moves(chunk))
    for load in loads[4:]:
        load.start()

    shift = 0.5 / rows - row.astype(jnp.float32) / rows
    half_turn = jnp.zeros((1, 1), jnp.float32) + shift * math.pi
    half_cos = jnp.cos(half_turn)
    half_sin = jnp.sin(half_turn)
    edge_at = lax.broadcasted_iota(jnp.int32, edge.shape[1:], 0)
    edge_lane = lax.broadcasted_iota(jnp.int32, edge.shape[1:], 1)
    edge_angle = edge_at.astype(jnp.float32) * (math.pi / fast_len)
    edge[0] = jnp.where(edge_lane == 0, jnp.cos(edge_angle) * (1.0 / points), 0.0)
    edge[1] = jnp.where(edge_lane == 0, jnp.sin(edge_angle) * (1.0 / points), 0.0)

    def prod_copy(pair, part, origin):
        span = pl.ds(0, 2 * thick + (8 if part == 0 else 0))
        return pltpu.make_async_remote_copy(
            src_ref=send_prod.at[pair, part, span],
            dst_ref=recv_prod.at[pair * subs + origin, part, span],
            send_sem=prod_send.at[pair, part],
            recv_sem=prod_recv.at[pair * subs + origin, part],
            device_id={"sub": 1 - sub},
            device_id_type=MESH,
        )

    def part_chunks(part):
        return range(part * CHUNKS // HALVES, (part + 1) * CHUNKS // HALVES)

    def contract(pair, part):
        chunks = part_chunks(part)
        real, imag = (
            stacked([gathered[slot, pair, chunk, at] for slot in range(rows) for chunk in chunks])
            for at in range(2)
        )
        data = split(jnp.concatenate([real, imag], 1))
        moved = dot3((kern[0], kern[1]), data)
        real, imag = times((moved[:, :side], moved[:, side:]), (post[part, 0], post[part, 1]))
        mine = pair * subs + sub
        if part == 0:
            firsts = tuple(
                stacked([gathered[slot, pair, 0, at, :fast_local, :128] for slot in range(rows)])
                for at in range(2)
            )
            mean_a, mean_b = (
                jnp.sum(jnp.sum(raw, 0, keepdims=True), 1, keepdims=True)
                for raw in times(firsts, (edge[0], edge[1]))
            )
            row_at = lax.broadcasted_iota(jnp.int32, real.shape, 0)
            lane_at = lax.broadcasted_iota(jnp.int32, real.shape, 1)
            constant = (lane_at == 0) & (row_at % thick < fast_local)
            parity = jnp.where(constant, (1 - 2 * (row_at % 2)).astype(jnp.float32), 0.0)
            real = real - parity * (mean_a * half_cos + mean_b * half_sin)
            imag = imag - parity * (mean_b * half_cos - mean_a * half_sin)
            side_at = lax.broadcasted_iota(jnp.int32, (8, side), 1)
            means = jnp.where(side_at < side // 2, mean_a, mean_b)
            send_prod[pair, part, 2 * thick :] = means
            recv_prod[mine, part, 2 * thick :] = means

        for at in range(subs):
            span = slice(at * thick, (at + 1) * thick)

            @pl.when(sub == at)
            def _():
                recv_prod[mine, part, :thick] = real[span]
                recv_prod[mine, part, thick : 2 * thick] = imag[span]

            @pl.when(sub != at)
            def _():
                send_prod[pair, part, :thick] = real[span]
                send_prod[pair, part, thick : 2 * thick] = imag[span]

        prod_copy(pair, part, sub).start()

    def expand(pair):
        for part in range(HALVES):
            prod_copy(pair, part, 1 - sub).wait_recv()
        real, imag = (
            stacked(
                [
                    recv_prod[pair * subs + origin, part, at * thick : (at + 1) * thick]
                    for origin in range(subs)
                    for part in range(HALVES)
                ]
            )
            for at in range(2)
        )
        real, imag = lane_transform(real, imag, -1.0)
        for origin in range(subs):
            span = slice(origin * half, (origin + 1) * half)
            turned = times((real[span], imag[span]), (spin[0], -spin[1]))
            values = short_transform(slices(*turned), -1.0)
            for at in range(2):
                spread[pair * subs + origin, at] = stacked([value[at] for value in values])

    @pl.when(inner)
    def _():
        for chunk in range(CHUNKS):
            arrive(other, col, chunk)
            begin_if(inner, other_moves(chunk))
            arrive(beside, col, chunk)
            begin_if(inner, beside_moves(chunk))
        for chunk in range(CHUNKS):
            arrive(far, col, chunk)
            begin_if(inner, far_moves(chunk))

    @pl.when(outer)
    def _():
        for slot, moves in ((beside, beside_moves), (other, other_moves), (far, far_moves)):
            for chunk in range(CHUNKS):
                arrive(slot, col, chunk)
                begin_if(outer, moves(chunk))

    loads[4].wait()
    loads[5].wait()
    for part in range(HALVES):
        contract(col, part)
    expand(col)
    for part in range(HALVES):
        for slot in (row, beside, other, far):
            for chunk in part_chunks(part):
                arrive(slot, 1 - col, chunk)
        contract(1 - col, part)
    expand(1 - col)

    at_row = lax.broadcasted_iota(jnp.int32, (half, side), 0)
    flip = (1 - 2 * (at_row % 2)).astype(jnp.float32)
    part_cos = flip * half_cos
    part_sin = flip * half_sin

    def value(number):
        block, at = divmod(number, 2)
        lane_from = at * (side // 2)
        mean = recv_prod[block, 0, 2 * thick : 2 * thick + 1, lane_from : lane_from + 1]
        data = spread[block, at]
        return (mean + part_cos * data, part_sin * data)

    wire_a = value(0)
    wire_b = value(1)
    wire_c = value(2)
    gate = times(times(times(value(3), wire_a), wire_b), wire_c)
    gate = plus(gate, times(value(4), wire_a))
    gate = plus(gate, times(value(5), wire_b))
    gate = plus(gate, times(value(6), wire_c))
    gate = plus(gate, value(7))
    values = short_transform(slices(*gate), 1.0)
    real = stacked([value[0] for value in values])
    imag = stacked([value[1] for value in values])
    real, imag = times((real, imag), (spin[0], spin[1]))
    loads[6].wait()
    data = split(jnp.concatenate([real, imag], 0))
    breadth = side * low_len // members
    lane_piece = side // members
    tile_lanes = low_len * lane_piece
    tiles = side // tile_lanes
    lanes = lax.broadcasted_iota(jnp.int32, (2 * fast_local, tile_lanes), 1)
    low_side = (2 * row < rows).astype(jnp.int32)

    def tail_copy(target, slot):
        return pltpu.make_async_remote_copy(
            src_ref=send_tail.at[target],
            dst_ref=recv_tail.at[slot],
            send_sem=tail_send.at[target],
            recv_sem=tail_recv.at[slot],
            device_id=place(target),
            device_id_type=MESH,
        )

    for turn_at in range(tiles):
        tile = lax.rem(low_side + turn_at, tiles)
        real, imag = times(lane_tile(data, tile, 1.0), (twist[tile, 0], twist[tile, 1]))
        pieces = [
            jnp.concatenate(
                [
                    real[at * fast_local : (at + 1) * fast_local],
                    imag[at * fast_local : (at + 1) * fast_local],
                ],
                0,
            )
            for at in range(low_len)
        ]
        bit = low_len // 2
        while bit:
            keep = (lanes // (lane_piece * bit)) % 2 == 0
            for at in range(low_len):
                if at & bit == 0:
                    one, two = pieces[at], pieces[at + bit]
                    pieces[at] = jnp.where(keep, one, pltpu.roll(two, lane_piece * bit, 1))
                    pieces[at + bit] = jnp.where(
                        keep, pltpu.roll(one, tile_lanes - lane_piece * bit, 1), two
                    )
            bit //= 2
        for at in range(low_len):
            send_tail[tile * low_len + at] = pieces[at]
        for at in range(low_len):
            target = tile * low_len + lax.rem(at + low_side * (low_len // 2), low_len)

            @pl.when(target != me)
            def _():
                tail_copy(target, me).start()

    recv_tail[me] = send_tail[me]
    for step in range(1, members):
        source = lax.rem(me + step, members)
        tail_copy(source, source).wait_recv()
    out_ref[...] = recv_tail[...].reshape(members * 2 * fast_local, breadth)

    for step in range(1, members):
        target = lax.rem(me + step, members)
        tail_copy(target, me).wait_send()
    for pair in range(cols):
        for part in range(HALVES):
            prod_copy(pair, part, sub).wait_send()
    for chunk in range(CHUNKS):
        for moves in (
            own_moves,
            beside_moves,
            other_moves,
            far_moves,
        ):
            finish(moves(chunk))


def final_kernel(sizes, flat_ref, final_ref, out_ref):
    side, fast_len, fast_local, rows, groups, blocks = sizes
    low_len = side // fast_len
    lane_piece = side // (rows * groups)
    data = split(jnp.transpose(flat_ref[...]))
    result = dot3(data, (final_ref[0], final_ref[1]))
    for at in range(low_len):
        picked = result[at * lane_piece : (at + 1) * lane_piece]
        rows_at = pl.ds(at, lane_piece, stride=low_len)
        out_ref[0, rows_at] = picked[:, : rows * fast_len]
        out_ref[1, rows_at] = picked[:, rows * fast_len :]


def fused_on_device(sizes, trace):
    side, fast_len, fast_local, rows, groups, (cols, subs) = sizes
    low_len = side // fast_len
    half = low_len * fast_local
    deep = half // CHUNKS
    members = rows * groups
    *tables, final = [jnp.asarray(table) for table in fused_tables(sizes)]
    thick = half // HALVES
    block = jnp.transpose(trace, (0, 2, 1))
    vmem = pltpu.VMEM
    bf16 = jnp.bfloat16
    f32 = jnp.float32
    dma = pltpu.SemaphoreType.DMA
    breadth = side * low_len // members
    flat = pl.pallas_call(
        partial(fused_kernel, sizes),
        out_shape=vmem((members * 2 * fast_local, breadth), f32),
        in_specs=[pl.BlockSpec(memory_space=pltpu.HBM)] * (1 + len(tables)),
        out_specs=pl.BlockSpec(memory_space=vmem),
        scratch_shapes=[
            vmem(block.shape, f32),
            vmem((side // LANES, 2, side, side), bf16),
            vmem((2, half, side), f32),
            vmem((2, half, side), f32),
            vmem((2, subs * thick, rows * thick), bf16),
            vmem((HALVES, 2, subs * thick, side), f32),
            vmem((side // LANES, 2, half, LANES), f32),
            vmem((2, fast_len, 128), f32),
            vmem((rows, cols, CHUNKS, 2, deep, side), f32),
            vmem((cols, HALVES, 2 * thick + 8, side), f32),
            vmem((groups, HALVES, 2 * thick + 8, side), f32),
            vmem((groups, 2, half, side), f32),
            vmem((members, 2 * fast_local, breadth), f32),
            vmem((members, 2 * fast_local, breadth), f32),
            dma((8,)),
            dma((9, CHUNKS)),
            dma((rows, cols, CHUNKS)),
            dma((cols, HALVES)),
            dma((groups, HALVES)),
            dma((members,)),
            dma((members,)),
        ],
        compiler_params=pltpu.CompilerParams(
            collective_id=0, has_side_effects=True, vmem_limit_bytes=VMEM_LIMIT
        ),
    )(*[pltpu.with_memory_space_constraint(table, pltpu.HBM) for table in (block, *tables)])
    return pl.pallas_call(
        partial(final_kernel, sizes),
        out_shape=jax.ShapeDtypeStruct((2, breadth, rows * fast_len), f32),
        in_specs=[pl.BlockSpec(memory_space=vmem)] * 2,
        out_specs=pl.BlockSpec(memory_space=vmem),
        compiler_params=pltpu.CompilerParams(vmem_limit_bytes=VMEM_LIMIT),
    )(flat, final)


def fused_sizes(mesh, trace):
    shape = mesh.shape
    rows = shape["rows"]
    groups = shape["cols"] * shape["sub"]
    slow_len = trace.shape[1] // shape["groups"]
    fast_len = trace.shape[2]
    side = math.isqrt(slow_len * fast_len)
    fast_local = fast_len // rows
    local_cols = trace.shape[0] // groups
    low_len = side // fast_len
    fits = (
        side * side == slow_len * fast_len
        and low_len * fast_len == side
        and rows == 4
        and groups == rows
        and shape["cols"] == 2
        and shape["sub"] == 2
        and local_cols == 2
        and fast_local == 8
        and 2 * low_len * fast_local == 128
        and rows * groups == 2 * low_len
        and side == 2 * LANES
    )
    return (side, fast_len, fast_local, rows, groups, (shape["cols"], shape["sub"])) if fits else None


def solution(mesh):
    placed = (P(("cols", "sub"), "groups", "rows"),)

    def whole(trace):
        sizes = fused_sizes(mesh, trace)
        return jax.shard_map(
            on_device if sizes is None else partial(fused_on_device, sizes),
            mesh=mesh,
            in_specs=placed,
            out_specs=P("groups", ("rows", "cols", "sub"), None),
            check_vma=False,
        )(trace)

    return whole
```

```python
from functools import partial
import math

import jax
import jax.numpy as jnp
import numpy as np
from jax import lax
from jax.experimental import pallas as pl
from jax.experimental.pallas import tpu as pltpu
from jax.sharding import PartitionSpec as P


def dft_table(extent, orient):
    points = jnp.arange(extent, dtype=jnp.int32)
    product = points[:, None] * points[None, :] % extent
    angles = product.astype(jnp.float32) * (orient * 2.0 * math.pi / extent)
    return (jnp.cos(angles), jnp.sin(angles))


def complex_apply(table_real, table_imag, data_real, data_imag):
    matmul = partial(jnp.dot, precision=lax.Precision.HIGHEST, preferred_element_type=jnp.float32)
    out_real = matmul(table_real, data_real) - matmul(table_imag, data_imag)
    out_imag = matmul(table_real, data_imag) + matmul(table_imag, data_real)
    return (out_real, out_imag)


def rotate(data_real, data_imag, angles):
    cosine = jnp.cos(angles)
    sine = jnp.sin(angles)
    return (data_real * cosine - data_imag * sine, data_real * sine + data_imag * cosine)


def turn(index_product, modulus, orient):
    return (index_product % modulus).astype(jnp.float32) * (orient * 2.0 * math.pi / modulus)


def transform_lead(data_real, data_imag, orient):
    extent = data_real.shape[0]
    rest_shape = data_real.shape[1:]
    breadth = data_real.size // extent
    flat_real = data_real.reshape(extent, breadth)
    flat_imag = data_imag.reshape(extent, breadth)
    if extent <= 128:
        table_real, table_imag = dft_table(extent, orient)
        out_real, out_imag = complex_apply(table_real, table_imag, flat_real, flat_imag)
    else:
        outer_len = extent // 128
        first_real, first_imag = transform_lead(
            flat_real.reshape(outer_len, 128 * breadth),
            flat_imag.reshape(outer_len, 128 * breadth),
            orient,
        )
        first_real = first_real.reshape(outer_len, 128, breadth)
        first_imag = first_imag.reshape(outer_len, 128, breadth)
        outer_index = jnp.arange(outer_len, dtype=jnp.int32)[:, None]
        inner_index = jnp.arange(128, dtype=jnp.int32)[None, :]
        angles = turn(outer_index * inner_index, extent, orient)[:, :, None]
        first_real, first_imag = rotate(first_real, first_imag, angles)
        first_real = jnp.transpose(first_real, (1, 0, 2)).reshape(128, outer_len * breadth)
        first_imag = jnp.transpose(first_imag, (1, 0, 2)).reshape(128, outer_len * breadth)
        out_real, out_imag = transform_lead(first_real, first_imag, orient)
    return (out_real.reshape((extent,) + rest_shape), out_imag.reshape((extent,) + rest_shape))


def times(first, second):
    return (
        first[0] * second[0] - first[1] * second[1],
        first[0] * second[1] + first[1] * second[0],
    )


def plus(first, second):
    return (first[0] + second[0], first[1] + second[1])


def on_device(trace):
    local_cols = trace.shape[0]
    slow_len = trace.shape[1]
    fast_local = trace.shape[2]
    row_parts = lax.axis_size("rows")
    group_parts = lax.axis_size(("cols", "sub"))
    row_index = lax.axis_index("rows")
    group_index = lax.axis_index(("cols", "sub"))
    fast_len = fast_local * row_parts
    trace_len = slow_len * fast_len
    ext_len = 4 * trace_len
    ext_slow = 4 * fast_len
    slow_block = slow_len // row_parts
    ext_block = ext_slow // row_parts
    point_block = ext_block // group_parts
    coeff_block = slow_block // group_parts
    real_part = jnp.transpose(trace, (1, 0, 2))
    imag_part = jnp.zeros_like(real_part)
    real_part, imag_part = transform_lead(real_part, imag_part, 1.0)
    lead_index = jnp.arange(slow_len, dtype=jnp.int32)[:, None, None]
    fast_index = (row_index * fast_local + jnp.arange(fast_local, dtype=jnp.int32))[None, None, :]
    real_part, imag_part = rotate(
        real_part, imag_part, turn(lead_index * fast_index, trace_len, 1.0)
    )
    moved = lax.all_to_all(
        jnp.stack([real_part, imag_part]), "rows", split_axis=1, concat_axis=3, tiled=True
    )
    moved = jnp.transpose(moved, (0, 3, 2, 1))
    real_part, imag_part = transform_lead(moved[0], moved[1], 1.0)
    slow_index = (row_index * slow_block + jnp.arange(slow_block, dtype=jnp.int32))[None, None, :]
    coeff_index = jnp.arange(fast_len, dtype=jnp.int32)[:, None, None] * slow_len + slow_index
    shift_angle = coeff_index.astype(jnp.float32) * (math.pi / (4.0 * trace_len))
    real_part, imag_part = rotate(real_part / trace_len, imag_part / trace_len, shift_angle)
    padding = jnp.zeros((ext_slow - fast_len, local_cols, slow_index.shape[2]), jnp.float32)
    real_part = jnp.concatenate([real_part, padding], 0)
    imag_part = jnp.concatenate([imag_part, padding], 0)
    real_part, imag_part = transform_lead(real_part, imag_part, -1.0)
    ext_index = jnp.arange(ext_slow, dtype=jnp.int32)[:, None, None]
    real_part, imag_part = rotate(real_part, imag_part, turn(ext_index * slow_index, ext_len, -1.0))
    stacked = jnp.stack([real_part, imag_part])
    moved = lax.all_to_all(stacked, "rows", split_axis=1, concat_axis=3, tiled=True)
    moved = jnp.transpose(moved, (0, 3, 2, 1))
    real_part, imag_part = transform_lead(moved[0], moved[1], -1.0)
    joined = lax.all_to_all(
        jnp.stack([real_part, imag_part]), ("cols", "sub"), split_axis=3, concat_axis=2, tiled=True
    )
    real_part = joined[0]
    imag_part = joined[1]

    def column(number):
        return (real_part[:, number], imag_part[:, number])

    wire_a = column(0)
    wire_b = column(1)
    wire_c = column(2)
    gate = times(times(times(column(3), wire_a), wire_b), wire_c)
    gate = plus(gate, times(column(4), wire_a))
    gate = plus(gate, times(column(5), wire_b))
    gate = plus(gate, times(column(6), wire_c))
    gate = plus(gate, column(7))
    point_index = (
        row_index * ext_block + group_index * point_block + jnp.arange(point_block, dtype=jnp.int32)
    )
    quarter = (point_index % 4).astype(jnp.float32)
    vanish_angle = math.pi / 4.0 - math.pi / 2.0 * quarter
    vanish_real = (jnp.cos(vanish_angle) - 1.0)[None, :]
    vanish_imag = jnp.sin(vanish_angle)[None, :]
    magnitude = vanish_real * vanish_real + vanish_imag * vanish_imag
    ratio_real = (gate[0] * vanish_real + gate[1] * vanish_imag) / magnitude
    ratio_imag = (gate[1] * vanish_real - gate[0] * vanish_imag) / magnitude
    real_part, imag_part = transform_lead(ratio_real, ratio_imag, 1.0)
    freq_index = jnp.arange(slow_len, dtype=jnp.int32)[:, None]
    real_part, imag_part = rotate(
        real_part, imag_part, turn(freq_index * point_index[None, :], ext_len, 1.0)
    )
    moved = lax.all_to_all(
        lax.all_to_all(
            jnp.stack([real_part, imag_part]), "rows", split_axis=1, concat_axis=2, tiled=True
        ),
        ("cols", "sub"),
        split_axis=1,
        concat_axis=2,
        tiled=True,
    )
    moved = moved.reshape(2, coeff_block, group_parts, row_parts, point_block)
    moved = jnp.transpose(moved, (0, 3, 2, 4, 1)).reshape(2, ext_slow, coeff_block)
    real_part, imag_part = transform_lead(moved[0], moved[1], 1.0)
    low_index = (
        row_index * slow_block
        + group_index * coeff_block
        + jnp.arange(coeff_block, dtype=jnp.int32)
    )[None, :]
    final_index = jnp.arange(ext_slow, dtype=jnp.int32)[:, None] * slow_len + low_index
    final_angle = final_index.astype(jnp.float32) * (-math.pi / (4.0 * trace_len))
    real_part, imag_part = rotate(real_part, imag_part, final_angle)
    result = jnp.stack([real_part, imag_part]) * (1.0 / math.sqrt(ext_len))
    return jnp.transpose(result, (0, 2, 1))


MESH = pl.DeviceIdType.MESH
CHUNKS = 4
HALVES = 2
LANES = 128
VMEM_LIMIT = 12 * 2**20


def halves(table):
    high = table.astype(jnp.bfloat16)
    low = (table - high.astype(np.float64)).astype(jnp.bfloat16)
    return high, low


def fused_tables(sizes):
    side, fast_len, fast_local, rows, groups, blocks = sizes
    points = side * side
    ext = rows * points
    low_len = side // fast_len
    slow_len = side * low_len
    half = low_len * fast_local
    lows = low_len // HALVES
    cols, subs = blocks
    index = np.arange(side)
    angles = 2.0 * np.pi * (index[:, None] * index[None, :] % side) / side
    dft = np.stack(
        [
            halves(np.concatenate([np.cos(part), np.sin(part)], 1))
            for part in np.split(angles, side // LANES, 1)
        ]
    )
    low_at, fast_at = (
        grid.reshape(-1)
        for grid in np.meshgrid(np.arange(low_len), np.arange(fast_local), indexing="ij")
    )
    freq = low_at[:, None] + low_len * index[None, :]
    centred = freq - slow_len // 2
    members = np.arange(rows)
    inner = fast_local * members[:, None] + fast_at
    theta = 2.0 * np.pi * inner[:, :, None] * centred / points
    base = np.stack([np.cos(theta), np.sin(theta)], 1).astype(np.float32)
    shifts = 0.5 / rows - np.arange(rows) / rows
    angle = centred * (2.0 * np.pi / points) * shifts[:, None, None, None] - theta
    post = np.stack([np.cos(angle), np.sin(angle)], 1).astype(np.float32)
    post = post.reshape(rows, 2, cols, subs, HALVES, lows * fast_local, side)
    post = np.transpose(post, (0, 2, 4, 1, 3, 5, 6)).reshape(rows * cols, HALVES, 2, -1, side)
    slot_at, low_in, fast_in = (
        grid.reshape(-1)
        for grid in np.meshgrid(
            np.arange(rows), np.arange(lows), np.arange(fast_local), indexing="ij"
        )
    )
    inner = fast_local * slot_at + fast_in
    same = low_in[:, None] == low_in[None, :]
    sign = 1.0 - 2.0 * (inner[:, None] % 2)
    kernels = []
    for shift in shifts:
        gap = inner[None, :] - inner[:, None] + shift
        weight = sign / points * np.sin(np.pi * shift) / np.sin(np.pi * gap / fast_len)
        weight = np.where(same, weight, 0.0)
        for part in np.split(weight, cols):
            kernels.append(np.stack(halves(part)))
    kernels = np.stack(kernels)
    spin = 2.0 * np.pi * low_at[:, None] * index[None, :] / slow_len
    spin = np.stack([np.cos(spin), np.sin(spin)]).astype(np.float32)
    row_at, group_at = np.divmod(np.arange(rows * groups), groups)
    digit = rows * (fast_local * group_at[:, None] + fast_at) + row_at[:, None]
    angle = freq * (2 * digit[:, :, None] - 1) % (2 * ext) * (np.pi / ext)
    twist = np.stack([np.cos(angle), np.sin(angle)], 1).astype(np.float32)
    twist = np.stack(np.split(twist, side // LANES, 3), 1)
    source_row, source_group, fast_at = np.meshgrid(
        np.arange(rows), np.arange(groups), np.arange(fast_local), indexing="ij"
    )
    low_digit = rows * (fast_local * source_group + fast_at) + source_row
    vanish = np.exp(1j * (np.pi / rows - 2.0 * np.pi / rows * source_row)) - 1.0
    finals = np.arange(rows * fast_len)
    turns = np.exp(
        2j * np.pi * low_digit[..., None] * finals / (rows * fast_len)
        - 1j * np.pi * slow_len * finals / ext
    ) / (vanish[..., None] * math.sqrt(ext))
    real_rows = np.concatenate([turns.real, turns.imag], -1)
    imag_rows = np.concatenate([-turns.imag, turns.real], -1)
    final = np.stack([real_rows, imag_rows], 2).reshape(-1, 2 * rows * fast_len)
    final = np.stack(halves(final))
    return dft, spin, base, kernels, post, twist, final


def split(value):
    high = value.astype(jnp.bfloat16)
    return high, (value - high.astype(jnp.float32)).astype(jnp.bfloat16)


def dot3(left, right):
    mul = partial(jnp.dot, preferred_element_type=jnp.float32)
    count = left[0].shape[0]
    both = mul(jnp.concatenate(left, 0), right[0])
    return both[:count] + (both[count:] + mul(left[0], right[1]))


def short_transform(values, orient):
    count = len(values)
    if count == 1:
        return values
    even = short_transform(values[0::2], orient)
    odd = short_transform(values[1::2], orient)
    first, second = [], []
    for at in range(count // 2):
        cosine = math.cos(2.0 * math.pi * at / count)
        sine = orient * math.sin(2.0 * math.pi * at / count)
        real, imag = odd[at]
        if at == 0:
            spun = (real, imag)
        elif 4 * at == count:
            spun = (-orient * imag, orient * real)
        else:
            spun = (real * cosine - imag * sine, real * sine + imag * cosine)
        first.append(plus(even[at], spun))
        second.append((even[at][0] - spun[0], even[at][1] - spun[1]))
    return first + second


def fused_kernel(
    sizes,
    x_hbm,
    dft_hbm,
    spin_hbm,
    base_hbm,
    kern_hbm,
    post_hbm,
    twist_hbm,
    out_ref,
    x_ref,
    dft,
    spin,
    base,
    kern,
    post,
    twist,
    edge,
    gathered,
    send_prod,
    recv_prod,
    spread,
    send_tail,
    recv_tail,
    table_sem,
    gather_send,
    gather_recv,
    prod_send,
    prod_recv,
    tail_send,
    tail_recv,
):
    side, fast_len, fast_local, rows, groups, (cols, subs) = sizes
    points = side * side
    low_len = side // fast_len
    half = low_len * fast_local
    lows = low_len // CHUNKS
    deep = lows * fast_local
    thick = CHUNKS // HALVES * deep
    members = rows * groups
    row = lax.axis_index("rows")
    col = lax.axis_index("cols")
    sub = lax.axis_index("sub")
    group = col * subs + sub
    me = row * groups + group

    def place(member):
        inside = lax.rem(member, groups)
        return {
            "rows": lax.div(member, groups),
            "cols": lax.div(inside, subs),
            "sub": lax.rem(inside, subs),
        }

    first_load = pltpu.make_async_copy(x_hbm, x_ref, table_sem.at[0])
    first_load.start()
    barrier = pltpu.get_barrier_semaphore()

    @pl.when(row > 0)
    def _():
        pl.semaphore_signal(barrier, inc=1, device_id={"rows": row - 1}, device_id_type=MESH)

    @pl.when(row < rows - 1)
    def _():
        pl.semaphore_signal(barrier, inc=1, device_id={"rows": row + 1}, device_id_type=MESH)

    for near in ({"cols": 1 - col}, {"sub": 1 - sub}):
        pl.semaphore_signal(barrier, inc=1, device_id=near, device_id_type=MESH)

    loads = [
        first_load,
        pltpu.make_async_copy(spin_hbm, spin, table_sem.at[1]),
        pltpu.make_async_copy(dft_hbm, dft, table_sem.at[2]),
        pltpu.make_async_copy(base_hbm.at[row], base, table_sem.at[3]),
        pltpu.make_async_copy(kern_hbm.at[row * cols + col], kern, table_sem.at[4]),
        pltpu.make_async_copy(post_hbm.at[row * cols + col], post, table_sem.at[5]),
        pltpu.make_async_copy(twist_hbm.at[me], twist, table_sem.at[6]),
    ]
    for load in loads[1:4]:
        load.start()

    def stacked(values):
        return jnp.concatenate([value for value in values], 0)

    def slices(real, imag):
        return [
            (real[at * fast_local : (at + 1) * fast_local], imag[at * fast_local : (at + 1) * fast_local])
            for at in range(low_len)
        ]

    def lane_tile(data, tile, orient):
        count = data[0].shape[0] // 2
        out = dot3(data, (dft[tile, 0], dft[tile, 1]))
        cosines, sines = out[:, :LANES], out[:, LANES:]
        return (
            cosines[:count] - orient * sines[count:],
            cosines[count:] + orient * sines[:count],
        )

    def lane_transform(real, imag, orient):
        data = split(jnp.concatenate([real, imag], 0))
        tiles = [lane_tile(data, tile, orient) for tile in range(side // LANES)]
        return tuple(jnp.concatenate([tile[at] for tile in tiles], 1) for at in range(2))

    loads[0].wait()
    values = [
        (
            x_ref[0, :, at * side : (at + 1) * side],
            x_ref[1, :, at * side : (at + 1) * side],
        )
        for at in range(low_len)
    ]
    values = short_transform(values, 1.0)
    real = stacked([value[0] for value in values])
    imag = stacked([value[1] for value in values])
    loads[1].wait()
    real, imag = times((real, imag), (spin[0], spin[1]))
    loads[2].wait()
    loads[3].wait()
    spread_rows = (real, imag)

    def prepare(part):
        span = slice(part * thick, (part + 1) * thick)
        real, imag = lane_transform(spread_rows[0][span], spread_rows[1][span], 1.0)
        real, imag = times((real, imag), (base[0, span], base[1, span]))
        for order in range(CHUNKS // HALVES):
            chunk = part * CHUNKS // HALVES + order
            gathered[row, col, chunk, 0] = real[order * deep : (order + 1) * deep]
            gathered[row, col, chunk, 1] = imag[order * deep : (order + 1) * deep]

    prepare(0)
    pl.semaphore_wait(
        barrier,
        2 + (row > 0).astype(jnp.int32) + (row < rows - 1).astype(jnp.int32),
    )

    inner = (row > 0) & (row < rows - 1)
    outer = jnp.logical_not(inner)
    end = jnp.where(2 * row < rows, 0, rows - 1)
    far = rows - 1 - end
    beside = jnp.where(row == 0, 1, jnp.where(row == rows - 1, rows - 2, rows - 1 - row))
    other = jnp.where(inner, end, jnp.where(end == 0, rows - 2, 1))
    across = {"cols": 1 - col}

    def hop(slot, pair, chunk, way, target):
        return pltpu.make_async_remote_copy(
            src_ref=gathered.at[slot, pair, chunk],
            dst_ref=gathered.at[slot, pair, chunk],
            send_sem=gather_send.at[way, chunk],
            recv_sem=gather_recv.at[slot, pair, chunk],
            device_id=target,
            device_id_type=MESH,
        )

    def arrive(slot, pair, chunk):
        hop(slot, pair, chunk, 0, across).wait_recv()

    def own_moves(chunk):
        return [
            (None, hop(row, col, chunk, 0, {"rows": beside})),
            (inner, hop(row, col, chunk, 1, {"rows": end})),
            (None, hop(row, col, chunk, 2, across)),
        ]

    def beside_moves(chunk):
        return [
            (inner, hop(beside, col, chunk, 3, {"rows": end})),
            (None, hop(beside, col, chunk, 4, across)),
        ]

    def other_moves(chunk):
        return [
            (inner, hop(other, col, chunk, 5, {"rows": beside})),
            (None, hop(other, col, chunk, 6, across)),
        ]

    def far_moves(chunk):
        return [
            (inner, hop(far, col, chunk, 7, {"rows": end})),
            (None, hop(far, col, chunk, 8, across)),
        ]

    def begin(moves):
        for need, move in moves:
            if need is None:
                move.start()
            else:
                pl.when(need)(move.start)

    def begin_if(need, moves):
        for on, move in moves:
            if on is None or on is need:
                move.start()

    def finish(moves):
        for need, move in moves:
            if need is None:
                move.wait_send()
            else:
                pl.when(need)(move.wait_send)

    for part in range(HALVES):
        if part:
            prepare(part)
        for chunk in range(part * CHUNKS // HALVES, (part + 1) * CHUNKS // HALVES):
            begin(own_moves(chunk))
    for load in loads[4:]:
        load.start()

    shift = 0.5 / rows - row.astype(jnp.float32) / rows
    half_turn = jnp.zeros((1, 1), jnp.float32) + shift * math.pi
    half_cos = jnp.cos(half_turn)
    half_sin = jnp.sin(half_turn)
    edge_at = lax.broadcasted_iota(jnp.int32, edge.shape[1:], 0)
    edge_lane = lax.broadcasted_iota(jnp.int32, edge.shape[1:], 1)
    edge_angle = edge_at.astype(jnp.float32) * (math.pi / fast_len)
    edge[0] = jnp.where(edge_lane == 0, jnp.cos(edge_angle) * (1.0 / points), 0.0)
    edge[1] = jnp.where(edge_lane == 0, jnp.sin(edge_angle) * (1.0 / points), 0.0)

    def prod_copy(pair, part, origin):
        span = pl.ds(0, 2 * thick + (8 if part == 0 else 0))
        return pltpu.make_async_remote_copy(
            src_ref=send_prod.at[pair, part, span],
            dst_ref=recv_prod.at[pair * subs + origin, part, span],
            send_sem=prod_send.at[pair, part],
            recv_sem=prod_recv.at[pair * subs + origin, part],
            device_id={"sub": 1 - sub},
            device_id_type=MESH,
        )

    def part_chunks(part):
        return range(part * CHUNKS // HALVES, (part + 1) * CHUNKS // HALVES)

    def contract(pair, part):
        chunks = part_chunks(part)
        real, imag = (
            stacked([gathered[slot, pair, chunk, at] for slot in range(rows) for chunk in chunks])
            for at in range(2)
        )
        data = split(jnp.concatenate([real, imag], 1))
        moved = dot3((kern[0], kern[1]), data)
        real, imag = times((moved[:, :side], moved[:, side:]), (post[part, 0], post[part, 1]))
        mine = pair * subs + sub
        if part == 0:
            firsts = tuple(
                stacked([gathered[slot, pair, 0, at, :fast_local, :128] for slot in range(rows)])
                for at in range(2)
            )
            mean_a, mean_b = (
                jnp.sum(jnp.sum(raw, 0, keepdims=True), 1, keepdims=True)
                for raw in times(firsts, (edge[0], edge[1]))
            )
            row_at = lax.broadcasted_iota(jnp.int32, real.shape, 0)
            lane_at = lax.broadcasted_iota(jnp.int32, real.shape, 1)
            constant = (lane_at == 0) & (row_at % thick < fast_local)
            parity = jnp.where(constant, (1 - 2 * (row_at % 2)).astype(jnp.float32), 0.0)
            real = real - parity * (mean_a * half_cos + mean_b * half_sin)
            imag = imag - parity * (mean_b * half_cos - mean_a * half_sin)
            side_at = lax.broadcasted_iota(jnp.int32, (8, side), 1)
            means = jnp.where(side_at < side // 2, mean_a, mean_b)
            send_prod[pair, part, 2 * thick :] = means
            recv_prod[mine, part, 2 * thick :] = means

        for at in range(subs):
            span = slice(at * thick, (at + 1) * thick)

            @pl.when(sub == at)
            def _():
                recv_prod[mine, part, :thick] = real[span]
                recv_prod[mine, part, thick : 2 * thick] = imag[span]

            @pl.when(sub != at)
            def _():
                send_prod[pair, part, :thick] = real[span]
                send_prod[pair, part, thick : 2 * thick] = imag[span]

        prod_copy(pair, part, sub).start()

    def expand(pair):
        for part in range(HALVES):
            prod_copy(pair, part, 1 - sub).wait_recv()
        real, imag = (
            stacked(
                [
                    recv_prod[pair * subs + origin, part, at * thick : (at + 1) * thick]
                    for origin in range(subs)
                    for part in range(HALVES)
                ]
            )
            for at in range(2)
        )
        real, imag = lane_transform(real, imag, -1.0)
        for origin in range(subs):
            span = slice(origin * half, (origin + 1) * half)
            turned = times((real[span], imag[span]), (spin[0], -spin[1]))
            values = short_transform(slices(*turned), -1.0)
            for at in range(2):
                spread[pair * subs + origin, at] = stacked([value[at] for value in values])

    @pl.when(inner)
    def _():
        for chunk in range(CHUNKS):
            arrive(other, col, chunk)
            begin_if(inner, other_moves(chunk))
            arrive(beside, col, chunk)
            begin_if(inner, beside_moves(chunk))
        for chunk in range(CHUNKS):
            arrive(far, col, chunk)
            begin_if(inner, far_moves(chunk))

    @pl.when(outer)
    def _():
        for slot, moves in ((beside, beside_moves), (other, other_moves), (far, far_moves)):
            for chunk in range(CHUNKS):
                arrive(slot, col, chunk)
                begin_if(outer, moves(chunk))

    loads[4].wait()
    loads[5].wait()
    for part in range(HALVES):
        contract(col, part)
    expand(col)
    for part in range(HALVES):
        for slot in (row, beside, other, far):
            for chunk in part_chunks(part):
                arrive(slot, 1 - col, chunk)
        contract(1 - col, part)
    expand(1 - col)

    at_row = lax.broadcasted_iota(jnp.int32, (half, side), 0)
    flip = (1 - 2 * (at_row % 2)).astype(jnp.float32)
    part_cos = flip * half_cos
    part_sin = flip * half_sin

    def value(number):
        block, at = divmod(number, 2)
        lane_from = at * (side // 2)
        mean = recv_prod[block, 0, 2 * thick : 2 * thick + 1, lane_from : lane_from + 1]
        data = spread[block, at]
        return (mean + part_cos * data, part_sin * data)

    wire_a = value(0)
    wire_b = value(1)
    wire_c = value(2)
    gate = times(times(times(value(3), wire_a), wire_b), wire_c)
    gate = plus(gate, times(value(4), wire_a))
    gate = plus(gate, times(value(5), wire_b))
    gate = plus(gate, times(value(6), wire_c))
    gate = plus(gate, value(7))
    values = short_transform(slices(*gate), 1.0)
    real = stacked([value[0] for value in values])
    imag = stacked([value[1] for value in values])
    real, imag = times((real, imag), (spin[0], spin[1]))
    loads[6].wait()
    data = split(jnp.concatenate([real, imag], 0))
    breadth = side * low_len // members
    lane_piece = side // members
    tile_lanes = low_len * lane_piece
    tiles = side // tile_lanes
    lanes = lax.broadcasted_iota(jnp.int32, (2 * fast_local, tile_lanes), 1)
    low_side = (2 * row < rows).astype(jnp.int32)

    def tail_copy(target, slot):
        return pltpu.make_async_remote_copy(
            src_ref=send_tail.at[target],
            dst_ref=recv_tail.at[slot],
            send_sem=tail_send.at[target],
            recv_sem=tail_recv.at[slot],
            device_id=place(target),
            device_id_type=MESH,
        )

    for turn_at in range(tiles):
        tile = lax.rem(low_side + turn_at, tiles)
        real, imag = times(lane_tile(data, tile, 1.0), (twist[tile, 0], twist[tile, 1]))
        pieces = [
            jnp.concatenate(
                [
                    real[at * fast_local : (at + 1) * fast_local],
                    imag[at * fast_local : (at + 1) * fast_local],
                ],
                0,
            )
            for at in range(low_len)
        ]
        bit = low_len // 2
        while bit:
            keep = (lanes // (lane_piece * bit)) % 2 == 0
            for at in range(low_len):
                if at & bit == 0:
                    one, two = pieces[at], pieces[at + bit]
                    pieces[at] = jnp.where(keep, one, pltpu.roll(two, lane_piece * bit, 1))
                    pieces[at + bit] = jnp.where(
                        keep, pltpu.roll(one, tile_lanes - lane_piece * bit, 1), two
                    )
            bit //= 2
        for at in range(low_len):
            send_tail[tile * low_len + at] = pieces[at]
        for at in range(low_len):
            target = tile * low_len + lax.rem(at + low_side * (low_len // 2), low_len)

            @pl.when(target != me)
            def _():
                tail_copy(target, me).start()

    recv_tail[me] = send_tail[me]
    for step in range(1, members):
        source = lax.rem(me + step, members)
        tail_copy(source, source).wait_recv()
    out_ref[...] = recv_tail[...].reshape(members * 2 * fast_local, breadth)

    for step in range(1, members):
        target = lax.rem(me + step, members)
        tail_copy(target, me).wait_send()
    for pair in range(cols):
        for part in range(HALVES):
            prod_copy(pair, part, sub).wait_send()
    for chunk in range(CHUNKS):
        for moves in (
            own_moves,
            beside_moves,
            other_moves,
            far_moves,
        ):
            finish(moves(chunk))


def final_kernel(sizes, flat_ref, final_ref, out_ref):
    side, fast_len, fast_local, rows, groups, blocks = sizes
    low_len = side // fast_len
    lane_piece = side // (rows * groups)
    data = split(jnp.transpose(flat_ref[...]))
    result = dot3(data, (final_ref[0], final_ref[1]))
    for at in range(low_len):
        picked = result[at * lane_piece : (at + 1) * lane_piece]
        rows_at = pl.ds(at, lane_piece, stride=low_len)
        out_ref[0, rows_at] = picked[:, : rows * fast_len]
        out_ref[1, rows_at] = picked[:, rows * fast_len :]


def fused_on_device(sizes, trace):
    side, fast_len, fast_local, rows, groups, (cols, subs) = sizes
    low_len = side // fast_len
    half = low_len * fast_local
    deep = half // CHUNKS
    members = rows * groups
    *tables, final = [jnp.asarray(table) for table in fused_tables(sizes)]
    thick = half // HALVES
    block = jnp.transpose(trace, (0, 2, 1))
    vmem = pltpu.VMEM
    bf16 = jnp.bfloat16
    f32 = jnp.float32
    dma = pltpu.SemaphoreType.DMA
    breadth = side * low_len // members
    flat = pl.pallas_call(
        partial(fused_kernel, sizes),
        out_shape=vmem((members * 2 * fast_local, breadth), f32),
        in_specs=[pl.BlockSpec(memory_space=pltpu.HBM)] * (1 + len(tables)),
        out_specs=pl.BlockSpec(memory_space=vmem),
        scratch_shapes=[
            vmem(block.shape, f32),
            vmem((side // LANES, 2, side, side), bf16),
            vmem((2, half, side), f32),
            vmem((2, half, side), f32),
            vmem((2, subs * thick, rows * thick), bf16),
            vmem((HALVES, 2, subs * thick, side), f32),
            vmem((side // LANES, 2, half, LANES), f32),
            vmem((2, fast_len, 128), f32),
            vmem((rows, cols, CHUNKS, 2, deep, side), f32),
            vmem((cols, HALVES, 2 * thick + 8, side), f32),
            vmem((groups, HALVES, 2 * thick + 8, side), f32),
            vmem((groups, 2, half, side), f32),
            vmem((members, 2 * fast_local, breadth), f32),
            vmem((members, 2 * fast_local, breadth), f32),
            dma((8,)),
            dma((9, CHUNKS)),
            dma((rows, cols, CHUNKS)),
            dma((cols, HALVES)),
            dma((groups, HALVES)),
            dma((members,)),
            dma((members,)),
        ],
        compiler_params=pltpu.CompilerParams(
            collective_id=0, has_side_effects=True, vmem_limit_bytes=VMEM_LIMIT
        ),
    )(*[pltpu.with_memory_space_constraint(table, pltpu.HBM) for table in (block, *tables)])
    return pl.pallas_call(
        partial(final_kernel, sizes),
        out_shape=jax.ShapeDtypeStruct((2, breadth, rows * fast_len), f32),
        in_specs=[pl.BlockSpec(memory_space=vmem)] * 2,
        out_specs=pl.BlockSpec(memory_space=vmem),
        compiler_params=pltpu.CompilerParams(vmem_limit_bytes=VMEM_LIMIT),
    )(flat, final)


def fused_sizes(mesh, trace):
    shape = mesh.shape
    rows = shape["rows"]
    groups = shape["cols"] * shape["sub"]
    slow_len = trace.shape[1] // shape["groups"]
    fast_len = trace.shape[2]
    side = math.isqrt(slow_len * fast_len)
    fast_local = fast_len // rows
    local_cols = trace.shape[0] // groups
    low_len = side // fast_len
    fits = (
        side * side == slow_len * fast_len
        and low_len * fast_len == side
        and rows == 4
        and groups == rows
        and shape["cols"] == 2
        and shape["sub"] == 2
        and local_cols == 2
        and fast_local == 8
        and 2 * low_len * fast_local == 128
        and rows * groups == 2 * low_len
        and side == 2 * LANES
    )
    return (side, fast_len, fast_local, rows, groups, (shape["cols"], shape["sub"])) if fits else None


def solution(mesh):
    placed = (P(("cols", "sub"), "groups", "rows"),)

    def whole(trace):
        sizes = fused_sizes(mesh, trace)
        return jax.shard_map(
            on_device if sizes is None else partial(fused_on_device, sizes),
            mesh=mesh,
            in_specs=placed,
            out_specs=P("groups", ("rows", "cols", "sub"), None),
            check_vma=False,
        )(trace)

    return whole
```

```python
from functools import partial
import math

import jax
import jax.numpy as jnp
import numpy as np
from jax import lax
from jax.experimental import pallas as pl
from jax.experimental.pallas import tpu as pltpu
from jax.sharding import PartitionSpec as P


def dft_table(extent, orient):
    points = jnp.arange(extent, dtype=jnp.int32)
    product = points[:, None] * points[None, :] % extent
    angles = product.astype(jnp.float32) * (orient * 2.0 * math.pi / extent)
    return (jnp.cos(angles), jnp.sin(angles))


def complex_apply(table_real, table_imag, data_real, data_imag):
    matmul = partial(jnp.dot, precision=lax.Precision.HIGHEST, preferred_element_type=jnp.float32)
    out_real = matmul(table_real, data_real) - matmul(table_imag, data_imag)
    out_imag = matmul(table_real, data_imag) + matmul(table_imag, data_real)
    return (out_real, out_imag)


def rotate(data_real, data_imag, angles):
    cosine = jnp.cos(angles)
    sine = jnp.sin(angles)
    return (data_real * cosine - data_imag * sine, data_real * sine + data_imag * cosine)


def turn(index_product, modulus, orient):
    return (index_product % modulus).astype(jnp.float32) * (orient * 2.0 * math.pi / modulus)


def transform_lead(data_real, data_imag, orient):
    extent = data_real.shape[0]
    rest_shape = data_real.shape[1:]
    breadth = data_real.size // extent
    flat_real = data_real.reshape(extent, breadth)
    flat_imag = data_imag.reshape(extent, breadth)
    if extent <= 128:
        table_real, table_imag = dft_table(extent, orient)
        out_real, out_imag = complex_apply(table_real, table_imag, flat_real, flat_imag)
    else:
        outer_len = extent // 128
        first_real, first_imag = transform_lead(
            flat_real.reshape(outer_len, 128 * breadth),
            flat_imag.reshape(outer_len, 128 * breadth),
            orient,
        )
        first_real = first_real.reshape(outer_len, 128, breadth)
        first_imag = first_imag.reshape(outer_len, 128, breadth)
        outer_index = jnp.arange(outer_len, dtype=jnp.int32)[:, None]
        inner_index = jnp.arange(128, dtype=jnp.int32)[None, :]
        angles = turn(outer_index * inner_index, extent, orient)[:, :, None]
        first_real, first_imag = rotate(first_real, first_imag, angles)
        first_real = jnp.transpose(first_real, (1, 0, 2)).reshape(128, outer_len * breadth)
        first_imag = jnp.transpose(first_imag, (1, 0, 2)).reshape(128, outer_len * breadth)
        out_real, out_imag = transform_lead(first_real, first_imag, orient)
    return (out_real.reshape((extent,) + rest_shape), out_imag.reshape((extent,) + rest_shape))


def times(first, second):
    return (
        first[0] * second[0] - first[1] * second[1],
        first[0] * second[1] + first[1] * second[0],
    )


def plus(first, second):
    return (first[0] + second[0], first[1] + second[1])


def on_device(trace):
    local_cols = trace.shape[0]
    slow_len = trace.shape[1]
    fast_local = trace.shape[2]
    row_parts = lax.axis_size("rows")
    group_parts = lax.axis_size(("cols", "sub"))
    row_index = lax.axis_index("rows")
    group_index = lax.axis_index(("cols", "sub"))
    fast_len = fast_local * row_parts
    trace_len = slow_len * fast_len
    ext_len = 4 * trace_len
    ext_slow = 4 * fast_len
    slow_block = slow_len // row_parts
    ext_block = ext_slow // row_parts
    point_block = ext_block // group_parts
    coeff_block = slow_block // group_parts
    real_part = jnp.transpose(trace, (1, 0, 2))
    imag_part = jnp.zeros_like(real_part)
    real_part, imag_part = transform_lead(real_part, imag_part, 1.0)
    lead_index = jnp.arange(slow_len, dtype=jnp.int32)[:, None, None]
    fast_index = (row_index * fast_local + jnp.arange(fast_local, dtype=jnp.int32))[None, None, :]
    real_part, imag_part = rotate(
        real_part, imag_part, turn(lead_index * fast_index, trace_len, 1.0)
    )
    moved = lax.all_to_all(
        jnp.stack([real_part, imag_part]), "rows", split_axis=1, concat_axis=3, tiled=True
    )
    moved = jnp.transpose(moved, (0, 3, 2, 1))
    real_part, imag_part = transform_lead(moved[0], moved[1], 1.0)
    slow_index = (row_index * slow_block + jnp.arange(slow_block, dtype=jnp.int32))[None, None, :]
    coeff_index = jnp.arange(fast_len, dtype=jnp.int32)[:, None, None] * slow_len + slow_index
    shift_angle = coeff_index.astype(jnp.float32) * (math.pi / (4.0 * trace_len))
    real_part, imag_part = rotate(real_part / trace_len, imag_part / trace_len, shift_angle)
    padding = jnp.zeros((ext_slow - fast_len, local_cols, slow_index.shape[2]), jnp.float32)
    real_part = jnp.concatenate([real_part, padding], 0)
    imag_part = jnp.concatenate([imag_part, padding], 0)
    real_part, imag_part = transform_lead(real_part, imag_part, -1.0)
    ext_index = jnp.arange(ext_slow, dtype=jnp.int32)[:, None, None]
    real_part, imag_part = rotate(real_part, imag_part, turn(ext_index * slow_index, ext_len, -1.0))
    stacked = jnp.stack([real_part, imag_part])
    moved = lax.all_to_all(stacked, "rows", split_axis=1, concat_axis=3, tiled=True)
    moved = jnp.transpose(moved, (0, 3, 2, 1))
    real_part, imag_part = transform_lead(moved[0], moved[1], -1.0)
    joined = lax.all_to_all(
        jnp.stack([real_part, imag_part]), ("cols", "sub"), split_axis=3, concat_axis=2, tiled=True
    )
    real_part = joined[0]
    imag_part = joined[1]

    def column(number):
        return (real_part[:, number], imag_part[:, number])

    wire_a = column(0)
    wire_b = column(1)
    wire_c = column(2)
    gate = times(times(times(column(3), wire_a), wire_b), wire_c)
    gate = plus(gate, times(column(4), wire_a))
    gate = plus(gate, times(column(5), wire_b))
    gate = plus(gate, times(column(6), wire_c))
    gate = plus(gate, column(7))
    point_index = (
        row_index * ext_block + group_index * point_block + jnp.arange(point_block, dtype=jnp.int32)
    )
    quarter = (point_index % 4).astype(jnp.float32)
    vanish_angle = math.pi / 4.0 - math.pi / 2.0 * quarter
    vanish_real = (jnp.cos(vanish_angle) - 1.0)[None, :]
    vanish_imag = jnp.sin(vanish_angle)[None, :]
    magnitude = vanish_real * vanish_real + vanish_imag * vanish_imag
    ratio_real = (gate[0] * vanish_real + gate[1] * vanish_imag) / magnitude
    ratio_imag = (gate[1] * vanish_real - gate[0] * vanish_imag) / magnitude
    real_part, imag_part = transform_lead(ratio_real, ratio_imag, 1.0)
    freq_index = jnp.arange(slow_len, dtype=jnp.int32)[:, None]
    real_part, imag_part = rotate(
        real_part, imag_part, turn(freq_index * point_index[None, :], ext_len, 1.0)
    )
    moved = lax.all_to_all(
        lax.all_to_all(
            jnp.stack([real_part, imag_part]), "rows", split_axis=1, concat_axis=2, tiled=True
        ),
        ("cols", "sub"),
        split_axis=1,
        concat_axis=2,
        tiled=True,
    )
    moved = moved.reshape(2, coeff_block, group_parts, row_parts, point_block)
    moved = jnp.transpose(moved, (0, 3, 2, 4, 1)).reshape(2, ext_slow, coeff_block)
    real_part, imag_part = transform_lead(moved[0], moved[1], 1.0)
    low_index = (
        row_index * slow_block
        + group_index * coeff_block
        + jnp.arange(coeff_block, dtype=jnp.int32)
    )[None, :]
    final_index = jnp.arange(ext_slow, dtype=jnp.int32)[:, None] * slow_len + low_index
    final_angle = final_index.astype(jnp.float32) * (-math.pi / (4.0 * trace_len))
    real_part, imag_part = rotate(real_part, imag_part, final_angle)
    result = jnp.stack([real_part, imag_part]) * (1.0 / math.sqrt(ext_len))
    return jnp.transpose(result, (0, 2, 1))


MESH = pl.DeviceIdType.MESH
CHUNKS = 4
HALVES = 2
LANES = 128
VMEM_LIMIT = 12 * 2**20


def halves(table):
    high = table.astype(jnp.bfloat16)
    low = (table - high.astype(np.float64)).astype(jnp.bfloat16)
    return high, low


def fused_tables(sizes):
    side, fast_len, fast_local, rows, groups, blocks = sizes
    points = side * side
    ext = rows * points
    low_len = side // fast_len
    slow_len = side * low_len
    half = low_len * fast_local
    lows = low_len // HALVES
    cols, subs = blocks
    index = np.arange(side)
    angles = 2.0 * np.pi * (index[:, None] * index[None, :] % side) / side
    dft = np.stack(
        [
            halves(np.concatenate([np.cos(part), np.sin(part)], 1))
            for part in np.split(angles, side // LANES, 1)
        ]
    )
    low_at, fast_at = (
        grid.reshape(-1)
        for grid in np.meshgrid(np.arange(low_len), np.arange(fast_local), indexing="ij")
    )
    freq = low_at[:, None] + low_len * index[None, :]
    centred = freq - slow_len // 2
    members = np.arange(rows)
    inner = fast_local * members[:, None] + fast_at
    theta = 2.0 * np.pi * inner[:, :, None] * centred / points
    base = np.stack([np.cos(theta), np.sin(theta)], 1).astype(np.float32)
    shifts = 0.5 / rows - np.arange(rows) / rows
    angle = centred * (2.0 * np.pi / points) * shifts[:, None, None, None] - theta
    post = np.stack([np.cos(angle), np.sin(angle)], 1).astype(np.float32)
    post = post.reshape(rows, 2, cols, subs, HALVES, lows * fast_local, side)
    post = np.transpose(post, (0, 2, 4, 1, 3, 5, 6)).reshape(rows * cols, HALVES, 2, -1, side)
    slot_at, low_in, fast_in = (
        grid.reshape(-1)
        for grid in np.meshgrid(
            np.arange(rows), np.arange(lows), np.arange(fast_local), indexing="ij"
        )
    )
    inner = fast_local * slot_at + fast_in
    same = low_in[:, None] == low_in[None, :]
    sign = 1.0 - 2.0 * (inner[:, None] % 2)
    kernels = []
    for shift in shifts:
        gap = inner[None, :] - inner[:, None] + shift
        weight = sign / points * np.sin(np.pi * shift) / np.sin(np.pi * gap / fast_len)
        weight = np.where(same, weight, 0.0)
        for part in np.split(weight, cols):
            kernels.append(np.stack(halves(part)))
    kernels = np.stack(kernels)
    spin = 2.0 * np.pi * low_at[:, None] * index[None, :] / slow_len
    spin = np.stack([np.cos(spin), np.sin(spin)]).astype(np.float32)
    row_at, group_at = np.divmod(np.arange(rows * groups), groups)
    digit = rows * (fast_local * group_at[:, None] + fast_at) + row_at[:, None]
    angle = freq * (2 * digit[:, :, None] - 1) % (2 * ext) * (np.pi / ext)
    twist = np.stack([np.cos(angle), np.sin(angle)], 1).astype(np.float32)
    twist = np.stack(np.split(twist, side // LANES, 3), 1)
    source_row, source_group, fast_at = np.meshgrid(
        np.arange(rows), np.arange(groups), np.arange(fast_local), indexing="ij"
    )
    low_digit = rows * (fast_local * source_group + fast_at) + source_row
    vanish = np.exp(1j * (np.pi / rows - 2.0 * np.pi / rows * source_row)) - 1.0
    finals = np.arange(rows * fast_len)
    turns = np.exp(
        2j * np.pi * low_digit[..., None] * finals / (rows * fast_len)
        - 1j * np.pi * slow_len * finals / ext
    ) / (vanish[..., None] * math.sqrt(ext))
    real_rows = np.concatenate([turns.real, turns.imag], -1)
    imag_rows = np.concatenate([-turns.imag, turns.real], -1)
    final = np.stack([real_rows, imag_rows], 2).reshape(-1, 2 * rows * fast_len)
    final = np.stack(halves(final))
    return dft, spin, base, kernels, post, twist, final


def split(value):
    high = value.astype(jnp.bfloat16)
    return high, (value - high.astype(jnp.float32)).astype(jnp.bfloat16)


def dot3(left, right):
    mul = partial(jnp.dot, preferred_element_type=jnp.float32)
    count = left[0].shape[0]
    both = mul(jnp.concatenate(left, 0), right[0])
    return both[:count] + (both[count:] + mul(left[0], right[1]))


def short_transform(values, orient):
    count = len(values)
    if count == 1:
        return values
    even = short_transform(values[0::2], orient)
    odd = short_transform(values[1::2], orient)
    first, second = [], []
    for at in range(count // 2):
        cosine = math.cos(2.0 * math.pi * at / count)
        sine = orient * math.sin(2.0 * math.pi * at / count)
        real, imag = odd[at]
        if at == 0:
            spun = (real, imag)
        elif 4 * at == count:
            spun = (-orient * imag, orient * real)
        else:
            spun = (real * cosine - imag * sine, real * sine + imag * cosine)
        first.append(plus(even[at], spun))
        second.append((even[at][0] - spun[0], even[at][1] - spun[1]))
    return first + second


def fused_kernel(
    sizes,
    x_hbm,
    dft_hbm,
    spin_hbm,
    base_hbm,
    kern_hbm,
    post_hbm,
    twist_hbm,
    out_ref,
    x_ref,
    dft,
    spin,
    base,
    kern,
    post,
    twist,
    edge,
    gathered,
    send_prod,
    recv_prod,
    spread,
    send_tail,
    recv_tail,
    table_sem,
    gather_send,
    gather_recv,
    prod_send,
    prod_recv,
    tail_send,
    tail_recv,
):
    side, fast_len, fast_local, rows, groups, (cols, subs) = sizes
    points = side * side
    low_len = side // fast_len
    half = low_len * fast_local
    lows = low_len // CHUNKS
    deep = lows * fast_local
    thick = CHUNKS // HALVES * deep
    members = rows * groups
    row = lax.axis_index("rows")
    col = lax.axis_index("cols")
    sub = lax.axis_index("sub")
    group = col * subs + sub
    me = row * groups + group

    def place(member):
        inside = lax.rem(member, groups)
        return {
            "rows": lax.div(member, groups),
            "cols": lax.div(inside, subs),
            "sub": lax.rem(inside, subs),
        }

    first_load = pltpu.make_async_copy(x_hbm, x_ref, table_sem.at[0])
    first_load.start()
    barrier = pltpu.get_barrier_semaphore()

    @pl.when(row > 0)
    def _():
        pl.semaphore_signal(barrier, inc=1, device_id={"rows": row - 1}, device_id_type=MESH)

    @pl.when(row < rows - 1)
    def _():
        pl.semaphore_signal(barrier, inc=1, device_id={"rows": row + 1}, device_id_type=MESH)

    for near in ({"cols": 1 - col}, {"sub": 1 - sub}):
        pl.semaphore_signal(barrier, inc=1, device_id=near, device_id_type=MESH)

    loads = [
        first_load,
        pltpu.make_async_copy(spin_hbm, spin, table_sem.at[1]),
        pltpu.make_async_copy(dft_hbm, dft, table_sem.at[2]),
        pltpu.make_async_copy(base_hbm.at[row], base, table_sem.at[3]),
        pltpu.make_async_copy(kern_hbm.at[row * cols + col], kern, table_sem.at[4]),
        pltpu.make_async_copy(post_hbm.at[row * cols + col], post, table_sem.at[5]),
        pltpu.make_async_copy(twist_hbm.at[me], twist, table_sem.at[6]),
    ]
    for load in loads[1:4]:
        load.start()

    def stacked(values):
        return jnp.concatenate([value for value in values], 0)

    def slices(real, imag):
        return [
            (real[at * fast_local : (at + 1) * fast_local], imag[at * fast_local : (at + 1) * fast_local])
            for at in range(low_len)
        ]

    def lane_tile(data, tile, orient):
        count = data[0].shape[0] // 2
        out = dot3(data, (dft[tile, 0], dft[tile, 1]))
        cosines, sines = out[:, :LANES], out[:, LANES:]
        return (
            cosines[:count] - orient * sines[count:],
            cosines[count:] + orient * sines[:count],
        )

    def lane_transform(real, imag, orient):
        data = split(jnp.concatenate([real, imag], 0))
        tiles = [lane_tile(data, tile, orient) for tile in range(side // LANES)]
        return tuple(jnp.concatenate([tile[at] for tile in tiles], 1) for at in range(2))

    loads[0].wait()
    values = [
        (
            x_ref[0, :, at * side : (at + 1) * side],
            x_ref[1, :, at * side : (at + 1) * side],
        )
        for at in range(low_len)
    ]
    values = short_transform(values, 1.0)
    real = stacked([value[0] for value in values])
    imag = stacked([value[1] for value in values])
    loads[1].wait()
    real, imag = times((real, imag), (spin[0], spin[1]))
    loads[2].wait()
    real, imag = lane_transform(real, imag, 1.0)
    loads[3].wait()
    real, imag = times((real, imag), (base[0], base[1]))
    for chunk in range(CHUNKS):
        gathered[row, col, chunk, 0] = real[chunk * deep : (chunk + 1) * deep]
        gathered[row, col, chunk, 1] = imag[chunk * deep : (chunk + 1) * deep]

    pl.semaphore_wait(
        barrier,
        2 + (row > 0).astype(jnp.int32) + (row < rows - 1).astype(jnp.int32),
    )

    inner = (row > 0) & (row < rows - 1)
    outer = jnp.logical_not(inner)
    end = jnp.where(2 * row < rows, 0, rows - 1)
    far = rows - 1 - end
    beside = jnp.where(row == 0, 1, jnp.where(row == rows - 1, rows - 2, rows - 1 - row))
    other = jnp.where(inner, end, jnp.where(end == 0, rows - 2, 1))
    across = {"cols": 1 - col}

    def hop(slot, pair, chunk, way, target):
        return pltpu.make_async_remote_copy(
            src_ref=gathered.at[slot, pair, chunk],
            dst_ref=gathered.at[slot, pair, chunk],
            send_sem=gather_send.at[way, chunk],
            recv_sem=gather_recv.at[slot, pair, chunk],
            device_id=target,
            device_id_type=MESH,
        )

    def arrive(slot, pair, chunk):
        hop(slot, pair, chunk, 0, across).wait_recv()

    def own_moves(chunk):
        return [
            (None, hop(row, col, chunk, 0, {"rows": beside})),
            (inner, hop(row, col, chunk, 1, {"rows": end})),
            (None, hop(row, col, chunk, 2, across)),
        ]

    def beside_moves(chunk):
        return [
            (inner, hop(beside, col, chunk, 3, {"rows": end})),
            (None, hop(beside, col, chunk, 4, across)),
        ]

    def other_moves(chunk):
        return [
            (inner, hop(other, col, chunk, 5, {"rows": beside})),
            (None, hop(other, col, chunk, 6, across)),
        ]

    def far_moves(chunk):
        return [
            (inner, hop(far, col, chunk, 7, {"rows": end})),
            (None, hop(far, col, chunk, 8, across)),
        ]

    def begin(moves):
        for need, move in moves:
            if need is None:
                move.start()
            else:
                pl.when(need)(move.start)

    def begin_if(need, moves):
        for on, move in moves:
            if on is None or on is need:
                move.start()

    def finish(moves):
        for need, move in moves:
            if need is None:
                move.wait_send()
            else:
                pl.when(need)(move.wait_send)

    for chunk in range(CHUNKS):
        begin(own_moves(chunk))
    for load in loads[4:]:
        load.start()

    shift = 0.5 / rows - row.astype(jnp.float32) / rows
    half_turn = jnp.zeros((1, 1), jnp.float32) + shift * math.pi
    half_cos = jnp.cos(half_turn)
    half_sin = jnp.sin(half_turn)
    edge_at = lax.broadcasted_iota(jnp.int32, edge.shape[1:], 0)
    edge_lane = lax.broadcasted_iota(jnp.int32, edge.shape[1:], 1)
    edge_angle = edge_at.astype(jnp.float32) * (math.pi / fast_len)
    edge[0] = jnp.where(edge_lane == 0, jnp.cos(edge_angle) * (1.0 / points), 0.0)
    edge[1] = jnp.where(edge_lane == 0, jnp.sin(edge_angle) * (1.0 / points), 0.0)

    def prod_copy(pair, part, origin):
        span = pl.ds(0, 2 * thick + (8 if part == 0 else 0))
        return pltpu.make_async_remote_copy(
            src_ref=send_prod.at[pair, part, span],
            dst_ref=recv_prod.at[pair * subs + origin, part, span],
            send_sem=prod_send.at[pair, part],
            recv_sem=prod_recv.at[pair * subs + origin, part],
            device_id={"sub": 1 - sub},
            device_id_type=MESH,
        )

    def part_chunks(part):
        return range(part * CHUNKS // HALVES, (part + 1) * CHUNKS // HALVES)

    def contract(pair, part):
        chunks = part_chunks(part)
        real, imag = (
            stacked([gathered[slot, pair, chunk, at] for slot in range(rows) for chunk in chunks])
            for at in range(2)
        )
        data = split(jnp.concatenate([real, imag], 1))
        moved = dot3((kern[0], kern[1]), data)
        real, imag = times((moved[:, :side], moved[:, side:]), (post[part, 0], post[part, 1]))
        mine = pair * subs + sub
        if part == 0:
            firsts = tuple(
                stacked([gathered[slot, pair, 0, at, :fast_local, :128] for slot in range(rows)])
                for at in range(2)
            )
            mean_a, mean_b = (
                jnp.sum(jnp.sum(raw, 0, keepdims=True), 1, keepdims=True)
                for raw in times(firsts, (edge[0], edge[1]))
            )
            row_at = lax.broadcasted_iota(jnp.int32, real.shape, 0)
            lane_at = lax.broadcasted_iota(jnp.int32, real.shape, 1)
            constant = (lane_at == 0) & (row_at % thick < fast_local)
            parity = jnp.where(constant, (1 - 2 * (row_at % 2)).astype(jnp.float32), 0.0)
            real = real - parity * (mean_a * half_cos + mean_b * half_sin)
            imag = imag - parity * (mean_b * half_cos - mean_a * half_sin)
            side_at = lax.broadcasted_iota(jnp.int32, (8, side), 1)
            means = jnp.where(side_at < side // 2, mean_a, mean_b)
            send_prod[pair, part, 2 * thick :] = means
            recv_prod[mine, part, 2 * thick :] = means

        for at in range(subs):
            span = slice(at * thick, (at + 1) * thick)

            @pl.when(sub == at)
            def _():
                recv_prod[mine, part, :thick] = real[span]
                recv_prod[mine, part, thick : 2 * thick] = imag[span]

            @pl.when(sub != at)
            def _():
                send_prod[pair, part, :thick] = real[span]
                send_prod[pair, part, thick : 2 * thick] = imag[span]

        prod_copy(pair, part, sub).start()

    def expand(pair):
        for part in range(HALVES):
            prod_copy(pair, part, 1 - sub).wait_recv()
        real, imag = (
            stacked(
                [
                    recv_prod[pair * subs + origin, part, at * thick : (at + 1) * thick]
                    for origin in range(subs)
                    for part in range(HALVES)
                ]
            )
            for at in range(2)
        )
        real, imag = lane_transform(real, imag, -1.0)
        for origin in range(subs):
            span = slice(origin * half, (origin + 1) * half)
            turned = times((real[span], imag[span]), (spin[0], -spin[1]))
            values = short_transform(slices(*turned), -1.0)
            for at in range(2):
                spread[pair * subs + origin, at] = stacked([value[at] for value in values])

    @pl.when(inner)
    def _():
        for chunk in range(CHUNKS):
            arrive(beside, col, chunk)
            begin_if(inner, beside_moves(chunk))
            arrive(other, col, chunk)
            begin_if(inner, other_moves(chunk))
        for chunk in range(CHUNKS):
            arrive(far, col, chunk)
            begin_if(inner, far_moves(chunk))

    @pl.when(outer)
    def _():
        for slot, moves in ((beside, beside_moves), (other, other_moves), (far, far_moves)):
            for chunk in range(CHUNKS):
                arrive(slot, col, chunk)
                begin_if(outer, moves(chunk))

    loads[4].wait()
    loads[5].wait()
    for part in range(HALVES):
        contract(col, part)
    expand(col)
    for part in range(HALVES):
        for slot in (row, beside, other, far):
            for chunk in part_chunks(part):
                arrive(slot, 1 - col, chunk)
        contract(1 - col, part)
    expand(1 - col)

    at_row = lax.broadcasted_iota(jnp.int32, (half, side), 0)
    flip = (1 - 2 * (at_row % 2)).astype(jnp.float32)
    part_cos = flip * half_cos
    part_sin = flip * half_sin

    def value(number):
        block, at = divmod(number, 2)
        lane_from = at * (side // 2)
        mean = recv_prod[block, 0, 2 * thick : 2 * thick + 1, lane_from : lane_from + 1]
        data = spread[block, at]
        return (mean + part_cos * data, part_sin * data)

    wire_a = value(0)
    wire_b = value(1)
    wire_c = value(2)
    gate = times(times(times(value(3), wire_a), wire_b), wire_c)
    gate = plus(gate, times(value(4), wire_a))
    gate = plus(gate, times(value(5), wire_b))
    gate = plus(gate, times(value(6), wire_c))
    gate = plus(gate, value(7))
    values = short_transform(slices(*gate), 1.0)
    real = stacked([value[0] for value in values])
    imag = stacked([value[1] for value in values])
    real, imag = times((real, imag), (spin[0], spin[1]))
    loads[6].wait()
    data = split(jnp.concatenate([real, imag], 0))
    breadth = side * low_len // members
    lane_piece = side // members
    tile_lanes = low_len * lane_piece
    tiles = side // tile_lanes
    lanes = lax.broadcasted_iota(jnp.int32, (2 * fast_local, tile_lanes), 1)
    low_side = (2 * row < rows).astype(jnp.int32)

    def tail_copy(target, slot):
        return pltpu.make_async_remote_copy(
            src_ref=send_tail.at[target],
            dst_ref=recv_tail.at[slot],
            send_sem=tail_send.at[target],
            recv_sem=tail_recv.at[slot],
            device_id=place(target),
            device_id_type=MESH,
        )

    for turn_at in range(tiles):
        tile = lax.rem(low_side + turn_at, tiles)
        real, imag = times(lane_tile(data, tile, 1.0), (twist[tile, 0], twist[tile, 1]))
        pieces = [
            jnp.concatenate(
                [
                    real[at * fast_local : (at + 1) * fast_local],
                    imag[at * fast_local : (at + 1) * fast_local],
                ],
                0,
            )
            for at in range(low_len)
        ]
        bit = low_len // 2
        while bit:
            keep = (lanes // (lane_piece * bit)) % 2 == 0
            for at in range(low_len):
                if at & bit == 0:
                    one, two = pieces[at], pieces[at + bit]
                    pieces[at] = jnp.where(keep, one, pltpu.roll(two, lane_piece * bit, 1))
                    pieces[at + bit] = jnp.where(
                        keep, pltpu.roll(one, tile_lanes - lane_piece * bit, 1), two
                    )
            bit //= 2
        for at in range(low_len):
            send_tail[tile * low_len + at] = pieces[at]
        for at in range(low_len):
            target = tile * low_len + lax.rem(at + low_side * (low_len // 2), low_len)

            @pl.when(target != me)
            def _():
                tail_copy(target, me).start()

    recv_tail[me] = send_tail[me]
    for step in range(1, members):
        source = lax.rem(me + step, members)
        tail_copy(source, source).wait_recv()
    out_ref[...] = recv_tail[...].reshape(members * 2 * fast_local, breadth)

    for step in range(1, members):
        target = lax.rem(me + step, members)
        tail_copy(target, me).wait_send()
    for pair in range(cols):
        for part in range(HALVES):
            prod_copy(pair, part, sub).wait_send()
    for chunk in range(CHUNKS):
        for moves in (
            own_moves,
            beside_moves,
            other_moves,
            far_moves,
        ):
            finish(moves(chunk))


def final_kernel(sizes, flat_ref, final_ref, out_ref):
    side, fast_len, fast_local, rows, groups, blocks = sizes
    low_len = side // fast_len
    lane_piece = side // (rows * groups)
    data = split(jnp.transpose(flat_ref[...]))
    result = dot3(data, (final_ref[0], final_ref[1]))
    for at in range(low_len):
        picked = result[at * lane_piece : (at + 1) * lane_piece]
        rows_at = pl.ds(at, lane_piece, stride=low_len)
        out_ref[0, rows_at] = picked[:, : rows * fast_len]
        out_ref[1, rows_at] = picked[:, rows * fast_len :]


def fused_on_device(sizes, trace):
    side, fast_len, fast_local, rows, groups, (cols, subs) = sizes
    low_len = side // fast_len
    half = low_len * fast_local
    deep = half // CHUNKS
    members = rows * groups
    *tables, final = [jnp.asarray(table) for table in fused_tables(sizes)]
    thick = half // HALVES
    block = jnp.transpose(trace, (0, 2, 1))
    vmem = pltpu.VMEM
    bf16 = jnp.bfloat16
    f32 = jnp.float32
    dma = pltpu.SemaphoreType.DMA
    breadth = side * low_len // members
    flat = pl.pallas_call(
        partial(fused_kernel, sizes),
        out_shape=vmem((members * 2 * fast_local, breadth), f32),
        in_specs=[pl.BlockSpec(memory_space=pltpu.HBM)] * (1 + len(tables)),
        out_specs=pl.BlockSpec(memory_space=vmem),
        scratch_shapes=[
            vmem(block.shape, f32),
            vmem((side // LANES, 2, side, side), bf16),
            vmem((2, half, side), f32),
            vmem((2, half, side), f32),
            vmem((2, subs * thick, rows * thick), bf16),
            vmem((HALVES, 2, subs * thick, side), f32),
            vmem((side // LANES, 2, half, LANES), f32),
            vmem((2, fast_len, 128), f32),
            vmem((rows, cols, CHUNKS, 2, deep, side), f32),
            vmem((cols, HALVES, 2 * thick + 8, side), f32),
            vmem((groups, HALVES, 2 * thick + 8, side), f32),
            vmem((groups, 2, half, side), f32),
            vmem((members, 2 * fast_local, breadth), f32),
            vmem((members, 2 * fast_local, breadth), f32),
            dma((8,)),
            dma((9, CHUNKS)),
            dma((rows, cols, CHUNKS)),
            dma((cols, HALVES)),
            dma((groups, HALVES)),
            dma((members,)),
            dma((members,)),
        ],
        compiler_params=pltpu.CompilerParams(
            collective_id=0, has_side_effects=True, vmem_limit_bytes=VMEM_LIMIT
        ),
    )(*[pltpu.with_memory_space_constraint(table, pltpu.HBM) for table in (block, *tables)])
    return pl.pallas_call(
        partial(final_kernel, sizes),
        out_shape=jax.ShapeDtypeStruct((2, breadth, rows * fast_len), f32),
        in_specs=[pl.BlockSpec(memory_space=vmem)] * 2,
        out_specs=pl.BlockSpec(memory_space=vmem),
        compiler_params=pltpu.CompilerParams(vmem_limit_bytes=VMEM_LIMIT),
    )(flat, final)


def fused_sizes(mesh, trace):
    shape = mesh.shape
    rows = shape["rows"]
    groups = shape["cols"] * shape["sub"]
    slow_len = trace.shape[1] // shape["groups"]
    fast_len = trace.shape[2]
    side = math.isqrt(slow_len * fast_len)
    fast_local = fast_len // rows
    local_cols = trace.shape[0] // groups
    low_len = side // fast_len
    fits = (
        side * side == slow_len * fast_len
        and low_len * fast_len == side
        and rows == 4
        and groups == rows
        and shape["cols"] == 2
        and shape["sub"] == 2
        and local_cols == 2
        and fast_local == 8
        and 2 * low_len * fast_local == 128
        and rows * groups == 2 * low_len
        and side == 2 * LANES
    )
    return (side, fast_len, fast_local, rows, groups, (shape["cols"], shape["sub"])) if fits else None


def solution(mesh):
    placed = (P(("cols", "sub"), "groups", "rows"),)

    def whole(trace):
        sizes = fused_sizes(mesh, trace)
        return jax.shard_map(
            on_device if sizes is None else partial(fused_on_device, sizes),
            mesh=mesh,
            in_specs=placed,
            out_specs=P("groups", ("rows", "cols", "sub"), None),
            check_vma=False,
        )(trace)

    return whole
```

```python
from functools import partial
import math

import jax
import jax.numpy as jnp
import numpy as np
from jax import lax
from jax.experimental import pallas as pl
from jax.experimental.pallas import tpu as pltpu
from jax.sharding import PartitionSpec as P


def dft_table(extent, orient):
    points = jnp.arange(extent, dtype=jnp.int32)
    product = points[:, None] * points[None, :] % extent
    angles = product.astype(jnp.float32) * (orient * 2.0 * math.pi / extent)
    return (jnp.cos(angles), jnp.sin(angles))


def complex_apply(table_real, table_imag, data_real, data_imag):
    matmul = partial(jnp.dot, precision=lax.Precision.HIGHEST, preferred_element_type=jnp.float32)
    out_real = matmul(table_real, data_real) - matmul(table_imag, data_imag)
    out_imag = matmul(table_real, data_imag) + matmul(table_imag, data_real)
    return (out_real, out_imag)


def rotate(data_real, data_imag, angles):
    cosine = jnp.cos(angles)
    sine = jnp.sin(angles)
    return (data_real * cosine - data_imag * sine, data_real * sine + data_imag * cosine)


def turn(index_product, modulus, orient):
    return (index_product % modulus).astype(jnp.float32) * (orient * 2.0 * math.pi / modulus)


def transform_lead(data_real, data_imag, orient):
    extent = data_real.shape[0]
    rest_shape = data_real.shape[1:]
    breadth = data_real.size // extent
    flat_real = data_real.reshape(extent, breadth)
    flat_imag = data_imag.reshape(extent, breadth)
    if extent <= 128:
        table_real, table_imag = dft_table(extent, orient)
        out_real, out_imag = complex_apply(table_real, table_imag, flat_real, flat_imag)
    else:
        outer_len = extent // 128
        first_real, first_imag = transform_lead(
            flat_real.reshape(outer_len, 128 * breadth),
            flat_imag.reshape(outer_len, 128 * breadth),
            orient,
        )
        first_real = first_real.reshape(outer_len, 128, breadth)
        first_imag = first_imag.reshape(outer_len, 128, breadth)
        outer_index = jnp.arange(outer_len, dtype=jnp.int32)[:, None]
        inner_index = jnp.arange(128, dtype=jnp.int32)[None, :]
        angles = turn(outer_index * inner_index, extent, orient)[:, :, None]
        first_real, first_imag = rotate(first_real, first_imag, angles)
        first_real = jnp.transpose(first_real, (1, 0, 2)).reshape(128, outer_len * breadth)
        first_imag = jnp.transpose(first_imag, (1, 0, 2)).reshape(128, outer_len * breadth)
        out_real, out_imag = transform_lead(first_real, first_imag, orient)
    return (out_real.reshape((extent,) + rest_shape), out_imag.reshape((extent,) + rest_shape))


def times(first, second):
    return (
        first[0] * second[0] - first[1] * second[1],
        first[0] * second[1] + first[1] * second[0],
    )


def plus(first, second):
    return (first[0] + second[0], first[1] + second[1])


def on_device(trace):
    local_cols = trace.shape[0]
    slow_len = trace.shape[1]
    fast_local = trace.shape[2]
    row_parts = lax.axis_size("rows")
    group_parts = lax.axis_size(("cols", "sub"))
    row_index = lax.axis_index("rows")
    group_index = lax.axis_index(("cols", "sub"))
    fast_len = fast_local * row_parts
    trace_len = slow_len * fast_len
    ext_len = 4 * trace_len
    ext_slow = 4 * fast_len
    slow_block = slow_len // row_parts
    ext_block = ext_slow // row_parts
    point_block = ext_block // group_parts
    coeff_block = slow_block // group_parts
    real_part = jnp.transpose(trace, (1, 0, 2))
    imag_part = jnp.zeros_like(real_part)
    real_part, imag_part = transform_lead(real_part, imag_part, 1.0)
    lead_index = jnp.arange(slow_len, dtype=jnp.int32)[:, None, None]
    fast_index = (row_index * fast_local + jnp.arange(fast_local, dtype=jnp.int32))[None, None, :]
    real_part, imag_part = rotate(
        real_part, imag_part, turn(lead_index * fast_index, trace_len, 1.0)
    )
    moved = lax.all_to_all(
        jnp.stack([real_part, imag_part]), "rows", split_axis=1, concat_axis=3, tiled=True
    )
    moved = jnp.transpose(moved, (0, 3, 2, 1))
    real_part, imag_part = transform_lead(moved[0], moved[1], 1.0)
    slow_index = (row_index * slow_block + jnp.arange(slow_block, dtype=jnp.int32))[None, None, :]
    coeff_index = jnp.arange(fast_len, dtype=jnp.int32)[:, None, None] * slow_len + slow_index
    shift_angle = coeff_index.astype(jnp.float32) * (math.pi / (4.0 * trace_len))
    real_part, imag_part = rotate(real_part / trace_len, imag_part / trace_len, shift_angle)
    padding = jnp.zeros((ext_slow - fast_len, local_cols, slow_index.shape[2]), jnp.float32)
    real_part = jnp.concatenate([real_part, padding], 0)
    imag_part = jnp.concatenate([imag_part, padding], 0)
    real_part, imag_part = transform_lead(real_part, imag_part, -1.0)
    ext_index = jnp.arange(ext_slow, dtype=jnp.int32)[:, None, None]
    real_part, imag_part = rotate(real_part, imag_part, turn(ext_index * slow_index, ext_len, -1.0))
    stacked = jnp.stack([real_part, imag_part])
    moved = lax.all_to_all(stacked, "rows", split_axis=1, concat_axis=3, tiled=True)
    moved = jnp.transpose(moved, (0, 3, 2, 1))
    real_part, imag_part = transform_lead(moved[0], moved[1], -1.0)
    joined = lax.all_to_all(
        jnp.stack([real_part, imag_part]), ("cols", "sub"), split_axis=3, concat_axis=2, tiled=True
    )
    real_part = joined[0]
    imag_part = joined[1]

    def column(number):
        return (real_part[:, number], imag_part[:, number])

    wire_a = column(0)
    wire_b = column(1)
    wire_c = column(2)
    gate = times(times(times(column(3), wire_a), wire_b), wire_c)
    gate = plus(gate, times(column(4), wire_a))
    gate = plus(gate, times(column(5), wire_b))
    gate = plus(gate, times(column(6), wire_c))
    gate = plus(gate, column(7))
    point_index = (
        row_index * ext_block + group_index * point_block + jnp.arange(point_block, dtype=jnp.int32)
    )
    quarter = (point_index % 4).astype(jnp.float32)
    vanish_angle = math.pi / 4.0 - math.pi / 2.0 * quarter
    vanish_real = (jnp.cos(vanish_angle) - 1.0)[None, :]
    vanish_imag = jnp.sin(vanish_angle)[None, :]
    magnitude = vanish_real * vanish_real + vanish_imag * vanish_imag
    ratio_real = (gate[0] * vanish_real + gate[1] * vanish_imag) / magnitude
    ratio_imag = (gate[1] * vanish_real - gate[0] * vanish_imag) / magnitude
    real_part, imag_part = transform_lead(ratio_real, ratio_imag, 1.0)
    freq_index = jnp.arange(slow_len, dtype=jnp.int32)[:, None]
    real_part, imag_part = rotate(
        real_part, imag_part, turn(freq_index * point_index[None, :], ext_len, 1.0)
    )
    moved = lax.all_to_all(
        lax.all_to_all(
            jnp.stack([real_part, imag_part]), "rows", split_axis=1, concat_axis=2, tiled=True
        ),
        ("cols", "sub"),
        split_axis=1,
        concat_axis=2,
        tiled=True,
    )
    moved = moved.reshape(2, coeff_block, group_parts, row_parts, point_block)
    moved = jnp.transpose(moved, (0, 3, 2, 4, 1)).reshape(2, ext_slow, coeff_block)
    real_part, imag_part = transform_lead(moved[0], moved[1], 1.0)
    low_index = (
        row_index * slow_block
        + group_index * coeff_block
        + jnp.arange(coeff_block, dtype=jnp.int32)
    )[None, :]
    final_index = jnp.arange(ext_slow, dtype=jnp.int32)[:, None] * slow_len + low_index
    final_angle = final_index.astype(jnp.float32) * (-math.pi / (4.0 * trace_len))
    real_part, imag_part = rotate(real_part, imag_part, final_angle)
    result = jnp.stack([real_part, imag_part]) * (1.0 / math.sqrt(ext_len))
    return jnp.transpose(result, (0, 2, 1))


MESH = pl.DeviceIdType.MESH
CHUNKS = 4
HALVES = 2
LANES = 128
VMEM_LIMIT = 12 * 2**20


def halves(table):
    high = table.astype(jnp.bfloat16)
    low = (table - high.astype(np.float64)).astype(jnp.bfloat16)
    return high, low


def fused_tables(sizes):
    side, fast_len, fast_local, rows, groups, blocks = sizes
    points = side * side
    ext = rows * points
    low_len = side // fast_len
    slow_len = side * low_len
    half = low_len * fast_local
    lows = low_len // HALVES
    cols, subs = blocks
    index = np.arange(side)
    angles = 2.0 * np.pi * (index[:, None] * index[None, :] % side) / side
    dft = np.stack(
        [
            halves(np.concatenate([np.cos(part), np.sin(part)], 1))
            for part in np.split(angles, side // LANES, 1)
        ]
    )
    low_at, fast_at = (
        grid.reshape(-1)
        for grid in np.meshgrid(np.arange(low_len), np.arange(fast_local), indexing="ij")
    )
    freq = low_at[:, None] + low_len * index[None, :]
    centred = freq - slow_len // 2
    members = np.arange(rows)
    inner = fast_local * members[:, None] + fast_at
    theta = 2.0 * np.pi * inner[:, :, None] * centred / points
    base = np.stack([np.cos(theta), np.sin(theta)], 1).astype(np.float32)
    shifts = 0.5 / rows - np.arange(rows) / rows
    angle = centred * (2.0 * np.pi / points) * shifts[:, None, None, None] - theta
    post = np.stack([np.cos(angle), np.sin(angle)], 1).astype(np.float32)
    post = post.reshape(rows, 2, cols, subs, HALVES, lows * fast_local, side)
    post = np.transpose(post, (0, 2, 4, 1, 3, 5, 6)).reshape(rows * cols, HALVES, 2, -1, side)
    slot_at, low_in, fast_in = (
        grid.reshape(-1)
        for grid in np.meshgrid(
            np.arange(rows), np.arange(lows), np.arange(fast_local), indexing="ij"
        )
    )
    inner = fast_local * slot_at + fast_in
    same = low_in[:, None] == low_in[None, :]
    sign = 1.0 - 2.0 * (inner[:, None] % 2)
    kernels = []
    for shift in shifts:
        gap = inner[None, :] - inner[:, None] + shift
        weight = sign / points * np.sin(np.pi * shift) / np.sin(np.pi * gap / fast_len)
        weight = np.where(same, weight, 0.0)
        for part in np.split(weight, cols):
            kernels.append(np.stack(halves(part)))
    kernels = np.stack(kernels)
    spin = 2.0 * np.pi * low_at[:, None] * index[None, :] / slow_len
    spin = np.stack([np.cos(spin), np.sin(spin)]).astype(np.float32)
    row_at, group_at = np.divmod(np.arange(rows * groups), groups)
    digit = rows * (fast_local * group_at[:, None] + fast_at) + row_at[:, None]
    angle = freq * (2 * digit[:, :, None] - 1) % (2 * ext) * (np.pi / ext)
    twist = np.stack([np.cos(angle), np.sin(angle)], 1).astype(np.float32)
    twist = np.stack(np.split(twist, side // LANES, 3), 1)
    source_row, source_group, fast_at = np.meshgrid(
        np.arange(rows), np.arange(groups), np.arange(fast_local), indexing="ij"
    )
    low_digit = rows * (fast_local * source_group + fast_at) + source_row
    vanish = np.exp(1j * (np.pi / rows - 2.0 * np.pi / rows * source_row)) - 1.0
    finals = np.arange(rows * fast_len)
    turns = np.exp(
        2j * np.pi * low_digit[..., None] * finals / (rows * fast_len)
        - 1j * np.pi * slow_len * finals / ext
    ) / (vanish[..., None] * math.sqrt(ext))
    real_rows = np.concatenate([turns.real, turns.imag], -1)
    imag_rows = np.concatenate([-turns.imag, turns.real], -1)
    final = np.stack([real_rows, imag_rows], 2).reshape(-1, 2 * rows * fast_len)
    final = np.stack(halves(final))
    return dft, spin, base, kernels, post, twist, final


def split(value):
    high = value.astype(jnp.bfloat16)
    return high, (value - high.astype(jnp.float32)).astype(jnp.bfloat16)


def dot3(left, right):
    mul = partial(jnp.dot, preferred_element_type=jnp.float32)
    count = left[0].shape[0]
    both = mul(jnp.concatenate(left, 0), right[0])
    return both[:count] + (both[count:] + mul(left[0], right[1]))


def short_transform(values, orient):
    count = len(values)
    if count == 1:
        return values
    even = short_transform(values[0::2], orient)
    odd = short_transform(values[1::2], orient)
    first, second = [], []
    for at in range(count // 2):
        cosine = math.cos(2.0 * math.pi * at / count)
        sine = orient * math.sin(2.0 * math.pi * at / count)
        real, imag = odd[at]
        if at == 0:
            spun = (real, imag)
        elif 4 * at == count:
            spun = (-orient * imag, orient * real)
        else:
            spun = (real * cosine - imag * sine, real * sine + imag * cosine)
        first.append(plus(even[at], spun))
        second.append((even[at][0] - spun[0], even[at][1] - spun[1]))
    return first + second


def fused_kernel(
    sizes,
    x_hbm,
    dft_hbm,
    spin_hbm,
    base_hbm,
    kern_hbm,
    post_hbm,
    twist_hbm,
    out_ref,
    x_ref,
    dft,
    spin,
    base,
    kern,
    post,
    twist,
    edge,
    gathered,
    send_prod,
    recv_prod,
    spread,
    send_tail,
    recv_tail,
    table_sem,
    gather_send,
    gather_recv,
    prod_send,
    prod_recv,
    tail_send,
    tail_recv,
):
    side, fast_len, fast_local, rows, groups, (cols, subs) = sizes
    points = side * side
    low_len = side // fast_len
    half = low_len * fast_local
    lows = low_len // CHUNKS
    deep = lows * fast_local
    thick = CHUNKS // HALVES * deep
    members = rows * groups
    row = lax.axis_index("rows")
    col = lax.axis_index("cols")
    sub = lax.axis_index("sub")
    group = col * subs + sub
    me = row * groups + group

    def place(member):
        inside = lax.rem(member, groups)
        return {
            "rows": lax.div(member, groups),
            "cols": lax.div(inside, subs),
            "sub": lax.rem(inside, subs),
        }

    first_load = pltpu.make_async_copy(x_hbm, x_ref, table_sem.at[0])
    first_load.start()
    barrier = pltpu.get_barrier_semaphore()

    @pl.when(row > 0)
    def _():
        pl.semaphore_signal(barrier, inc=1, device_id={"rows": row - 1}, device_id_type=MESH)

    @pl.when(row < rows - 1)
    def _():
        pl.semaphore_signal(barrier, inc=1, device_id={"rows": row + 1}, device_id_type=MESH)

    for near in ({"cols": 1 - col}, {"sub": 1 - sub}):
        pl.semaphore_signal(barrier, inc=1, device_id=near, device_id_type=MESH)

    loads = [
        first_load,
        pltpu.make_async_copy(spin_hbm, spin, table_sem.at[1]),
        pltpu.make_async_copy(dft_hbm, dft, table_sem.at[2]),
        pltpu.make_async_copy(base_hbm.at[row], base, table_sem.at[3]),
        pltpu.make_async_copy(kern_hbm.at[row * cols + col], kern, table_sem.at[4]),
        pltpu.make_async_copy(post_hbm.at[row * cols + col], post, table_sem.at[5]),
        pltpu.make_async_copy(twist_hbm.at[me], twist, table_sem.at[6]),
    ]
    for load in loads[1:4]:
        load.start()

    def stacked(values):
        return jnp.concatenate([value for value in values], 0)

    def slices(real, imag):
        return [
            (real[at * fast_local : (at + 1) * fast_local], imag[at * fast_local : (at + 1) * fast_local])
            for at in range(low_len)
        ]

    def lane_tile(data, tile, orient):
        count = data[0].shape[0] // 2
        out = dot3(data, (dft[tile, 0], dft[tile, 1]))
        cosines, sines = out[:, :LANES], out[:, LANES:]
        return (
            cosines[:count] - orient * sines[count:],
            cosines[count:] + orient * sines[:count],
        )

    def lane_transform(real, imag, orient):
        data = split(jnp.concatenate([real, imag], 0))
        tiles = [lane_tile(data, tile, orient) for tile in range(side // LANES)]
        return tuple(jnp.concatenate([tile[at] for tile in tiles], 1) for at in range(2))

    loads[0].wait()
    values = [
        (
            x_ref[0, :, at * side : (at + 1) * side],
            x_ref[1, :, at * side : (at + 1) * side],
        )
        for at in range(low_len)
    ]
    values = short_transform(values, 1.0)
    real = stacked([value[0] for value in values])
    imag = stacked([value[1] for value in values])
    loads[1].wait()
    real, imag = times((real, imag), (spin[0], spin[1]))
    loads[2].wait()
    real, imag = lane_transform(real, imag, 1.0)
    loads[3].wait()
    real, imag = times((real, imag), (base[0], base[1]))
    for chunk in range(CHUNKS):
        gathered[row, col, chunk, 0] = real[chunk * deep : (chunk + 1) * deep]
        gathered[row, col, chunk, 1] = imag[chunk * deep : (chunk + 1) * deep]

    pl.semaphore_wait(
        barrier,
        2 + (row > 0).astype(jnp.int32) + (row < rows - 1).astype(jnp.int32),
    )

    inner = (row > 0) & (row < rows - 1)
    outer = jnp.logical_not(inner)
    end = jnp.where(2 * row < rows, 0, rows - 1)
    far = rows - 1 - end
    beside = jnp.where(row == 0, 1, jnp.where(row == rows - 1, rows - 2, rows - 1 - row))
    other = jnp.where(inner, end, jnp.where(end == 0, rows - 2, 1))
    across = {"cols": 1 - col}

    def hop(slot, pair, chunk, way, target):
        return pltpu.make_async_remote_copy(
            src_ref=gathered.at[slot, pair, chunk],
            dst_ref=gathered.at[slot, pair, chunk],
            send_sem=gather_send.at[way, chunk],
            recv_sem=gather_recv.at[slot, pair, chunk],
            device_id=target,
            device_id_type=MESH,
        )

    def arrive(slot, pair, chunk):
        hop(slot, pair, chunk, 0, across).wait_recv()

    def own_moves(chunk):
        return [
            (None, hop(row, col, chunk, 0, {"rows": beside})),
            (inner, hop(row, col, chunk, 1, {"rows": end})),
            (None, hop(row, col, chunk, 2, across)),
        ]

    def beside_moves(chunk):
        return [
            (inner, hop(beside, col, chunk, 3, {"rows": end})),
            (None, hop(beside, col, chunk, 4, across)),
        ]

    def other_moves(chunk):
        return [
            (inner, hop(other, col, chunk, 5, {"rows": beside})),
            (None, hop(other, col, chunk, 6, across)),
        ]

    def far_moves(chunk):
        return [
            (inner, hop(far, col, chunk, 7, {"rows": end})),
            (None, hop(far, col, chunk, 8, across)),
        ]

    def begin(moves):
        for need, move in moves:
            if need is None:
                move.start()
            else:
                pl.when(need)(move.start)

    def begin_if(need, moves):
        for on, move in moves:
            if on is None or on is need:
                move.start()

    def finish(moves):
        for need, move in moves:
            if need is None:
                move.wait_send()
            else:
                pl.when(need)(move.wait_send)

    for chunk in range(CHUNKS):
        begin(own_moves(chunk))
    for load in loads[4:]:
        load.start()

    shift = 0.5 / rows - row.astype(jnp.float32) / rows
    half_turn = jnp.zeros((1, 1), jnp.float32) + shift * math.pi
    half_cos = jnp.cos(half_turn)
    half_sin = jnp.sin(half_turn)
    edge_at = lax.broadcasted_iota(jnp.int32, edge.shape[1:], 0)
    edge_lane = lax.broadcasted_iota(jnp.int32, edge.shape[1:], 1)
    edge_angle = edge_at.astype(jnp.float32) * (math.pi / fast_len)
    edge[0] = jnp.where(edge_lane == 0, jnp.cos(edge_angle) * (1.0 / points), 0.0)
    edge[1] = jnp.where(edge_lane == 0, jnp.sin(edge_angle) * (1.0 / points), 0.0)

    def prod_copy(pair, part, origin):
        span = pl.ds(0, 2 * thick + (8 if part == 0 else 0))
        return pltpu.make_async_remote_copy(
            src_ref=send_prod.at[pair, part, span],
            dst_ref=recv_prod.at[pair * subs + origin, part, span],
            send_sem=prod_send.at[pair, part],
            recv_sem=prod_recv.at[pair * subs + origin, part],
            device_id={"sub": 1 - sub},
            device_id_type=MESH,
        )

    def part_chunks(part):
        return range(part * CHUNKS // HALVES, (part + 1) * CHUNKS // HALVES)

    def contract(pair, part):
        chunks = part_chunks(part)
        real, imag = (
            stacked([gathered[slot, pair, chunk, at] for slot in range(rows) for chunk in chunks])
            for at in range(2)
        )
        data = split(jnp.concatenate([real, imag], 1))
        moved = dot3((kern[0], kern[1]), data)
        real, imag = times((moved[:, :side], moved[:, side:]), (post[part, 0], post[part, 1]))
        mine = pair * subs + sub
        if part == 0:
            firsts = tuple(
                stacked([gathered[slot, pair, 0, at, :fast_local, :128] for slot in range(rows)])
                for at in range(2)
            )
            mean_a, mean_b = (
                jnp.sum(jnp.sum(raw, 0, keepdims=True), 1, keepdims=True)
                for raw in times(firsts, (edge[0], edge[1]))
            )
            row_at = lax.broadcasted_iota(jnp.int32, real.shape, 0)
            lane_at = lax.broadcasted_iota(jnp.int32, real.shape, 1)
            constant = (lane_at == 0) & (row_at % thick < fast_local)
            parity = jnp.where(constant, (1 - 2 * (row_at % 2)).astype(jnp.float32), 0.0)
            real = real - parity * (mean_a * half_cos + mean_b * half_sin)
            imag = imag - parity * (mean_b * half_cos - mean_a * half_sin)
            side_at = lax.broadcasted_iota(jnp.int32, (8, side), 1)
            means = jnp.where(side_at < side // 2, mean_a, mean_b)
            send_prod[pair, part, 2 * thick :] = means
            recv_prod[mine, part, 2 * thick :] = means

        for at in range(subs):
            span = slice(at * thick, (at + 1) * thick)

            @pl.when(sub == at)
            def _():
                recv_prod[mine, part, :thick] = real[span]
                recv_prod[mine, part, thick : 2 * thick] = imag[span]

            @pl.when(sub != at)
            def _():
                send_prod[pair, part, :thick] = real[span]
                send_prod[pair, part, thick : 2 * thick] = imag[span]

        prod_copy(pair, part, sub).start()

    def expand(pair):
        for part in range(HALVES):
            prod_copy(pair, part, 1 - sub).wait_recv()
        real, imag = (
            stacked(
                [
                    recv_prod[pair * subs + origin, part, at * thick : (at + 1) * thick]
                    for origin in range(subs)
                    for part in range(HALVES)
                ]
            )
            for at in range(2)
        )
        real, imag = lane_transform(real, imag, -1.0)
        for origin in range(subs):
            span = slice(origin * half, (origin + 1) * half)
            turned = times((real[span], imag[span]), (spin[0], -spin[1]))
            values = short_transform(slices(*turned), -1.0)
            for at in range(2):
                spread[pair * subs + origin, at] = stacked([value[at] for value in values])

    @pl.when(inner)
    def _():
        for chunk in range(CHUNKS):
            arrive(beside, col, chunk)
            begin_if(inner, beside_moves(chunk))
            arrive(other, col, chunk)
            begin_if(inner, other_moves(chunk))
        for chunk in range(CHUNKS):
            arrive(far, col, chunk)
            begin_if(inner, far_moves(chunk))

    @pl.when(outer)
    def _():
        for slot, moves in ((beside, beside_moves), (other, other_moves), (far, far_moves)):
            for chunk in range(CHUNKS):
                arrive(slot, col, chunk)
                begin_if(outer, moves(chunk))

    loads[4].wait()
    loads[5].wait()
    for part in range(HALVES):
        contract(col, part)
    expand(col)
    for part in range(HALVES):
        for slot in (row, beside, other, far):
            for chunk in part_chunks(part):
                arrive(slot, 1 - col, chunk)
        contract(1 - col, part)
    expand(1 - col)

    at_row = lax.broadcasted_iota(jnp.int32, (half, side), 0)
    flip = (1 - 2 * (at_row % 2)).astype(jnp.float32)
    part_cos = flip * half_cos
    part_sin = flip * half_sin

    def value(number):
        block, at = divmod(number, 2)
        lane_from = at * (side // 2)
        mean = recv_prod[block, 0, 2 * thick : 2 * thick + 1, lane_from : lane_from + 1]
        data = spread[block, at]
        return (mean + part_cos * data, part_sin * data)

    wire_a = value(0)
    wire_b = value(1)
    wire_c = value(2)
    gate = times(times(times(value(3), wire_a), wire_b), wire_c)
    gate = plus(gate, times(value(4), wire_a))
    gate = plus(gate, times(value(5), wire_b))
    gate = plus(gate, times(value(6), wire_c))
    gate = plus(gate, value(7))
    values = short_transform(slices(*gate), 1.0)
    real = stacked([value[0] for value in values])
    imag = stacked([value[1] for value in values])
    real, imag = times((real, imag), (spin[0], spin[1]))
    loads[6].wait()
    data = split(jnp.concatenate([real, imag], 0))
    breadth = side * low_len // members
    lane_piece = side // members
    tile_lanes = low_len * lane_piece
    tiles = side // tile_lanes
    lanes = lax.broadcasted_iota(jnp.int32, (2 * fast_local, tile_lanes), 1)
    low_side = (2 * row < rows).astype(jnp.int32)

    def tail_copy(target, slot):
        return pltpu.make_async_remote_copy(
            src_ref=send_tail.at[target],
            dst_ref=recv_tail.at[slot],
            send_sem=tail_send.at[target],
            recv_sem=tail_recv.at[slot],
            device_id=place(target),
            device_id_type=MESH,
        )

    for turn_at in range(tiles):
        tile = lax.rem(low_side + turn_at, tiles)
        real, imag = times(lane_tile(data, tile, 1.0), (twist[tile, 0], twist[tile, 1]))
        pieces = [
            jnp.concatenate(
                [
                    real[at * fast_local : (at + 1) * fast_local],
                    imag[at * fast_local : (at + 1) * fast_local],
                ],
                0,
            )
            for at in range(low_len)
        ]
        bit = low_len // 2
        while bit:
            keep = (lanes // (lane_piece * bit)) % 2 == 0
            for at in range(low_len):
                if at & bit == 0:
                    one, two = pieces[at], pieces[at + bit]
                    pieces[at] = jnp.where(keep, one, pltpu.roll(two, lane_piece * bit, 1))
                    pieces[at + bit] = jnp.where(
                        keep, pltpu.roll(one, tile_lanes - lane_piece * bit, 1), two
                    )
            bit //= 2
        for at in range(low_len):
            send_tail[tile * low_len + at] = pieces[at]
        for at in range(low_len):
            target = tile * low_len + lax.rem(at + low_side * (low_len // 2), low_len)

            @pl.when(target != me)
            def _():
                tail_copy(target, me).start()

    out_ref[me] = send_tail[me]
    for step in range(1, members):
        source = lax.rem(me + step, members)
        tail_copy(source, source).wait_recv()
        out_ref[source] = recv_tail[source]

    for step in range(1, members):
        target = lax.rem(me + step, members)
        tail_copy(target, me).wait_send()
    for pair in range(cols):
        for part in range(HALVES):
            prod_copy(pair, part, sub).wait_send()
    for chunk in range(CHUNKS):
        for moves in (
            own_moves,
            beside_moves,
            other_moves,
            far_moves,
        ):
            finish(moves(chunk))


def final_kernel(sizes, flat_ref, final_ref, out_ref):
    side, fast_len, fast_local, rows, groups, blocks = sizes
    low_len = side // fast_len
    lane_piece = side // (rows * groups)
    flat = flat_ref[...].reshape(-1, flat_ref.shape[2])
    data = split(jnp.transpose(flat))
    result = dot3(data, (final_ref[0], final_ref[1]))
    for at in range(low_len):
        picked = result[at * lane_piece : (at + 1) * lane_piece]
        rows_at = pl.ds(at, lane_piece, stride=low_len)
        out_ref[0, rows_at] = picked[:, : rows * fast_len]
        out_ref[1, rows_at] = picked[:, rows * fast_len :]


def fused_on_device(sizes, trace):
    side, fast_len, fast_local, rows, groups, (cols, subs) = sizes
    low_len = side // fast_len
    half = low_len * fast_local
    deep = half // CHUNKS
    members = rows * groups
    *tables, final = [jnp.asarray(table) for table in fused_tables(sizes)]
    thick = half // HALVES
    block = jnp.transpose(trace, (0, 2, 1))
    vmem = pltpu.VMEM
    bf16 = jnp.bfloat16
    f32 = jnp.float32
    dma = pltpu.SemaphoreType.DMA
    breadth = side * low_len // members
    flat = pl.pallas_call(
        partial(fused_kernel, sizes),
        out_shape=vmem((members, 2 * fast_local, breadth), f32),
        in_specs=[pl.BlockSpec(memory_space=pltpu.HBM)] * (1 + len(tables)),
        out_specs=pl.BlockSpec(memory_space=vmem),
        scratch_shapes=[
            vmem(block.shape, f32),
            vmem((side // LANES, 2, side, side), bf16),
            vmem((2, half, side), f32),
            vmem((2, half, side), f32),
            vmem((2, subs * thick, rows * thick), bf16),
            vmem((HALVES, 2, subs * thick, side), f32),
            vmem((side // LANES, 2, half, LANES), f32),
            vmem((2, fast_len, 128), f32),
            vmem((rows, cols, CHUNKS, 2, deep, side), f32),
            vmem((cols, HALVES, 2 * thick + 8, side), f32),
            vmem((groups, HALVES, 2 * thick + 8, side), f32),
            vmem((groups, 2, half, side), f32),
            vmem((members, 2 * fast_local, breadth), f32),
            vmem((members, 2 * fast_local, breadth), f32),
            dma((8,)),
            dma((9, CHUNKS)),
            dma((rows, cols, CHUNKS)),
            dma((cols, HALVES)),
            dma((groups, HALVES)),
            dma((members,)),
            dma((members,)),
        ],
        compiler_params=pltpu.CompilerParams(
            collective_id=0, has_side_effects=True, vmem_limit_bytes=VMEM_LIMIT
        ),
    )(*[pltpu.with_memory_space_constraint(table, pltpu.HBM) for table in (block, *tables)])
    return pl.pallas_call(
        partial(final_kernel, sizes),
        out_shape=jax.ShapeDtypeStruct((2, breadth, rows * fast_len), f32),
        in_specs=[pl.BlockSpec(memory_space=vmem)] * 2,
        out_specs=pl.BlockSpec(memory_space=vmem),
        compiler_params=pltpu.CompilerParams(vmem_limit_bytes=VMEM_LIMIT),
    )(flat, final)


def fused_sizes(mesh, trace):
    shape = mesh.shape
    rows = shape["rows"]
    groups = shape["cols"] * shape["sub"]
    slow_len = trace.shape[1] // shape["groups"]
    fast_len = trace.shape[2]
    side = math.isqrt(slow_len * fast_len)
    fast_local = fast_len // rows
    local_cols = trace.shape[0] // groups
    low_len = side // fast_len
    fits = (
        side * side == slow_len * fast_len
        and low_len * fast_len == side
        and rows == 4
        and groups == rows
        and shape["cols"] == 2
        and shape["sub"] == 2
        and local_cols == 2
        and fast_local == 8
        and 2 * low_len * fast_local == 128
        and rows * groups == 2 * low_len
        and side == 2 * LANES
    )
    return (side, fast_len, fast_local, rows, groups, (shape["cols"], shape["sub"])) if fits else None


def solution(mesh):
    placed = (P(("cols", "sub"), "groups", "rows"),)

    def whole(trace):
        sizes = fused_sizes(mesh, trace)
        return jax.shard_map(
            on_device if sizes is None else partial(fused_on_device, sizes),
            mesh=mesh,
            in_specs=placed,
            out_specs=P("groups", ("rows", "cols", "sub"), None),
            check_vma=False,
        )(trace)

    return whole
```

```python
from functools import partial
import math

import jax
import jax.numpy as jnp
import numpy as np
from jax import lax
from jax.experimental import pallas as pl
from jax.experimental.pallas import tpu as pltpu
from jax.sharding import PartitionSpec as P


def dft_table(extent, orient):
    points = jnp.arange(extent, dtype=jnp.int32)
    product = points[:, None] * points[None, :] % extent
    angles = product.astype(jnp.float32) * (orient * 2.0 * math.pi / extent)
    return (jnp.cos(angles), jnp.sin(angles))


def complex_apply(table_real, table_imag, data_real, data_imag):
    matmul = partial(jnp.dot, precision=lax.Precision.HIGHEST, preferred_element_type=jnp.float32)
    out_real = matmul(table_real, data_real) - matmul(table_imag, data_imag)
    out_imag = matmul(table_real, data_imag) + matmul(table_imag, data_real)
    return (out_real, out_imag)


def rotate(data_real, data_imag, angles):
    cosine = jnp.cos(angles)
    sine = jnp.sin(angles)
    return (data_real * cosine - data_imag * sine, data_real * sine + data_imag * cosine)


def turn(index_product, modulus, orient):
    return (index_product % modulus).astype(jnp.float32) * (orient * 2.0 * math.pi / modulus)


def transform_lead(data_real, data_imag, orient):
    extent = data_real.shape[0]
    rest_shape = data_real.shape[1:]
    breadth = data_real.size // extent
    flat_real = data_real.reshape(extent, breadth)
    flat_imag = data_imag.reshape(extent, breadth)
    if extent <= 128:
        table_real, table_imag = dft_table(extent, orient)
        out_real, out_imag = complex_apply(table_real, table_imag, flat_real, flat_imag)
    else:
        outer_len = extent // 128
        first_real, first_imag = transform_lead(
            flat_real.reshape(outer_len, 128 * breadth),
            flat_imag.reshape(outer_len, 128 * breadth),
            orient,
        )
        first_real = first_real.reshape(outer_len, 128, breadth)
        first_imag = first_imag.reshape(outer_len, 128, breadth)
        outer_index = jnp.arange(outer_len, dtype=jnp.int32)[:, None]
        inner_index = jnp.arange(128, dtype=jnp.int32)[None, :]
        angles = turn(outer_index * inner_index, extent, orient)[:, :, None]
        first_real, first_imag = rotate(first_real, first_imag, angles)
        first_real = jnp.transpose(first_real, (1, 0, 2)).reshape(128, outer_len * breadth)
        first_imag = jnp.transpose(first_imag, (1, 0, 2)).reshape(128, outer_len * breadth)
        out_real, out_imag = transform_lead(first_real, first_imag, orient)
    return (out_real.reshape((extent,) + rest_shape), out_imag.reshape((extent,) + rest_shape))


def times(first, second):
    return (
        first[0] * second[0] - first[1] * second[1],
        first[0] * second[1] + first[1] * second[0],
    )


def plus(first, second):
    return (first[0] + second[0], first[1] + second[1])


def on_device(trace):
    local_cols = trace.shape[0]
    slow_len = trace.shape[1]
    fast_local = trace.shape[2]
    row_parts = lax.axis_size("rows")
    group_parts = lax.axis_size(("cols", "sub"))
    row_index = lax.axis_index("rows")
    group_index = lax.axis_index(("cols", "sub"))
    fast_len = fast_local * row_parts
    trace_len = slow_len * fast_len
    ext_len = 4 * trace_len
    ext_slow = 4 * fast_len
    slow_block = slow_len // row_parts
    ext_block = ext_slow // row_parts
    point_block = ext_block // group_parts
    coeff_block = slow_block // group_parts
    real_part = jnp.transpose(trace, (1, 0, 2))
    imag_part = jnp.zeros_like(real_part)
    real_part, imag_part = transform_lead(real_part, imag_part, 1.0)
    lead_index = jnp.arange(slow_len, dtype=jnp.int32)[:, None, None]
    fast_index = (row_index * fast_local + jnp.arange(fast_local, dtype=jnp.int32))[None, None, :]
    real_part, imag_part = rotate(
        real_part, imag_part, turn(lead_index * fast_index, trace_len, 1.0)
    )
    moved = lax.all_to_all(
        jnp.stack([real_part, imag_part]), "rows", split_axis=1, concat_axis=3, tiled=True
    )
    moved = jnp.transpose(moved, (0, 3, 2, 1))
    real_part, imag_part = transform_lead(moved[0], moved[1], 1.0)
    slow_index = (row_index * slow_block + jnp.arange(slow_block, dtype=jnp.int32))[None, None, :]
    coeff_index = jnp.arange(fast_len, dtype=jnp.int32)[:, None, None] * slow_len + slow_index
    shift_angle = coeff_index.astype(jnp.float32) * (math.pi / (4.0 * trace_len))
    real_part, imag_part = rotate(real_part / trace_len, imag_part / trace_len, shift_angle)
    padding = jnp.zeros((ext_slow - fast_len, local_cols, slow_index.shape[2]), jnp.float32)
    real_part = jnp.concatenate([real_part, padding], 0)
    imag_part = jnp.concatenate([imag_part, padding], 0)
    real_part, imag_part = transform_lead(real_part, imag_part, -1.0)
    ext_index = jnp.arange(ext_slow, dtype=jnp.int32)[:, None, None]
    real_part, imag_part = rotate(real_part, imag_part, turn(ext_index * slow_index, ext_len, -1.0))
    stacked = jnp.stack([real_part, imag_part])
    moved = lax.all_to_all(stacked, "rows", split_axis=1, concat_axis=3, tiled=True)
    moved = jnp.transpose(moved, (0, 3, 2, 1))
    real_part, imag_part = transform_lead(moved[0], moved[1], -1.0)
    joined = lax.all_to_all(
        jnp.stack([real_part, imag_part]), ("cols", "sub"), split_axis=3, concat_axis=2, tiled=True
    )
    real_part = joined[0]
    imag_part = joined[1]

    def column(number):
        return (real_part[:, number], imag_part[:, number])

    wire_a = column(0)
    wire_b = column(1)
    wire_c = column(2)
    gate = times(times(times(column(3), wire_a), wire_b), wire_c)
    gate = plus(gate, times(column(4), wire_a))
    gate = plus(gate, times(column(5), wire_b))
    gate = plus(gate, times(column(6), wire_c))
    gate = plus(gate, column(7))
    point_index = (
        row_index * ext_block + group_index * point_block + jnp.arange(point_block, dtype=jnp.int32)
    )
    quarter = (point_index % 4).astype(jnp.float32)
    vanish_angle = math.pi / 4.0 - math.pi / 2.0 * quarter
    vanish_real = (jnp.cos(vanish_angle) - 1.0)[None, :]
    vanish_imag = jnp.sin(vanish_angle)[None, :]
    magnitude = vanish_real * vanish_real + vanish_imag * vanish_imag
    ratio_real = (gate[0] * vanish_real + gate[1] * vanish_imag) / magnitude
    ratio_imag = (gate[1] * vanish_real - gate[0] * vanish_imag) / magnitude
    real_part, imag_part = transform_lead(ratio_real, ratio_imag, 1.0)
    freq_index = jnp.arange(slow_len, dtype=jnp.int32)[:, None]
    real_part, imag_part = rotate(
        real_part, imag_part, turn(freq_index * point_index[None, :], ext_len, 1.0)
    )
    moved = lax.all_to_all(
        lax.all_to_all(
            jnp.stack([real_part, imag_part]), "rows", split_axis=1, concat_axis=2, tiled=True
        ),
        ("cols", "sub"),
        split_axis=1,
        concat_axis=2,
        tiled=True,
    )
    moved = moved.reshape(2, coeff_block, group_parts, row_parts, point_block)
    moved = jnp.transpose(moved, (0, 3, 2, 4, 1)).reshape(2, ext_slow, coeff_block)
    real_part, imag_part = transform_lead(moved[0], moved[1], 1.0)
    low_index = (
        row_index * slow_block
        + group_index * coeff_block
        + jnp.arange(coeff_block, dtype=jnp.int32)
    )[None, :]
    final_index = jnp.arange(ext_slow, dtype=jnp.int32)[:, None] * slow_len + low_index
    final_angle = final_index.astype(jnp.float32) * (-math.pi / (4.0 * trace_len))
    real_part, imag_part = rotate(real_part, imag_part, final_angle)
    result = jnp.stack([real_part, imag_part]) * (1.0 / math.sqrt(ext_len))
    return jnp.transpose(result, (0, 2, 1))


MESH = pl.DeviceIdType.MESH
CHUNKS = 4
HALVES = 2
LANES = 128
VMEM_LIMIT = 12 * 2**20


def halves(table):
    high = table.astype(jnp.bfloat16)
    low = (table - high.astype(np.float64)).astype(jnp.bfloat16)
    return high, low


def fused_tables(sizes):
    side, fast_len, fast_local, rows, groups, blocks = sizes
    points = side * side
    ext = rows * points
    low_len = side // fast_len
    slow_len = side * low_len
    half = low_len * fast_local
    lows = low_len // HALVES
    cols, subs = blocks
    index = np.arange(side)
    angles = 2.0 * np.pi * (index[:, None] * index[None, :] % side) / side
    dft = np.stack(
        [
            halves(np.concatenate([np.cos(part), np.sin(part)], 1))
            for part in np.split(angles, side // LANES, 1)
        ]
    )
    low_at, fast_at = (
        grid.reshape(-1)
        for grid in np.meshgrid(np.arange(low_len), np.arange(fast_local), indexing="ij")
    )
    freq = low_at[:, None] + low_len * index[None, :]
    centred = freq - slow_len // 2
    members = np.arange(rows)
    inner = fast_local * members[:, None] + fast_at
    theta = 2.0 * np.pi * inner[:, :, None] * centred / points
    base = np.stack([np.cos(theta), np.sin(theta)], 1).astype(np.float32)
    shifts = 0.5 / rows - np.arange(rows) / rows
    angle = centred * (2.0 * np.pi / points) * shifts[:, None, None, None] - theta
    post = np.stack([np.cos(angle), np.sin(angle)], 1).astype(np.float32)
    post = post.reshape(rows, 2, cols, subs, HALVES, lows * fast_local, side)
    post = np.transpose(post, (0, 2, 4, 1, 3, 5, 6)).reshape(rows * cols, HALVES, 2, -1, side)
    slot_at, low_in, fast_in = (
        grid.reshape(-1)
        for grid in np.meshgrid(
            np.arange(rows), np.arange(lows), np.arange(fast_local), indexing="ij"
        )
    )
    inner = fast_local * slot_at + fast_in
    same = low_in[:, None] == low_in[None, :]
    sign = 1.0 - 2.0 * (inner[:, None] % 2)
    kernels = []
    for shift in shifts:
        gap = inner[None, :] - inner[:, None] + shift
        weight = sign / points * np.sin(np.pi * shift) / np.sin(np.pi * gap / fast_len)
        weight = np.where(same, weight, 0.0)
        for part in np.split(weight, cols):
            kernels.append(np.stack(halves(part)))
    kernels = np.stack(kernels)
    spin = 2.0 * np.pi * low_at[:, None] * index[None, :] / slow_len
    spin = np.stack([np.cos(spin), np.sin(spin)]).astype(np.float32)
    row_at, group_at = np.divmod(np.arange(rows * groups), groups)
    digit = rows * (fast_local * group_at[:, None] + fast_at) + row_at[:, None]
    angle = freq * (2 * digit[:, :, None] - 1) % (2 * ext) * (np.pi / ext)
    twist = np.stack([np.cos(angle), np.sin(angle)], 1).astype(np.float32)
    twist = np.stack(np.split(twist, side // LANES, 3), 1)
    source_row, source_group, fast_at = np.meshgrid(
        np.arange(rows), np.arange(groups), np.arange(fast_local), indexing="ij"
    )
    low_digit = rows * (fast_local * source_group + fast_at) + source_row
    vanish = np.exp(1j * (np.pi / rows - 2.0 * np.pi / rows * source_row)) - 1.0
    finals = np.arange(rows * fast_len)
    turns = np.exp(
        2j * np.pi * low_digit[..., None] * finals / (rows * fast_len)
        - 1j * np.pi * slow_len * finals / ext
    ) / (vanish[..., None] * math.sqrt(ext))
    real_rows = np.concatenate([turns.real, turns.imag], -1)
    imag_rows = np.concatenate([-turns.imag, turns.real], -1)
    final = np.stack([real_rows, imag_rows], 2).reshape(-1, 2 * rows * fast_len)
    final = np.stack(halves(final))
    return dft, spin, base, kernels, post, twist, final


def split(value):
    high = value.astype(jnp.bfloat16)
    return high, (value - high.astype(jnp.float32)).astype(jnp.bfloat16)


def dot3(left, right):
    mul = partial(jnp.dot, preferred_element_type=jnp.float32)
    count = left[0].shape[0]
    both = mul(jnp.concatenate(left, 0), right[0])
    return both[:count] + (both[count:] + mul(left[0], right[1]))


def short_transform(values, orient):
    count = len(values)
    if count == 1:
        return values
    even = short_transform(values[0::2], orient)
    odd = short_transform(values[1::2], orient)
    first, second = [], []
    for at in range(count // 2):
        cosine = math.cos(2.0 * math.pi * at / count)
        sine = orient * math.sin(2.0 * math.pi * at / count)
        real, imag = odd[at]
        if at == 0:
            spun = (real, imag)
        elif 4 * at == count:
            spun = (-orient * imag, orient * real)
        else:
            spun = (real * cosine - imag * sine, real * sine + imag * cosine)
        first.append(plus(even[at], spun))
        second.append((even[at][0] - spun[0], even[at][1] - spun[1]))
    return first + second


def fused_kernel(
    sizes,
    x_hbm,
    dft_hbm,
    spin_hbm,
    base_hbm,
    kern_hbm,
    post_hbm,
    twist_hbm,
    out_ref,
    x_ref,
    dft,
    spin,
    base,
    kern,
    post,
    twist,
    edge,
    gathered,
    send_prod,
    recv_prod,
    spread,
    send_tail,
    recv_tail,
    table_sem,
    gather_send,
    gather_recv,
    prod_send,
    prod_recv,
    tail_send,
    tail_recv,
):
    side, fast_len, fast_local, rows, groups, (cols, subs) = sizes
    points = side * side
    low_len = side // fast_len
    half = low_len * fast_local
    lows = low_len // CHUNKS
    deep = lows * fast_local
    thick = CHUNKS // HALVES * deep
    members = rows * groups
    row = lax.axis_index("rows")
    col = lax.axis_index("cols")
    sub = lax.axis_index("sub")
    group = col * subs + sub
    me = row * groups + group

    def place(member):
        inside = lax.rem(member, groups)
        return {
            "rows": lax.div(member, groups),
            "cols": lax.div(inside, subs),
            "sub": lax.rem(inside, subs),
        }

    first_load = pltpu.make_async_copy(x_hbm, x_ref, table_sem.at[0])
    first_load.start()
    barrier = pltpu.get_barrier_semaphore()

    @pl.when(row > 0)
    def _():
        pl.semaphore_signal(barrier, inc=1, device_id={"rows": row - 1}, device_id_type=MESH)

    @pl.when(row < rows - 1)
    def _():
        pl.semaphore_signal(barrier, inc=1, device_id={"rows": row + 1}, device_id_type=MESH)

    for near in ({"cols": 1 - col}, {"sub": 1 - sub}):
        pl.semaphore_signal(barrier, inc=1, device_id=near, device_id_type=MESH)

    loads = [
        first_load,
        pltpu.make_async_copy(spin_hbm, spin, table_sem.at[1]),
        pltpu.make_async_copy(dft_hbm, dft, table_sem.at[2]),
        pltpu.make_async_copy(base_hbm.at[row], base, table_sem.at[3]),
        pltpu.make_async_copy(kern_hbm.at[row * cols + col], kern, table_sem.at[4]),
        pltpu.make_async_copy(post_hbm.at[row * cols + col], post, table_sem.at[5]),
        pltpu.make_async_copy(twist_hbm.at[me], twist, table_sem.at[6]),
    ]
    for load in (loads[2], loads[1], loads[3]):
        load.start()

    def stacked(values):
        return jnp.concatenate([value for value in values], 0)

    def slices(real, imag):
        return [
            (real[at * fast_local : (at + 1) * fast_local], imag[at * fast_local : (at + 1) * fast_local])
            for at in range(low_len)
        ]

    def lane_tile(data, tile, orient):
        count = data[0].shape[0] // 2
        out = dot3(data, (dft[tile, 0], dft[tile, 1]))
        cosines, sines = out[:, :LANES], out[:, LANES:]
        return (
            cosines[:count] - orient * sines[count:],
            cosines[count:] + orient * sines[:count],
        )

    def lane_transform(real, imag, orient):
        data = split(jnp.concatenate([real, imag], 0))
        tiles = [lane_tile(data, tile, orient) for tile in range(side // LANES)]
        return tuple(jnp.concatenate([tile[at] for tile in tiles], 1) for at in range(2))

    loads[0].wait()
    values = [
        (
            x_ref[0, :, at * side : (at + 1) * side],
            x_ref[1, :, at * side : (at + 1) * side],
        )
        for at in range(low_len)
    ]
    values = short_transform(values, 1.0)
    real = stacked([value[0] for value in values])
    imag = stacked([value[1] for value in values])
    loads[1].wait()
    real, imag = times((real, imag), (spin[0], spin[1]))
    loads[2].wait()
    real, imag = lane_transform(real, imag, 1.0)
    loads[3].wait()
    real, imag = times((real, imag), (base[0], base[1]))
    for chunk in range(CHUNKS):
        gathered[row, col, chunk, 0] = real[chunk * deep : (chunk + 1) * deep]
        gathered[row, col, chunk, 1] = imag[chunk * deep : (chunk + 1) * deep]

    pl.semaphore_wait(
        barrier,
        2 + (row > 0).astype(jnp.int32) + (row < rows - 1).astype(jnp.int32),
    )

    inner = (row > 0) & (row < rows - 1)
    outer = jnp.logical_not(inner)
    end = jnp.where(2 * row < rows, 0, rows - 1)
    far = rows - 1 - end
    beside = jnp.where(row == 0, 1, jnp.where(row == rows - 1, rows - 2, rows - 1 - row))
    other = jnp.where(inner, end, jnp.where(end == 0, rows - 2, 1))
    across = {"cols": 1 - col}

    def hop(slot, pair, chunk, way, target):
        return pltpu.make_async_remote_copy(
            src_ref=gathered.at[slot, pair, chunk],
            dst_ref=gathered.at[slot, pair, chunk],
            send_sem=gather_send.at[way, chunk],
            recv_sem=gather_recv.at[slot, pair, chunk],
            device_id=target,
            device_id_type=MESH,
        )

    def arrive(slot, pair, chunk):
        hop(slot, pair, chunk, 0, across).wait_recv()

    def own_moves(chunk):
        return [
            (None, hop(row, col, chunk, 0, {"rows": beside})),
            (inner, hop(row, col, chunk, 1, {"rows": end})),
            (None, hop(row, col, chunk, 2, across)),
        ]

    def beside_moves(chunk):
        return [
            (inner, hop(beside, col, chunk, 3, {"rows": end})),
            (None, hop(beside, col, chunk, 4, across)),
        ]

    def other_moves(chunk):
        return [
            (inner, hop(other, col, chunk, 5, {"rows": beside})),
            (None, hop(other, col, chunk, 6, across)),
        ]

    def far_moves(chunk):
        return [
            (inner, hop(far, col, chunk, 7, {"rows": end})),
            (None, hop(far, col, chunk, 8, across)),
        ]

    def begin(moves):
        for need, move in moves:
            if need is None:
                move.start()
            else:
                pl.when(need)(move.start)

    def begin_if(need, moves):
        for on, move in moves:
            if on is None or on is need:
                move.start()

    def finish(moves):
        for need, move in moves:
            if need is None:
                move.wait_send()
            else:
                pl.when(need)(move.wait_send)

    for chunk in range(CHUNKS):
        begin(own_moves(chunk))
    for load in loads[4:]:
        load.start()

    shift = 0.5 / rows - row.astype(jnp.float32) / rows
    half_turn = jnp.zeros((1, 1), jnp.float32) + shift * math.pi
    half_cos = jnp.cos(half_turn)
    half_sin = jnp.sin(half_turn)
    edge_at = lax.broadcasted_iota(jnp.int32, edge.shape[1:], 0)
    edge_lane = lax.broadcasted_iota(jnp.int32, edge.shape[1:], 1)
    edge_angle = edge_at.astype(jnp.float32) * (math.pi / fast_len)
    edge[0] = jnp.where(edge_lane == 0, jnp.cos(edge_angle) * (1.0 / points), 0.0)
    edge[1] = jnp.where(edge_lane == 0, jnp.sin(edge_angle) * (1.0 / points), 0.0)

    def prod_copy(pair, part, origin):
        span = pl.ds(0, 2 * thick + (8 if part == 0 else 0))
        return pltpu.make_async_remote_copy(
            src_ref=send_prod.at[pair, part, span],
            dst_ref=recv_prod.at[pair * subs + origin, part, span],
            send_sem=prod_send.at[pair, part],
            recv_sem=prod_recv.at[pair * subs + origin, part],
            device_id={"sub": 1 - sub},
            device_id_type=MESH,
        )

    def part_chunks(part):
        return range(part * CHUNKS // HALVES, (part + 1) * CHUNKS // HALVES)

    def contract(pair, part):
        chunks = part_chunks(part)
        real, imag = (
            stacked([gathered[slot, pair, chunk, at] for slot in range(rows) for chunk in chunks])
            for at in range(2)
        )
        data = split(jnp.concatenate([real, imag], 1))
        moved = dot3((kern[0], kern[1]), data)
        real, imag = times((moved[:, :side], moved[:, side:]), (post[part, 0], post[part, 1]))
        mine = pair * subs + sub
        if part == 0:
            firsts = tuple(
                stacked([gathered[slot, pair, 0, at, :fast_local, :128] for slot in range(rows)])
                for at in range(2)
            )
            mean_a, mean_b = (
                jnp.sum(jnp.sum(raw, 0, keepdims=True), 1, keepdims=True)
                for raw in times(firsts, (edge[0], edge[1]))
            )
            row_at = lax.broadcasted_iota(jnp.int32, real.shape, 0)
            lane_at = lax.broadcasted_iota(jnp.int32, real.shape, 1)
            constant = (lane_at == 0) & (row_at % thick < fast_local)
            parity = jnp.where(constant, (1 - 2 * (row_at % 2)).astype(jnp.float32), 0.0)
            real = real - parity * (mean_a * half_cos + mean_b * half_sin)
            imag = imag - parity * (mean_b * half_cos - mean_a * half_sin)
            side_at = lax.broadcasted_iota(jnp.int32, (8, side), 1)
            means = jnp.where(side_at < side // 2, mean_a, mean_b)
            send_prod[pair, part, 2 * thick :] = means
            recv_prod[mine, part, 2 * thick :] = means

        for at in range(subs):
            span = slice(at * thick, (at + 1) * thick)

            @pl.when(sub == at)
            def _():
                recv_prod[mine, part, :thick] = real[span]
                recv_prod[mine, part, thick : 2 * thick] = imag[span]

            @pl.when(sub != at)
            def _():
                send_prod[pair, part, :thick] = real[span]
                send_prod[pair, part, thick : 2 * thick] = imag[span]

        prod_copy(pair, part, sub).start()

    def expand(pair):
        for part in range(HALVES):
            prod_copy(pair, part, 1 - sub).wait_recv()
        real, imag = (
            stacked(
                [
                    recv_prod[pair * subs + origin, part, at * thick : (at + 1) * thick]
                    for origin in range(subs)
                    for part in range(HALVES)
                ]
            )
            for at in range(2)
        )
        real, imag = lane_transform(real, imag, -1.0)
        for origin in range(subs):
            span = slice(origin * half, (origin + 1) * half)
            turned = times((real[span], imag[span]), (spin[0], -spin[1]))
            values = short_transform(slices(*turned), -1.0)
            for at in range(2):
                spread[pair * subs + origin, at] = stacked([value[at] for value in values])

    @pl.when(inner)
    def _():
        for chunk in range(CHUNKS):
            arrive(beside, col, chunk)
            begin_if(inner, beside_moves(chunk))
            arrive(other, col, chunk)
            begin_if(inner, other_moves(chunk))
        for chunk in range(CHUNKS):
            arrive(far, col, chunk)
            begin_if(inner, far_moves(chunk))

    @pl.when(outer)
    def _():
        for slot, moves in ((beside, beside_moves), (other, other_moves), (far, far_moves)):
            for chunk in range(CHUNKS):
                arrive(slot, col, chunk)
                begin_if(outer, moves(chunk))

    loads[4].wait()
    loads[5].wait()
    for part in range(HALVES):
        contract(col, part)
    expand(col)
    for part in range(HALVES):
        for slot in (row, beside, other, far):
            for chunk in part_chunks(part):
                arrive(slot, 1 - col, chunk)
        contract(1 - col, part)
    expand(1 - col)

    at_row = lax.broadcasted_iota(jnp.int32, (half, side), 0)
    flip = (1 - 2 * (at_row % 2)).astype(jnp.float32)
    part_cos = flip * half_cos
    part_sin = flip * half_sin

    def value(number):
        block, at = divmod(number, 2)
        lane_from = at * (side // 2)
        mean = recv_prod[block, 0, 2 * thick : 2 * thick + 1, lane_from : lane_from + 1]
        data = spread[block, at]
        return (mean + part_cos * data, part_sin * data)

    wire_a = value(0)
    wire_b = value(1)
    wire_c = value(2)
    gate = times(times(times(value(3), wire_a), wire_b), wire_c)
    gate = plus(gate, times(value(4), wire_a))
    gate = plus(gate, times(value(5), wire_b))
    gate = plus(gate, times(value(6), wire_c))
    gate = plus(gate, value(7))
    values = short_transform(slices(*gate), 1.0)
    real = stacked([value[0] for value in values])
    imag = stacked([value[1] for value in values])
    real, imag = times((real, imag), (spin[0], spin[1]))
    loads[6].wait()
    data = split(jnp.concatenate([real, imag], 0))
    breadth = side * low_len // members
    lane_piece = side // members
    tile_lanes = low_len * lane_piece
    tiles = side // tile_lanes
    lanes = lax.broadcasted_iota(jnp.int32, (2 * fast_local, tile_lanes), 1)
    low_side = (2 * row < rows).astype(jnp.int32)

    def tail_copy(target, slot):
        return pltpu.make_async_remote_copy(
            src_ref=send_tail.at[target],
            dst_ref=recv_tail.at[slot],
            send_sem=tail_send.at[target],
            recv_sem=tail_recv.at[slot],
            device_id=place(target),
            device_id_type=MESH,
        )

    for turn_at in range(tiles):
        tile = lax.rem(low_side + turn_at, tiles)
        real, imag = times(lane_tile(data, tile, 1.0), (twist[tile, 0], twist[tile, 1]))
        pieces = [
            jnp.concatenate(
                [
                    real[at * fast_local : (at + 1) * fast_local],
                    imag[at * fast_local : (at + 1) * fast_local],
                ],
                0,
            )
            for at in range(low_len)
        ]
        bit = low_len // 2
        while bit:
            keep = (lanes // (lane_piece * bit)) % 2 == 0
            for at in range(low_len):
                if at & bit == 0:
                    one, two = pieces[at], pieces[at + bit]
                    pieces[at] = jnp.where(keep, one, pltpu.roll(two, lane_piece * bit, 1))
                    pieces[at + bit] = jnp.where(
                        keep, pltpu.roll(one, tile_lanes - lane_piece * bit, 1), two
                    )
            bit //= 2
        for at in range(low_len):
            send_tail[tile * low_len + at] = pieces[at]
        for at in range(low_len):
            ahead = low_side if turn_at == 0 else 1 - lax.rem(row, 2)
            target = tile * low_len + lax.rem(at + ahead * (low_len // 2), low_len)

            @pl.when(target != me)
            def _():
                tail_copy(target, me).start()

    out_ref[me] = send_tail[me]
    for step in range(1, members):
        source = lax.rem(me + step, members)
        tail_copy(source, source).wait_recv()
        out_ref[source] = recv_tail[source]

    for step in range(1, members):
        target = lax.rem(me + step, members)
        tail_copy(target, me).wait_send()
    for pair in range(cols):
        for part in range(HALVES):
            prod_copy(pair, part, sub).wait_send()
    for chunk in range(CHUNKS):
        for moves in (
            own_moves,
            beside_moves,
            other_moves,
            far_moves,
        ):
            finish(moves(chunk))


def final_kernel(sizes, flat_ref, final_ref, out_ref):
    side, fast_len, fast_local, rows, groups, blocks = sizes
    low_len = side // fast_len
    lane_piece = side // (rows * groups)
    flat = flat_ref[...].reshape(-1, flat_ref.shape[2])
    data = split(jnp.transpose(flat))
    result = dot3(data, (final_ref[0], final_ref[1]))
    for at in range(low_len):
        picked = result[at * lane_piece : (at + 1) * lane_piece]
        rows_at = pl.ds(at, lane_piece, stride=low_len)
        out_ref[0, rows_at] = picked[:, : rows * fast_len]
        out_ref[1, rows_at] = picked[:, rows * fast_len :]


def fused_on_device(sizes, trace):
    side, fast_len, fast_local, rows, groups, (cols, subs) = sizes
    low_len = side // fast_len
    half = low_len * fast_local
    deep = half // CHUNKS
    members = rows * groups
    *tables, final = [jnp.asarray(table) for table in fused_tables(sizes)]
    thick = half // HALVES
    block = jnp.transpose(trace, (0, 2, 1))
    vmem = pltpu.VMEM
    bf16 = jnp.bfloat16
    f32 = jnp.float32
    dma = pltpu.SemaphoreType.DMA
    breadth = side * low_len // members
    flat = pl.pallas_call(
        partial(fused_kernel, sizes),
        out_shape=vmem((members, 2 * fast_local, breadth), f32),
        in_specs=[pl.BlockSpec(memory_space=pltpu.HBM)] * (1 + len(tables)),
        out_specs=pl.BlockSpec(memory_space=vmem),
        scratch_shapes=[
            vmem(block.shape, f32),
            vmem((side // LANES, 2, side, side), bf16),
            vmem((2, half, side), f32),
            vmem((2, half, side), f32),
            vmem((2, subs * thick, rows * thick), bf16),
            vmem((HALVES, 2, subs * thick, side), f32),
            vmem((side // LANES, 2, half, LANES), f32),
            vmem((2, fast_len, 128), f32),
            vmem((rows, cols, CHUNKS, 2, deep, side), f32),
            vmem((cols, HALVES, 2 * thick + 8, side), f32),
            vmem((groups, HALVES, 2 * thick + 8, side), f32),
            vmem((groups, 2, half, side), f32),
            vmem((members, 2 * fast_local, breadth), f32),
            vmem((members, 2 * fast_local, breadth), f32),
            dma((8,)),
            dma((9, CHUNKS)),
            dma((rows, cols, CHUNKS)),
            dma((cols, HALVES)),
            dma((groups, HALVES)),
            dma((members,)),
            dma((members,)),
        ],
        compiler_params=pltpu.CompilerParams(
            collective_id=0, has_side_effects=True, vmem_limit_bytes=VMEM_LIMIT
        ),
    )(*[pltpu.with_memory_space_constraint(table, pltpu.HBM) for table in (block, *tables)])
    return pl.pallas_call(
        partial(final_kernel, sizes),
        out_shape=jax.ShapeDtypeStruct((2, breadth, rows * fast_len), f32),
        in_specs=[pl.BlockSpec(memory_space=vmem)] * 2,
        out_specs=pl.BlockSpec(memory_space=vmem),
        compiler_params=pltpu.CompilerParams(vmem_limit_bytes=VMEM_LIMIT),
    )(flat, final)


def fused_sizes(mesh, trace):
    shape = mesh.shape
    rows = shape["rows"]
    groups = shape["cols"] * shape["sub"]
    slow_len = trace.shape[1] // shape["groups"]
    fast_len = trace.shape[2]
    side = math.isqrt(slow_len * fast_len)
    fast_local = fast_len // rows
    local_cols = trace.shape[0] // groups
    low_len = side // fast_len
    fits = (
        side * side == slow_len * fast_len
        and low_len * fast_len == side
        and rows == 4
        and groups == rows
        and shape["cols"] == 2
        and shape["sub"] == 2
        and local_cols == 2
        and fast_local == 8
        and 2 * low_len * fast_local == 128
        and rows * groups == 2 * low_len
        and side == 2 * LANES
    )
    return (side, fast_len, fast_local, rows, groups, (shape["cols"], shape["sub"])) if fits else None


def solution(mesh):
    placed = (P(("cols", "sub"), "groups", "rows"),)

    def whole(trace):
        sizes = fused_sizes(mesh, trace)
        return jax.shard_map(
            on_device if sizes is None else partial(fused_on_device, sizes),
            mesh=mesh,
            in_specs=placed,
            out_specs=P("groups", ("rows", "cols", "sub"), None),
            check_vma=False,
        )(trace)

    return whole
```

```python
from functools import partial
import math

import jax
import jax.numpy as jnp
import numpy as np
from jax import lax
from jax.experimental import pallas as pl
from jax.experimental.pallas import tpu as pltpu
from jax.sharding import PartitionSpec as P


def dft_table(extent, orient):
    points = jnp.arange(extent, dtype=jnp.int32)
    product = points[:, None] * points[None, :] % extent
    angles = product.astype(jnp.float32) * (orient * 2.0 * math.pi / extent)
    return (jnp.cos(angles), jnp.sin(angles))


def complex_apply(table_real, table_imag, data_real, data_imag):
    matmul = partial(jnp.dot, precision=lax.Precision.HIGHEST, preferred_element_type=jnp.float32)
    out_real = matmul(table_real, data_real) - matmul(table_imag, data_imag)
    out_imag = matmul(table_real, data_imag) + matmul(table_imag, data_real)
    return (out_real, out_imag)


def rotate(data_real, data_imag, angles):
    cosine = jnp.cos(angles)
    sine = jnp.sin(angles)
    return (data_real * cosine - data_imag * sine, data_real * sine + data_imag * cosine)


def turn(index_product, modulus, orient):
    return (index_product % modulus).astype(jnp.float32) * (orient * 2.0 * math.pi / modulus)


def transform_lead(data_real, data_imag, orient):
    extent = data_real.shape[0]
    rest_shape = data_real.shape[1:]
    breadth = data_real.size // extent
    flat_real = data_real.reshape(extent, breadth)
    flat_imag = data_imag.reshape(extent, breadth)
    if extent <= 128:
        table_real, table_imag = dft_table(extent, orient)
        out_real, out_imag = complex_apply(table_real, table_imag, flat_real, flat_imag)
    else:
        outer_len = extent // 128
        first_real, first_imag = transform_lead(
            flat_real.reshape(outer_len, 128 * breadth),
            flat_imag.reshape(outer_len, 128 * breadth),
            orient,
        )
        first_real = first_real.reshape(outer_len, 128, breadth)
        first_imag = first_imag.reshape(outer_len, 128, breadth)
        outer_index = jnp.arange(outer_len, dtype=jnp.int32)[:, None]
        inner_index = jnp.arange(128, dtype=jnp.int32)[None, :]
        angles = turn(outer_index * inner_index, extent, orient)[:, :, None]
        first_real, first_imag = rotate(first_real, first_imag, angles)
        first_real = jnp.transpose(first_real, (1, 0, 2)).reshape(128, outer_len * breadth)
        first_imag = jnp.transpose(first_imag, (1, 0, 2)).reshape(128, outer_len * breadth)
        out_real, out_imag = transform_lead(first_real, first_imag, orient)
    return (out_real.reshape((extent,) + rest_shape), out_imag.reshape((extent,) + rest_shape))


def times(first, second):
    return (
        first[0] * second[0] - first[1] * second[1],
        first[0] * second[1] + first[1] * second[0],
    )


def plus(first, second):
    return (first[0] + second[0], first[1] + second[1])


def on_device(trace):
    local_cols = trace.shape[0]
    slow_len = trace.shape[1]
    fast_local = trace.shape[2]
    row_parts = lax.axis_size("rows")
    group_parts = lax.axis_size(("cols", "sub"))
    row_index = lax.axis_index("rows")
    group_index = lax.axis_index(("cols", "sub"))
    fast_len = fast_local * row_parts
    trace_len = slow_len * fast_len
    ext_len = 4 * trace_len
    ext_slow = 4 * fast_len
    slow_block = slow_len // row_parts
    ext_block = ext_slow // row_parts
    point_block = ext_block // group_parts
    coeff_block = slow_block // group_parts
    real_part = jnp.transpose(trace, (1, 0, 2))
    imag_part = jnp.zeros_like(real_part)
    real_part, imag_part = transform_lead(real_part, imag_part, 1.0)
    lead_index = jnp.arange(slow_len, dtype=jnp.int32)[:, None, None]
    fast_index = (row_index * fast_local + jnp.arange(fast_local, dtype=jnp.int32))[None, None, :]
    real_part, imag_part = rotate(
        real_part, imag_part, turn(lead_index * fast_index, trace_len, 1.0)
    )
    moved = lax.all_to_all(
        jnp.stack([real_part, imag_part]), "rows", split_axis=1, concat_axis=3, tiled=True
    )
    moved = jnp.transpose(moved, (0, 3, 2, 1))
    real_part, imag_part = transform_lead(moved[0], moved[1], 1.0)
    slow_index = (row_index * slow_block + jnp.arange(slow_block, dtype=jnp.int32))[None, None, :]
    coeff_index = jnp.arange(fast_len, dtype=jnp.int32)[:, None, None] * slow_len + slow_index
    shift_angle = coeff_index.astype(jnp.float32) * (math.pi / (4.0 * trace_len))
    real_part, imag_part = rotate(real_part / trace_len, imag_part / trace_len, shift_angle)
    padding = jnp.zeros((ext_slow - fast_len, local_cols, slow_index.shape[2]), jnp.float32)
    real_part = jnp.concatenate([real_part, padding], 0)
    imag_part = jnp.concatenate([imag_part, padding], 0)
    real_part, imag_part = transform_lead(real_part, imag_part, -1.0)
    ext_index = jnp.arange(ext_slow, dtype=jnp.int32)[:, None, None]
    real_part, imag_part = rotate(real_part, imag_part, turn(ext_index * slow_index, ext_len, -1.0))
    stacked = jnp.stack([real_part, imag_part])
    moved = lax.all_to_all(stacked, "rows", split_axis=1, concat_axis=3, tiled=True)
    moved = jnp.transpose(moved, (0, 3, 2, 1))
    real_part, imag_part = transform_lead(moved[0], moved[1], -1.0)
    joined = lax.all_to_all(
        jnp.stack([real_part, imag_part]), ("cols", "sub"), split_axis=3, concat_axis=2, tiled=True
    )
    real_part = joined[0]
    imag_part = joined[1]

    def column(number):
        return (real_part[:, number], imag_part[:, number])

    wire_a = column(0)
    wire_b = column(1)
    wire_c = column(2)
    gate = times(times(times(column(3), wire_a), wire_b), wire_c)
    gate = plus(gate, times(column(4), wire_a))
    gate = plus(gate, times(column(5), wire_b))
    gate = plus(gate, times(column(6), wire_c))
    gate = plus(gate, column(7))
    point_index = (
        row_index * ext_block + group_index * point_block + jnp.arange(point_block, dtype=jnp.int32)
    )
    quarter = (point_index % 4).astype(jnp.float32)
    vanish_angle = math.pi / 4.0 - math.pi / 2.0 * quarter
    vanish_real = (jnp.cos(vanish_angle) - 1.0)[None, :]
    vanish_imag = jnp.sin(vanish_angle)[None, :]
    magnitude = vanish_real * vanish_real + vanish_imag * vanish_imag
    ratio_real = (gate[0] * vanish_real + gate[1] * vanish_imag) / magnitude
    ratio_imag = (gate[1] * vanish_real - gate[0] * vanish_imag) / magnitude
    real_part, imag_part = transform_lead(ratio_real, ratio_imag, 1.0)
    freq_index = jnp.arange(slow_len, dtype=jnp.int32)[:, None]
    real_part, imag_part = rotate(
        real_part, imag_part, turn(freq_index * point_index[None, :], ext_len, 1.0)
    )
    moved = lax.all_to_all(
        lax.all_to_all(
            jnp.stack([real_part, imag_part]), "rows", split_axis=1, concat_axis=2, tiled=True
        ),
        ("cols", "sub"),
        split_axis=1,
        concat_axis=2,
        tiled=True,
    )
    moved = moved.reshape(2, coeff_block, group_parts, row_parts, point_block)
    moved = jnp.transpose(moved, (0, 3, 2, 4, 1)).reshape(2, ext_slow, coeff_block)
    real_part, imag_part = transform_lead(moved[0], moved[1], 1.0)
    low_index = (
        row_index * slow_block
        + group_index * coeff_block
        + jnp.arange(coeff_block, dtype=jnp.int32)
    )[None, :]
    final_index = jnp.arange(ext_slow, dtype=jnp.int32)[:, None] * slow_len + low_index
    final_angle = final_index.astype(jnp.float32) * (-math.pi / (4.0 * trace_len))
    real_part, imag_part = rotate(real_part, imag_part, final_angle)
    result = jnp.stack([real_part, imag_part]) * (1.0 / math.sqrt(ext_len))
    return jnp.transpose(result, (0, 2, 1))


MESH = pl.DeviceIdType.MESH
CHUNKS = 4
HALVES = 2
LANES = 128
VMEM_LIMIT = 12 * 2**20


def halves(table):
    high = table.astype(jnp.bfloat16)
    low = (table - high.astype(np.float64)).astype(jnp.bfloat16)
    return high, low


def fused_tables(sizes):
    side, fast_len, fast_local, rows, groups, blocks = sizes
    points = side * side
    ext = rows * points
    low_len = side // fast_len
    slow_len = side * low_len
    half = low_len * fast_local
    lows = low_len // HALVES
    cols, subs = blocks
    index = np.arange(side)
    angles = 2.0 * np.pi * (index[:, None] * index[None, :] % side) / side
    dft = np.stack(
        [
            halves(np.concatenate([np.cos(part), np.sin(part)], 1))
            for part in np.split(angles, side // LANES, 1)
        ]
    )
    low_at, fast_at = (
        grid.reshape(-1)
        for grid in np.meshgrid(np.arange(low_len), np.arange(fast_local), indexing="ij")
    )
    freq = low_at[:, None] + low_len * index[None, :]
    centred = freq - slow_len // 2
    members = np.arange(rows)
    inner = fast_local * members[:, None] + fast_at
    theta = 2.0 * np.pi * inner[:, :, None] * centred / points
    base = np.stack([np.cos(theta), np.sin(theta)], 1).astype(np.float32)
    shifts = 0.5 / rows - np.arange(rows) / rows
    angle = centred * (2.0 * np.pi / points) * shifts[:, None, None, None] - theta
    post = np.stack([np.cos(angle), np.sin(angle)], 1).astype(np.float32)
    post = post.reshape(rows, 2, cols, subs, HALVES, lows * fast_local, side)
    post = np.transpose(post, (0, 2, 4, 1, 3, 5, 6)).reshape(rows * cols, HALVES, 2, -1, side)
    slot_at, low_in, fast_in = (
        grid.reshape(-1)
        for grid in np.meshgrid(
            np.arange(rows), np.arange(lows), np.arange(fast_local), indexing="ij"
        )
    )
    inner = fast_local * slot_at + fast_in
    same = low_in[:, None] == low_in[None, :]
    sign = 1.0 - 2.0 * (inner[:, None] % 2)
    kernels = []
    for shift in shifts:
        gap = inner[None, :] - inner[:, None] + shift
        weight = sign / points * np.sin(np.pi * shift) / np.sin(np.pi * gap / fast_len)
        weight = np.where(same, weight, 0.0)
        for part in np.split(weight, cols):
            kernels.append(np.stack(halves(part)))
    kernels = np.stack(kernels)
    spin = 2.0 * np.pi * low_at[:, None] * index[None, :] / slow_len
    spin = np.stack([np.cos(spin), np.sin(spin)]).astype(np.float32)
    row_at, group_at = np.divmod(np.arange(rows * groups), groups)
    digit = rows * (fast_local * group_at[:, None] + fast_at) + row_at[:, None]
    angle = freq * (2 * digit[:, :, None] - 1) % (2 * ext) * (np.pi / ext)
    twist = np.stack([np.cos(angle), np.sin(angle)], 1).astype(np.float32)
    twist = np.stack(np.split(twist, side // LANES, 3), 1)
    source_row, source_group, fast_at = np.meshgrid(
        np.arange(rows), np.arange(groups), np.arange(fast_local), indexing="ij"
    )
    low_digit = rows * (fast_local * source_group + fast_at) + source_row
    vanish = np.exp(1j * (np.pi / rows - 2.0 * np.pi / rows * source_row)) - 1.0
    finals = np.arange(rows * fast_len)
    turns = np.exp(
        2j * np.pi * low_digit[..., None] * finals / (rows * fast_len)
        - 1j * np.pi * slow_len * finals / ext
    ) / (vanish[..., None] * math.sqrt(ext))
    real_rows = np.concatenate([turns.real, turns.imag], -1)
    imag_rows = np.concatenate([-turns.imag, turns.real], -1)
    final = np.stack([real_rows, imag_rows], 2).reshape(-1, 2 * rows * fast_len)
    final = np.stack(halves(final))
    return dft, spin, base, kernels, post, twist, final


def split(value):
    high = value.astype(jnp.bfloat16)
    return high, (value - high.astype(jnp.float32)).astype(jnp.bfloat16)


def dot3(left, right):
    mul = partial(jnp.dot, preferred_element_type=jnp.float32)
    count = left[0].shape[0]
    both = mul(jnp.concatenate(left, 0), right[0])
    return both[:count] + (both[count:] + mul(left[0], right[1]))


def short_transform(values, orient):
    count = len(values)
    if count == 1:
        return values
    even = short_transform(values[0::2], orient)
    odd = short_transform(values[1::2], orient)
    first, second = [], []
    for at in range(count // 2):
        cosine = math.cos(2.0 * math.pi * at / count)
        sine = orient * math.sin(2.0 * math.pi * at / count)
        real, imag = odd[at]
        if at == 0:
            spun = (real, imag)
        elif 4 * at == count:
            spun = (-orient * imag, orient * real)
        else:
            spun = (real * cosine - imag * sine, real * sine + imag * cosine)
        first.append(plus(even[at], spun))
        second.append((even[at][0] - spun[0], even[at][1] - spun[1]))
    return first + second


def fused_kernel(
    sizes,
    x_hbm,
    dft_hbm,
    spin_hbm,
    base_hbm,
    kern_hbm,
    post_hbm,
    twist_hbm,
    out_ref,
    x_ref,
    dft,
    spin,
    base,
    kern,
    post,
    twist,
    edge,
    gathered,
    send_prod,
    recv_prod,
    spread,
    send_tail,
    recv_tail,
    table_sem,
    gather_send,
    gather_recv,
    prod_send,
    prod_recv,
    tail_send,
    tail_recv,
):
    side, fast_len, fast_local, rows, groups, (cols, subs) = sizes
    points = side * side
    low_len = side // fast_len
    half = low_len * fast_local
    lows = low_len // CHUNKS
    deep = lows * fast_local
    thick = CHUNKS // HALVES * deep
    members = rows * groups
    row = lax.axis_index("rows")
    col = lax.axis_index("cols")
    sub = lax.axis_index("sub")
    group = col * subs + sub
    me = row * groups + group

    def place(member):
        inside = lax.rem(member, groups)
        return {
            "rows": lax.div(member, groups),
            "cols": lax.div(inside, subs),
            "sub": lax.rem(inside, subs),
        }

    first_load = pltpu.make_async_copy(x_hbm, x_ref, table_sem.at[0])
    first_load.start()
    barrier = pltpu.get_barrier_semaphore()

    @pl.when(row > 0)
    def _():
        pl.semaphore_signal(barrier, inc=1, device_id={"rows": row - 1}, device_id_type=MESH)

    @pl.when(row < rows - 1)
    def _():
        pl.semaphore_signal(barrier, inc=1, device_id={"rows": row + 1}, device_id_type=MESH)

    for near in ({"cols": 1 - col}, {"sub": 1 - sub}):
        pl.semaphore_signal(barrier, inc=1, device_id=near, device_id_type=MESH)

    loads = [
        first_load,
        pltpu.make_async_copy(spin_hbm, spin, table_sem.at[1]),
        pltpu.make_async_copy(dft_hbm, dft, table_sem.at[2]),
        pltpu.make_async_copy(base_hbm.at[row], base, table_sem.at[3]),
        pltpu.make_async_copy(kern_hbm.at[row * cols + col], kern, table_sem.at[4]),
        pltpu.make_async_copy(post_hbm.at[row * cols + col], post, table_sem.at[5]),
        pltpu.make_async_copy(twist_hbm.at[me], twist, table_sem.at[6]),
    ]
    for load in loads[1:4]:
        load.start()

    def stacked(values):
        return jnp.concatenate([value for value in values], 0)

    def slices(real, imag):
        return [
            (real[at * fast_local : (at + 1) * fast_local], imag[at * fast_local : (at + 1) * fast_local])
            for at in range(low_len)
        ]

    def lane_tile(data, tile, orient):
        count = data[0].shape[0] // 2
        out = dot3(data, (dft[tile, 0], dft[tile, 1]))
        cosines, sines = out[:, :LANES], out[:, LANES:]
        return (
            cosines[:count] - orient * sines[count:],
            cosines[count:] + orient * sines[:count],
        )

    def lane_transform(real, imag, orient):
        data = split(jnp.concatenate([real, imag], 0))
        tiles = [lane_tile(data, tile, orient) for tile in range(side // LANES)]
        return tuple(jnp.concatenate([tile[at] for tile in tiles], 1) for at in range(2))

    loads[0].wait()
    values = [
        (
            x_ref[0, :, at * side : (at + 1) * side],
            x_ref[1, :, at * side : (at + 1) * side],
        )
        for at in range(low_len)
    ]
    values = short_transform(values, 1.0)
    real = stacked([value[0] for value in values])
    imag = stacked([value[1] for value in values])
    loads[1].wait()
    real, imag = times((real, imag), (spin[0], spin[1]))
    loads[2].wait()
    loads[3].wait()
    spread_rows = (real, imag)

    def prepare(part):
        span = slice(part * thick, (part + 1) * thick)
        real, imag = lane_transform(spread_rows[0][span], spread_rows[1][span], 1.0)
        real, imag = times((real, imag), (base[0, span], base[1, span]))
        for order in range(CHUNKS // HALVES):
            chunk = part * CHUNKS // HALVES + order
            gathered[row, col, chunk, 0] = real[order * deep : (order + 1) * deep]
            gathered[row, col, chunk, 1] = imag[order * deep : (order + 1) * deep]

    prepare(0)
    pl.semaphore_wait(
        barrier,
        2 + (row > 0).astype(jnp.int32) + (row < rows - 1).astype(jnp.int32),
    )

    inner = (row > 0) & (row < rows - 1)
    outer = jnp.logical_not(inner)
    end = jnp.where(2 * row < rows, 0, rows - 1)
    far = rows - 1 - end
    beside = jnp.where(row == 0, 1, jnp.where(row == rows - 1, rows - 2, rows - 1 - row))
    other = jnp.where(inner, end, jnp.where(end == 0, rows - 2, 1))
    across = {"cols": 1 - col}

    def hop(slot, pair, chunk, way, target):
        return pltpu.make_async_remote_copy(
            src_ref=gathered.at[slot, pair, chunk],
            dst_ref=gathered.at[slot, pair, chunk],
            send_sem=gather_send.at[way, chunk],
            recv_sem=gather_recv.at[slot, pair, chunk],
            device_id=target,
            device_id_type=MESH,
        )

    def arrive(slot, pair, chunk):
        hop(slot, pair, chunk, 0, across).wait_recv()

    def own_moves(chunk):
        return [
            (None, hop(row, col, chunk, 0, {"rows": beside})),
            (inner, hop(row, col, chunk, 1, {"rows": end})),
            (None, hop(row, col, chunk, 2, across)),
        ]

    def beside_moves(chunk):
        return [
            (inner, hop(beside, col, chunk, 3, {"rows": end})),
            (None, hop(beside, col, chunk, 4, across)),
        ]

    def other_moves(chunk):
        return [
            (inner, hop(other, col, chunk, 5, {"rows": beside})),
            (None, hop(other, col, chunk, 6, across)),
        ]

    def far_moves(chunk):
        return [
            (inner, hop(far, col, chunk, 7, {"rows": end})),
            (None, hop(far, col, chunk, 8, across)),
        ]

    def begin(moves):
        for need, move in moves:
            if need is None:
                move.start()
            else:
                pl.when(need)(move.start)

    def begin_if(need, moves):
        for on, move in moves:
            if on is None or on is need:
                move.start()

    def finish(moves):
        for need, move in moves:
            if need is None:
                move.wait_send()
            else:
                pl.when(need)(move.wait_send)

    for part in range(HALVES):
        if part:
            prepare(part)
        for chunk in range(part * CHUNKS // HALVES, (part + 1) * CHUNKS // HALVES):
            begin(own_moves(chunk))
    for load in loads[4:]:
        load.start()

    shift = 0.5 / rows - row.astype(jnp.float32) / rows
    half_turn = jnp.zeros((1, 1), jnp.float32) + shift * math.pi
    half_cos = jnp.cos(half_turn)
    half_sin = jnp.sin(half_turn)
    edge_at = lax.broadcasted_iota(jnp.int32, edge.shape[1:], 0)
    edge_lane = lax.broadcasted_iota(jnp.int32, edge.shape[1:], 1)
    edge_angle = edge_at.astype(jnp.float32) * (math.pi / fast_len)
    edge[0] = jnp.where(edge_lane == 0, jnp.cos(edge_angle) * (1.0 / points), 0.0)
    edge[1] = jnp.where(edge_lane == 0, jnp.sin(edge_angle) * (1.0 / points), 0.0)

    def prod_copy(pair, part, origin):
        span = pl.ds(0, 2 * thick + (8 if part == 0 else 0))
        return pltpu.make_async_remote_copy(
            src_ref=send_prod.at[pair, part, span],
            dst_ref=recv_prod.at[pair * subs + origin, part, span],
            send_sem=prod_send.at[pair, part],
            recv_sem=prod_recv.at[pair * subs + origin, part],
            device_id={"sub": 1 - sub},
            device_id_type=MESH,
        )

    def part_chunks(part):
        return range(part * CHUNKS // HALVES, (part + 1) * CHUNKS // HALVES)

    def contract(pair, part):
        chunks = part_chunks(part)
        real, imag = (
            stacked([gathered[slot, pair, chunk, at] for slot in range(rows) for chunk in chunks])
            for at in range(2)
        )
        data = split(jnp.concatenate([real, imag], 1))
        moved = dot3((kern[0], kern[1]), data)
        real, imag = times((moved[:, :side], moved[:, side:]), (post[part, 0], post[part, 1]))
        mine = pair * subs + sub
        if part == 0:
            firsts = tuple(
                stacked([gathered[slot, pair, 0, at, :fast_local, :128] for slot in range(rows)])
                for at in range(2)
            )
            mean_a, mean_b = (
                jnp.sum(jnp.sum(raw, 0, keepdims=True), 1, keepdims=True)
                for raw in times(firsts, (edge[0], edge[1]))
            )
            row_at = lax.broadcasted_iota(jnp.int32, real.shape, 0)
            lane_at = lax.broadcasted_iota(jnp.int32, real.shape, 1)
            constant = (lane_at == 0) & (row_at % thick < fast_local)
            parity = jnp.where(constant, (1 - 2 * (row_at % 2)).astype(jnp.float32), 0.0)
            real = real - parity * (mean_a * half_cos + mean_b * half_sin)
            imag = imag - parity * (mean_b * half_cos - mean_a * half_sin)
            side_at = lax.broadcasted_iota(jnp.int32, (8, side), 1)
            means = jnp.where(side_at < side // 2, mean_a, mean_b)
            send_prod[pair, part, 2 * thick :] = means
            recv_prod[mine, part, 2 * thick :] = means

        for at in range(subs):
            span = slice(at * thick, (at + 1) * thick)

            @pl.when(sub == at)
            def _():
                recv_prod[mine, part, :thick] = real[span]
                recv_prod[mine, part, thick : 2 * thick] = imag[span]

            @pl.when(sub != at)
            def _():
                send_prod[pair, part, :thick] = real[span]
                send_prod[pair, part, thick : 2 * thick] = imag[span]

        prod_copy(pair, part, sub).start()

    def expand(pair):
        for part in range(HALVES):
            prod_copy(pair, part, 1 - sub).wait_recv()
        real, imag = (
            stacked(
                [
                    recv_prod[pair * subs + origin, part, at * thick : (at + 1) * thick]
                    for origin in range(subs)
                    for part in range(HALVES)
                ]
            )
            for at in range(2)
        )
        real, imag = lane_transform(real, imag, -1.0)
        for origin in range(subs):
            span = slice(origin * half, (origin + 1) * half)
            turned = times((real[span], imag[span]), (spin[0], -spin[1]))
            values = short_transform(slices(*turned), -1.0)
            for at in range(2):
                spread[pair * subs + origin, at] = stacked([value[at] for value in values])

    @pl.when(inner)
    def _():
        for chunk in range(CHUNKS):
            arrive(beside, col, chunk)
            begin_if(inner, beside_moves(chunk))
            arrive(other, col, chunk)
            begin_if(inner, other_moves(chunk))
        for chunk in range(CHUNKS):
            arrive(far, col, chunk)
            begin_if(inner, far_moves(chunk))

    @pl.when(outer)
    def _():
        for slot, moves in ((beside, beside_moves), (other, other_moves), (far, far_moves)):
            for chunk in range(CHUNKS):
                arrive(slot, col, chunk)
                begin_if(outer, moves(chunk))

    loads[4].wait()
    loads[5].wait()
    for part in range(HALVES):
        contract(col, part)
    expand(col)
    for part in range(HALVES):
        for slot in (row, beside, other, far):
            for chunk in part_chunks(part):
                arrive(slot, 1 - col, chunk)
        contract(1 - col, part)
    expand(1 - col)

    at_row = lax.broadcasted_iota(jnp.int32, (half, side), 0)
    flip = (1 - 2 * (at_row % 2)).astype(jnp.float32)
    part_cos = flip * half_cos
    part_sin = flip * half_sin

    def value(number):
        block, at = divmod(number, 2)
        lane_from = at * (side // 2)
        mean = recv_prod[block, 0, 2 * thick : 2 * thick + 1, lane_from : lane_from + 1]
        data = spread[block, at]
        return (mean + part_cos * data, part_sin * data)

    wire_a = value(0)
    wire_b = value(1)
    wire_c = value(2)
    gate = times(times(times(value(3), wire_a), wire_b), wire_c)
    gate = plus(gate, times(value(4), wire_a))
    gate = plus(gate, times(value(5), wire_b))
    gate = plus(gate, times(value(6), wire_c))
    gate = plus(gate, value(7))
    values = short_transform(slices(*gate), 1.0)
    real = stacked([value[0] for value in values])
    imag = stacked([value[1] for value in values])
    real, imag = times((real, imag), (spin[0], spin[1]))
    loads[6].wait()
    data = split(jnp.concatenate([real, imag], 0))
    breadth = side * low_len // members
    lane_piece = side // members
    tile_lanes = low_len * lane_piece
    tiles = side // tile_lanes
    lanes = lax.broadcasted_iota(jnp.int32, (2 * fast_local, tile_lanes), 1)
    low_side = (2 * row < rows).astype(jnp.int32)

    def tail_copy(target, slot):
        return pltpu.make_async_remote_copy(
            src_ref=send_tail.at[target],
            dst_ref=recv_tail.at[slot],
            send_sem=tail_send.at[target],
            recv_sem=tail_recv.at[slot],
            device_id=place(target),
            device_id_type=MESH,
        )

    for turn_at in range(tiles):
        tile = lax.rem(low_side + turn_at, tiles)
        real, imag = times(lane_tile(data, tile, 1.0), (twist[tile, 0], twist[tile, 1]))
        pieces = [
            jnp.concatenate(
                [
                    real[at * fast_local : (at + 1) * fast_local],
                    imag[at * fast_local : (at + 1) * fast_local],
                ],
                0,
            )
            for at in range(low_len)
        ]
        bit = low_len // 2
        while bit:
            keep = (lanes // (lane_piece * bit)) % 2 == 0
            for at in range(low_len):
                if at & bit == 0:
                    one, two = pieces[at], pieces[at + bit]
                    pieces[at] = jnp.where(keep, one, pltpu.roll(two, lane_piece * bit, 1))
                    pieces[at + bit] = jnp.where(
                        keep, pltpu.roll(one, tile_lanes - lane_piece * bit, 1), two
                    )
            bit //= 2
        for at in range(low_len):
            send_tail[tile * low_len + at] = pieces[at]
        for at in range(low_len):
            target = tile * low_len + lax.rem(at + low_side * (low_len // 2), low_len)

            @pl.when(target != me)
            def _():
                tail_copy(target, me).start()

    out_ref[me] = send_tail[me]
    for step in range(1, members):
        source = lax.rem(me + step, members)
        tail_copy(source, source).wait_recv()
        out_ref[source] = recv_tail[source]

    for step in range(1, members):
        target = lax.rem(me + step, members)
        tail_copy(target, me).wait_send()
    for pair in range(cols):
        for part in range(HALVES):
            prod_copy(pair, part, sub).wait_send()
    for chunk in range(CHUNKS):
        for moves in (
            own_moves,
            beside_moves,
            other_moves,
            far_moves,
        ):
            finish(moves(chunk))


def final_kernel(sizes, flat_ref, final_ref, out_ref):
    side, fast_len, fast_local, rows, groups, blocks = sizes
    low_len = side // fast_len
    lane_piece = side // (rows * groups)
    flat = flat_ref[...].reshape(-1, flat_ref.shape[2])
    data = split(jnp.transpose(flat))
    result = dot3(data, (final_ref[0], final_ref[1]))
    for at in range(low_len):
        picked = result[at * lane_piece : (at + 1) * lane_piece]
        rows_at = pl.ds(at, lane_piece, stride=low_len)
        out_ref[0, rows_at] = picked[:, : rows * fast_len]
        out_ref[1, rows_at] = picked[:, rows * fast_len :]


def fused_on_device(sizes, trace):
    side, fast_len, fast_local, rows, groups, (cols, subs) = sizes
    low_len = side // fast_len
    half = low_len * fast_local
    deep = half // CHUNKS
    members = rows * groups
    *tables, final = [jnp.asarray(table) for table in fused_tables(sizes)]
    thick = half // HALVES
    block = jnp.transpose(trace, (0, 2, 1))
    vmem = pltpu.VMEM
    bf16 = jnp.bfloat16
    f32 = jnp.float32
    dma = pltpu.SemaphoreType.DMA
    breadth = side * low_len // members
    flat = pl.pallas_call(
        partial(fused_kernel, sizes),
        out_shape=vmem((members, 2 * fast_local, breadth), f32),
        in_specs=[pl.BlockSpec(memory_space=pltpu.HBM)] * (1 + len(tables)),
        out_specs=pl.BlockSpec(memory_space=vmem),
        scratch_shapes=[
            vmem(block.shape, f32),
            vmem((side // LANES, 2, side, side), bf16),
            vmem((2, half, side), f32),
            vmem((2, half, side), f32),
            vmem((2, subs * thick, rows * thick), bf16),
            vmem((HALVES, 2, subs * thick, side), f32),
            vmem((side // LANES, 2, half, LANES), f32),
            vmem((2, fast_len, 128), f32),
            vmem((rows, cols, CHUNKS, 2, deep, side), f32),
            vmem((cols, HALVES, 2 * thick + 8, side), f32),
            vmem((groups, HALVES, 2 * thick + 8, side), f32),
            vmem((groups, 2, half, side), f32),
            vmem((members, 2 * fast_local, breadth), f32),
            vmem((members, 2 * fast_local, breadth), f32),
            dma((8,)),
            dma((9, CHUNKS)),
            dma((rows, cols, CHUNKS)),
            dma((cols, HALVES)),
            dma((groups, HALVES)),
            dma((members,)),
            dma((members,)),
        ],
        compiler_params=pltpu.CompilerParams(
            collective_id=0, has_side_effects=True, vmem_limit_bytes=VMEM_LIMIT
        ),
    )(*[pltpu.with_memory_space_constraint(table, pltpu.HBM) for table in (block, *tables)])
    return pl.pallas_call(
        partial(final_kernel, sizes),
        out_shape=jax.ShapeDtypeStruct((2, breadth, rows * fast_len), f32),
        in_specs=[pl.BlockSpec(memory_space=vmem)] * 2,
        out_specs=pl.BlockSpec(memory_space=vmem),
        compiler_params=pltpu.CompilerParams(vmem_limit_bytes=VMEM_LIMIT),
    )(flat, final)


def fused_sizes(mesh, trace):
    shape = mesh.shape
    rows = shape["rows"]
    groups = shape["cols"] * shape["sub"]
    slow_len = trace.shape[1] // shape["groups"]
    fast_len = trace.shape[2]
    side = math.isqrt(slow_len * fast_len)
    fast_local = fast_len // rows
    local_cols = trace.shape[0] // groups
    low_len = side // fast_len
    fits = (
        side * side == slow_len * fast_len
        and low_len * fast_len == side
        and rows == 4
        and groups == rows
        and shape["cols"] == 2
        and shape["sub"] == 2
        and local_cols == 2
        and fast_local == 8
        and 2 * low_len * fast_local == 128
        and rows * groups == 2 * low_len
        and side == 2 * LANES
    )
    return (side, fast_len, fast_local, rows, groups, (shape["cols"], shape["sub"])) if fits else None


def solution(mesh):
    placed = (P(("cols", "sub"), "groups", "rows"),)

    def whole(trace):
        sizes = fused_sizes(mesh, trace)
        return jax.shard_map(
            on_device if sizes is None else partial(fused_on_device, sizes),
            mesh=mesh,
            in_specs=placed,
            out_specs=P("groups", ("rows", "cols", "sub"), None),
            check_vma=False,
        )(trace)

    return whole
```
